32 devices in a mesh: dp: 8 (over z, x), tensor: 4 (over y, core).
Axes of the slice: x: 2, y: 2, z: 4, core: 2. Of those that a mesh axis runs over, the one named last changes fastest.
Arguments:
- tokens: bfloat16 [8192, 768], P('dp'), may hold values from -6 to 6
- row_length: int32 [48], replicated, may hold values from 128 to 256, as said below
- row_group: int32 [48], replicated, may hold values from 0 to 7, as said below
- row_step: int32 [48], replicated, may hold values from 0 to 999
- time_table: bfloat16 [1000, 768], replicated, may hold values from -3 to 3
- norm1_gain: float32 [768], replicated, may hold values from 0.1 to 1.9
- norm1_bias: float32 [768], replicated, may hold values from -1.75 to 1.75
- w_qkv: bfloat16 [768, 3, 768], P(None, None, 'tensor'), may hold values from -0.21875 to 0.21875
- w_out: bfloat16 [768, 768], P('tensor'), may hold values from -2.5 to 2.5
- norm2_gain: float32 [768], replicated, may hold values from 0.1 to 1.9
- norm2_bias: float32 [768], replicated, may hold values from -1.75 to 1.75
- w_up: bfloat16 [768, 3072], P(None, 'tensor'), may hold values from -0.21875 to 0.21875
- up_bias: float32 [3072], P('tensor'), may hold values from -3 to 3
- w_down: bfloat16 [3072, 768], P('tensor'), may hold values from -0.21875 to 0.21875
- down_bias: float32 [768], replicated, may hold values from -1.75 to 1.75
- cotangent: bfloat16 [8192, 768], P('dp'), may hold values from -6 to 6
Outputs:
- block_output: bfloat16 [8192, 768], P('dp')
- input_grad: bfloat16 [8192, 768], P('dp')
- time_grad: float32 [1000, 768], P(None, 'tensor')
- gain1_grad: float32 [768], replicated
- bias1_grad: float32 [768], replicated
- qkv_grad: float32 [768, 3, 768], P(None, None, 'tensor')
- out_proj_grad: float32 [768, 768], P('tensor')
- gain2_grad: float32 [768], replicated
- bias2_grad: float32 [768], replicated
- up_grad: float32 [768, 3072], P(None, 'tensor')
- up_bias_grad: float32 [3072], P('tensor')
- down_grad: float32 [3072, 768], P('tensor')
- down_bias_grad: float32 [768], replicated
The draws below stay inside these ranges and needn't reach their ends.
Inputs may be any that keep to these rules, and one draw needn't show every extreme that they name: `row_length`: each row holds 128 or 256 tokens. `row_group`: the rows of each group hold 1024 tokens in all, of which 0 to 4 rows have 2 * 128 tokens; both ends of that range are reached.
All inputs are finite; a program needn't handle non-finite values.
Results may differ from the reference program's by a relative error of at most 0.019.
Values may be sent and summed in bfloat16 or wider, within the bound.
No kernel may reach another device: no remote copies, remote signals or barrier semaphores. Data moves between devices by JAX's collectives and lax.ppermute only.
A program may use at most 128 MiB of HBM per device.

```python
import jax
import jax.numpy as jnp
from jax import lax

D = 768
HEADS = 12
HEAD_DIM = 64
FF = 3072
STEPS = 1000
SHORT = 128
BLOCK = 512
TOK_DEV = 1024
HD = 768
ROWS = 48
TOKENS = 8192
N_DP = 8
N_TENSOR = 4


def row_layout(key):
    slot_count = TOK_DEV // SHORT
    group_count = ROWS * 4 // (3 * slot_count)
    half_slots = slot_count // 2
    base_key = jax.random.fold_in(key, 11)
    key_order, key_count, key_shuffle = jax.random.split(base_key, 3)
    group_order = jax.random.permutation(key_order, group_count)
    long_draw = jax.random.randint(key_count, (group_count // 2,), 0, half_slots + 1)
    long_draw = long_draw.at[0].set(half_slots)
    long_count = jnp.zeros((group_count,), jnp.int32)
    long_count = long_count.at[group_order[:group_count // 2]].set(long_draw)
    long_count = long_count.at[group_order[group_count // 2:]].set(half_slots - long_draw)
    slot_index = jnp.arange(slot_count)[None, :]
    is_valid = slot_index < slot_count - long_count[:, None]
    lengths = jnp.where(slot_index < long_count[:, None], 2 * SHORT, SHORT)
    shuffle = jax.random.permutation(key_shuffle, group_count * slot_count)
    sort_key = jnp.where(is_valid.reshape(-1), 0, group_count * slot_count) + shuffle
    picked = jnp.argsort(sort_key)[:ROWS]
    return (lengths.reshape(-1)[picked].astype(jnp.int32), (picked // slot_count).astype(jnp.int32))


def draw_row_length(key, part):
    return row_layout(key)[0]


def draw_row_group(key, part):
    return row_layout(key)[1]


def place_ends(values, own_key, low, top_value):
    longest = values.shape.index(max(values.shape))
    spots = []
    for shift in (0, 1):
        where = [jax.random.randint(jax.random.fold_in(own_key, axis), (), 0, length) for axis, length in enumerate(values.shape)]
        where[longest] = (where[longest] + shift) % values.shape[longest]
        spots.append(tuple(where))
    return values.at[spots[0]].set(low).at[spots[1]].set(top_value)


def level_of(key, extent, cuts, smallest, top_value):
    def one(dim, parts):
        steps = jax.random.uniform(jax.random.fold_in(jax.random.fold_in(key, 6), dim), (parts,), jnp.float32, smallest / len(cuts), top_value / len(cuts))
        return jnp.repeat(jnp.exp(steps), extent[dim] // parts).reshape((-1,) + (1,) * (len(extent) - dim - 1))

    level = one(*cuts[0])
    for cut in cuts[1:]:
        level = level * one(*cut)
    return level


def gaussian(key, extent, scale, limit, shards=(), held_as=jnp.bfloat16):
    values = jax.random.normal(key, extent, jnp.float32) * scale
    if len(shards) > 0:
        values = level_of(key, extent, shards, -0.22, 0.18) * values
    return jnp.clip(values, min=-limit, max=limit).astype(held_as)


def setup_inputs(seed: int = 0) -> dict:
    arg_keys = jax.random.split(jax.random.key(seed), 17)
    return {
        "tokens": gaussian(arg_keys[0], (TOKENS, D), 1.0, 6.0, ((0, 8),)),
        "row_length": draw_row_length(jax.random.fold_in(arg_keys[16], 71), 0),
        "row_group": draw_row_group(jax.random.fold_in(arg_keys[16], 71), 0),
        "row_step": place_ends(jax.random.randint(arg_keys[3], (ROWS,), 0, STEPS), jax.random.fold_in(arg_keys[3], 1), 0, STEPS - 1).astype(jnp.int32),
        "time_table": gaussian(arg_keys[4], (STEPS, D), 0.5, 3.0),
        "norm1_gain": jnp.clip(1.0 + 0.18 * jax.random.normal(arg_keys[5], (D,), jnp.float32), 0.1, 1.9),
        "norm1_bias": gaussian(arg_keys[6], (D,), 0.3, 1.75, (), jnp.float32),
        "w_qkv": gaussian(arg_keys[7], (D, 3, HD), D ** -0.5, 0.21875, ((2, 4),)),
        "w_out": gaussian(arg_keys[8], (HD, D), (max(HD // 128, 1)) ** -0.5, 2.5, ((0, 4),)),
        "norm2_gain": jnp.clip(1.0 + 0.18 * jax.random.normal(arg_keys[9], (D,), jnp.float32), 0.1, 1.9),
        "norm2_bias": gaussian(arg_keys[10], (D,), 0.3, 1.75, (), jnp.float32),
        "w_up": gaussian(arg_keys[11], (D, FF), D ** -0.5, 0.21875, ((1, 4),)),
        "up_bias": gaussian(arg_keys[12], (FF,), 0.5, 3.0, ((0, 4),), jnp.float32),
        "w_down": gaussian(arg_keys[13], (FF, D), (FF // 4) ** -0.5, 0.21875, ((0, 4),)),
        "down_bias": gaussian(arg_keys[14], (D,), 0.3, 1.75, (), jnp.float32),
        "cotangent": gaussian(arg_keys[15], (TOKENS, D), 1.0, 6.0, ((0, 8),)),
    }


EPS = 1e-05
NEG = -1000000000.0
HIGHEST = lax.Precision.HIGHEST

@jax.custom_vjp
def low(v):
    return lax.optimization_barrier(v.astype(jnp.bfloat16)).astype(jnp.float32)

@jax.custom_vjp
def low_back(v):
    return v

def low_keep(v):
    return (low(v), None)

def low_pass(kept, grad):
    return (grad,)

def back_keep(v):
    return (v, None)

def back_low(kept, grad):
    return (low(grad),)
low.defvjp(low_keep, low_pass)
low_back.defvjp(back_keep, back_low)

def normalize(values, gain, bias):
    row_mean = lax.optimization_barrier(jnp.mean(values, axis=-1, keepdims=True))
    centred = values - row_mean
    variance = lax.optimization_barrier(jnp.mean(centred * centred, axis=-1, keepdims=True))
    return centred * lax.rsqrt(variance + EPS) * gain + bias

def row_offsets(row_length, row_group):
    row_number = jnp.arange(row_length.shape[0], dtype=jnp.int32)
    order_key = jnp.where(row_length > SHORT, 0, row_length.shape[0]) + row_number
    same_group = row_group[:, None] == row_group[None, :]
    earlier = same_group & (order_key[None, :] < order_key[:, None])
    return lax.optimization_barrier(jnp.sum(jnp.where(earlier, row_length[None, :], 0), axis=1)).astype(jnp.int32)

def token_rows(offsets, row_length, row_group, row_step, group_index):
    row_number = jnp.arange(row_length.shape[0], dtype=jnp.int32)
    position = jnp.arange(TOK_DEV, dtype=jnp.int32)
    member = (row_group[None, :] == group_index) & (position[:, None] >= offsets[None, :]) & (position[:, None] < (offsets + row_length)[None, :])
    token_row = lax.optimization_barrier(jnp.sum(jnp.where(member, row_number[None, :], 0), axis=1)).astype(jnp.int32)
    token_step = lax.optimization_barrier(jnp.sum(jnp.where(member, row_step[None, :], 0), axis=1)).astype(jnp.int32)
    return (token_row, token_step)

def group_layer(params, tokens_group, token_row, token_step):
    time_table, norm1_gain, norm1_bias, w_qkv, w_out, norm2_gain, norm2_bias, w_up, up_bias, w_down, down_bias = params
    scale_factor = HEAD_DIM ** (-0.5)
    blocks = TOK_DEV // BLOCK
    heads_local = HEADS // N_TENSOR
    width_local = heads_local * HEAD_DIM
    units_local = FF // N_TENSOR
    hidden_in = tokens_group + jnp.take(time_table, token_step, axis=0)
    normed = low(normalize(hidden_in, norm1_gain, norm1_bias))
    block_rows = token_row.reshape(blocks, BLOCK)
    allowed = block_rows[:, None, :, None] == block_rows[:, None, None, :]
    attended = jnp.zeros_like(hidden_in)
    for column_group in range(N_TENSOR):
        normed_copy = low_back(normed)
        lower = column_group * width_local
        projected = []
        for which in range(3):
            weight = w_qkv[:, which, lower:lower + width_local]
            result = low(low_back(jnp.dot(normed_copy, weight, precision=HIGHEST)))
            projected.append(result.reshape(blocks, BLOCK, heads_local, HEAD_DIM))
        query_block, key_block, value_block = projected
        scores = low_back(jnp.einsum('bqhd,bkhd->bhqk', query_block, key_block, precision=HIGHEST) * scale_factor)
        scores = jnp.where(allowed, scores, NEG)
        attention = jnp.exp(scores - jax.nn.logsumexp(scores, axis=-1, keepdims=True))
        context = jnp.einsum('bhqk,bkhd->bqhd', low(attention), value_block, precision=HIGHEST).reshape(TOK_DEV, width_local)
        context = low(low_back(context))
        attended = attended + low_back(low(jnp.dot(context, w_out[lower:lower + width_local], precision=HIGHEST)))
    residual = hidden_in + attended
    normed_two = low(normalize(residual, norm2_gain, norm2_bias))
    expanded = jnp.zeros_like(hidden_in)
    for column_group in range(N_TENSOR):
        normed_copy = low_back(normed_two)
        lower = column_group * units_local
        pre_act = low_back(jnp.dot(normed_copy, w_up[:, lower:lower + units_local], precision=HIGHEST)) + up_bias[lower:lower + units_local]
        activated = low(jax.nn.gelu(pre_act, approximate=False))
        expanded = expanded + low_back(low(jnp.dot(activated, w_down[lower:lower + units_local], precision=HIGHEST)))
    return residual + expanded + down_bias

def reference(tokens, row_length, row_group, row_step, time_table, norm1_gain, norm1_bias, w_qkv, w_out, norm2_gain, norm2_bias, w_up, up_bias, w_down, down_bias, cotangent):
    offsets = row_offsets(row_length, row_group)
    token_row, token_step = lax.map(lambda g: token_rows(offsets, row_length, row_group, row_step, g), jnp.arange(N_DP, dtype=jnp.int32))
    params = tuple((item.astype(jnp.float32) for item in (time_table, norm1_gain, norm1_bias, w_qkv, w_out, norm2_gain, norm2_bias, w_up, up_bias, w_down, down_bias)))
    x_groups = tokens.astype(jnp.float32).reshape(N_DP, TOK_DEV, D)
    layer_step = jax.checkpoint(group_layer)

    def forward(x_groups, params):

        def scan_step(carry, inputs):
            return (carry, layer_step(params, inputs[0], inputs[1], inputs[2]))
        final_carry, outputs = lax.scan(scan_step, jnp.zeros((), jnp.float32), (x_groups, token_row, token_step))
        return outputs
    outputs, pullback = jax.vjp(forward, x_groups, params)
    grad_x, grad_params = pullback(cotangent.astype(jnp.float32).reshape(N_DP, TOK_DEV, D))
    time_grad, gain1_grad, bias1_grad, qkv_grad, out_proj_grad, gain2_grad, bias2_grad, up_grad, up_bias_grad, down_grad, down_bias_grad = grad_params
    return (outputs.reshape(TOKENS, D).astype(jnp.bfloat16), grad_x.reshape(TOKENS, D).astype(jnp.bfloat16), time_grad, gain1_grad, bias1_grad, qkv_grad, out_proj_grad, gain2_grad, bias2_grad, up_grad, up_bias_grad, down_grad, down_bias_grad)
```

```python
import functools

import jax
import jax.numpy as jnp
from jax import lax
from jax.experimental import pallas as pl
from jax.experimental.pallas import tpu as pltpu
from jax.sharding import PartitionSpec as P

HEAD_DIM = 64
SHORT = 128
PAIR = 256
EPS = 1e-05
NEG = -1000000000.0
SQRT_HALF = 0.7071067811865476
PHI_ZERO = 0.3989422804014327
CHUNKS = 1
VMEM_MB = 40

F32 = jnp.float32
BF16 = jnp.bfloat16


def mm(left, right, left_dim, right_dim):
    return lax.dot_general(
        left, right, (((left_dim,), (right_dim,)), ((), ())), preferred_element_type=F32
    )


def params(dims=1):
    return pltpu.CompilerParams(
        dimension_semantics=("arbitrary",) * dims, vmem_limit_bytes=VMEM_MB << 20
    )


def cost(flops, nbytes):
    return pl.CostEstimate(flops=int(flops), bytes_accessed=int(nbytes), transcendentals=0)


def shape(dims, dtype):
    return jax.ShapeDtypeStruct(dims, dtype)


def whole(array):
    zeros = (0,) * array.ndim
    return pl.BlockSpec(array.shape, lambda *_: zeros)


def core_swap(value):
    pairs = [(i, i ^ 1) for i in range(lax.axis_size("tensor"))]
    return lax.ppermute(value, "tensor", pairs)


def chip_swap(value):
    pairs = [(i, i ^ 2) for i in range(lax.axis_size("tensor"))]
    return lax.ppermute(value, "tensor", pairs)


def dp_swap(value, bit):
    pairs = [(i, i ^ bit) for i in range(lax.axis_size("dp"))]
    return lax.ppermute(value, "dp", pairs)


def norm_stats(values):
    mean = jnp.mean(values, axis=-1, keepdims=True)
    centred = values - mean
    variance = jnp.mean(centred * centred, axis=-1, keepdims=True)
    scale = lax.rsqrt(variance + EPS)
    return centred * scale, scale


def fill_slots(slot_ref, group, row_length, row_group, row_step):
    rows = row_length.shape[0]

    def long_row(r, pos):
        slot_ref[pos] = row_step[r]
        slot_ref[pos + 1] = row_step[r]
        hit = (row_group[r] == group) & (row_length[r] > SHORT)
        return pos + jnp.where(hit, 2, 0)

    def short_row(r, pos):
        slot_ref[pos] = row_step[r]
        hit = (row_group[r] == group) & (row_length[r] <= SHORT)
        return pos + jnp.where(hit, 1, 0)

    long_slots = lax.fori_loop(0, rows, long_row, 0)
    lax.fori_loop(0, rows, short_row, long_slots)
    return long_slots


def block_of(i, ids, chunk, half, chunks):
    side = jnp.where(i < half, 1 - ids[0], ids[0])
    return side * (half * chunks) + chunk * half + lax.rem(i, half)


def attend_kernel(
    chunk, half, chunks, slots, ids, row_length, row_group, row_step,
    tokens, table, gain, bias, wq, wk, wv, wo,
    send, keep, hidden_out, normed_out, q_out, k_out, v_out, p_out, c_out,
    slot_ref, rows_ref, sems,
):
    i = pl.program_id(0)

    def fetch(s):
        step = slot_ref[s]
        start = pl.multiple_of((step // 8) * 8, 8)
        return pltpu.make_async_copy(table.at[pl.ds(start, 8), :], rows_ref.at[s], sems.at[s])

    @pl.when(i == 0)
    def _():
        slot_ref[slots + 2] = fill_slots(slot_ref, ids[1], row_length, row_group, row_step)
        for s in range(slots):
            fetch(s).start()
        for s in range(slots):
            fetch(s).wait()

    block = block_of(i, ids, chunk, half, chunks)
    sub = lax.broadcasted_iota(jnp.int32, (8, 1), 0)

    def row_of(s):
        picked = sub == lax.rem(slot_ref[s], 8)
        return jnp.sum(jnp.where(picked, rows_ref[s].astype(F32), 0.0), axis=0, keepdims=True)

    low_half = lax.broadcasted_iota(jnp.int32, (PAIR, 1), 0) < SHORT
    step_row = jnp.where(low_half, row_of(2 * block), row_of(2 * block + 1))
    hidden = tokens[...].astype(F32) + step_row
    unit, _ = norm_stats(hidden)
    normed = (unit * gain[...] + bias[...]).astype(BF16)
    normed_out[...] = normed
    q = mm(normed, wq[...], 1, 0).astype(BF16)
    k = mm(normed, wk[...], 1, 0).astype(BF16)
    v = mm(normed, wv[...], 1, 0).astype(BF16)
    q_out[...] = q
    k_out[...] = k
    v_out[...] = v
    split = (2 * block >= slot_ref[slots + 2]).astype(jnp.int32)
    row_half = lax.broadcasted_iota(jnp.int32, (PAIR, PAIR), 0) // SHORT
    col_half = lax.broadcasted_iota(jnp.int32, (PAIR, PAIR), 1) // SHORT
    allowed = ((row_half ^ col_half) * split) == 0
    width = q.shape[1]
    head = lax.broadcasted_iota(jnp.int32, (1, width), 1) // HEAD_DIM
    context = jnp.zeros((PAIR, width), F32)
    for h in range(width // HEAD_DIM):
        mine = head == h
        qh = jnp.where(mine, q, jnp.zeros_like(q))
        scores = mm(qh, k, 1, 1) * (HEAD_DIM**-0.5)
        scores = jnp.where(allowed, scores, NEG)
        top = jnp.max(scores, axis=-1, keepdims=True)
        powers = jnp.exp(scores - top)
        total = jnp.sum(powers, axis=-1, keepdims=True)
        weights = (powers * (1.0 / total)).astype(BF16)
        p_out[0, h] = weights
        context = context + mm(weights, jnp.where(mine, v, jnp.zeros_like(v)), 1, 0)
    low = context.astype(BF16)
    c_out[...] = low
    part = mm(low, wo[...], 1, 0).astype(BF16)

    @pl.when(i < half)
    def _():
        send[...] = part

    @pl.when(i >= half)
    def _():
        keep[...] = part
        hidden_out[...] = hidden


def attend(chunk, chunks, scalars, tokens, table, gain, bias, wq, wk, wv, wo):
    count, width = tokens.shape
    local = wo.shape[0]
    blocks = count // PAIR // chunks
    half = blocks // 2
    rows = blocks * PAIR
    slots = count // SHORT
    own = rows // 2
    heads = local // HEAD_DIM
    first = lambda i, *_: (jnp.minimum(i, half - 1), 0)
    second = lambda i, *_: (jnp.maximum(i - half, 0), 0)
    step = lambda i, *_: (i, 0)
    row = pl.BlockSpec((PAIR, width), step)
    thin = pl.BlockSpec((PAIR, local), step)
    return pl.pallas_call(
        functools.partial(attend_kernel, chunk, half, chunks, slots),
        grid_spec=pltpu.PrefetchScalarGridSpec(
            num_scalar_prefetch=4,
            grid=(blocks,),
            in_specs=[
                pl.BlockSpec((PAIR, width), lambda i, ids, *_: (block_of(i, ids, chunk, half, chunks), 0)),
                pl.BlockSpec(memory_space=pl.ANY),
                whole(gain), whole(bias), whole(wq), whole(wk), whole(wv), whole(wo),
            ],
            out_specs=[
                pl.BlockSpec((PAIR, width), first),
                pl.BlockSpec((PAIR, width), second),
                pl.BlockSpec((PAIR, width), second),
                row, thin, thin, thin,
                pl.BlockSpec((1, heads, PAIR, PAIR), lambda i, *_: (i, 0, 0, 0)),
                thin,
            ],
            scratch_shapes=[
                pltpu.SMEM((slots + 4,), jnp.int32),
                pltpu.VMEM((slots, 8, width), BF16),
                pltpu.SemaphoreType.DMA((slots,)),
            ],
        ),
        out_shape=[
            shape((own, width), BF16), shape((own, width), BF16), shape((own, width), F32),
            shape((rows, width), BF16),
            shape((rows, local), BF16), shape((rows, local), BF16), shape((rows, local), BF16),
            shape((blocks, heads, PAIR, PAIR), BF16),
            shape((rows, local), BF16),
        ],
        compiler_params=params(),
        cost_estimate=cost(rows * width * local * 8, rows * width * 8),
        name="attend",
    )(*scalars, tokens, table, gain, bias, wq, wk, wv, wo)


def mid_kernel(hidden, pair, other, gain, bias, residual_out, normed_out):
    residual = hidden[...] + (pair[...].astype(F32) + other[...].astype(F32))
    residual_out[...] = residual
    unit, _ = norm_stats(residual)
    normed_out[...] = (unit * gain[...] + bias[...]).astype(BF16)


def mid_forward(hidden, pair, other, gain, bias):
    rows, width = hidden.shape
    row = pl.BlockSpec((PAIR, width), lambda i: (i, 0))
    return pl.pallas_call(
        mid_kernel,
        grid=(rows // PAIR,),
        in_specs=[row, row, row, whole(gain), whole(bias)],
        out_specs=[row, row],
        out_shape=[shape((rows, width), F32), shape((rows, width), BF16)],
        compiler_params=params(),
        cost_estimate=cost(rows * width * 12, rows * width * 14),
        name="mid_forward",
    )(hidden, pair, other, gain, bias)


def expand_kernel(half, ids, peer, own, cot, w_up, up_bias, w_down, send, keep, act_out, low_out, bias_out):
    i = pl.program_id(0)
    normed = jnp.where(i < half, peer[...], own[...])
    pre = mm(normed, w_up[...], 1, 0) + up_bias[...]
    grad_act = mm(cot[...], w_down[...], 1, 1)
    cdf = 0.5 * (1.0 + lax.erf(pre * SQRT_HALF))
    act_out[...] = (pre * cdf).astype(BF16)
    slope = cdf + pre * (PHI_ZERO * jnp.exp(-0.5 * (pre * pre)))
    grad_pre = grad_act * slope

    @pl.when(i == 0)
    def _():
        bias_out[...] = jnp.zeros_like(bias_out)

    bias_out[...] += jnp.sum(grad_pre, axis=0, keepdims=True)
    low = grad_pre.astype(BF16)
    low_out[...] = low
    part = mm(low, w_up[...], 1, 1).astype(BF16)

    @pl.when(i < half)
    def _():
        send[...] = part

    @pl.when(i >= half)
    def _():
        keep[...] = part


def expand(chunk, chunks, ids, peer, own, cot, w_up, up_bias, w_down):
    count, width = cot.shape
    local = w_up.shape[1]
    blocks = count // PAIR // chunks
    half = blocks // 2
    rows = blocks * PAIR
    first = lambda i, *_: (jnp.minimum(i, half - 1), 0)
    second = lambda i, *_: (jnp.maximum(i - half, 0), 0)
    step = lambda i, *_: (i, 0)
    return pl.pallas_call(
        functools.partial(expand_kernel, half),
        grid_spec=pltpu.PrefetchScalarGridSpec(
            num_scalar_prefetch=1,
            grid=(blocks,),
            in_specs=[
                pl.BlockSpec((PAIR, width), first),
                pl.BlockSpec((PAIR, width), second),
                pl.BlockSpec((PAIR, width), lambda i, ids: (block_of(i, ids, chunk, half, chunks), 0)),
                whole(w_up), whole(up_bias), whole(w_down),
            ],
            out_specs=[
                pl.BlockSpec((PAIR, width), first),
                pl.BlockSpec((PAIR, width), second),
                pl.BlockSpec((PAIR, local), step),
                pl.BlockSpec((PAIR, local), step),
                whole(up_bias),
            ],
        ),
        out_shape=[
            shape((rows // 2, width), BF16), shape((rows // 2, width), BF16),
            shape((rows, local), BF16), shape((rows, local), BF16),
            shape((1, local), F32),
        ],
        compiler_params=params(),
        cost_estimate=cost(rows * width * local * 6, rows * width * 12),
        name="expand",
    )(ids, peer, own, cot, w_up, up_bias, w_down)


def contract_kernel(half, act, w_down, send, keep):
    i = pl.program_id(0)
    part = mm(act[...], w_down[...], 1, 0).astype(BF16)

    @pl.when(i < half)
    def _():
        send[...] = part

    @pl.when(i >= half)
    def _():
        keep[...] = part


def contract_rows(act, w_down):
    rows, local = act.shape
    width = w_down.shape[1]
    blocks = rows // PAIR
    half = blocks // 2
    return pl.pallas_call(
        functools.partial(contract_kernel, half),
        grid=(blocks,),
        in_specs=[pl.BlockSpec((PAIR, local), lambda i: (i, 0)), whole(w_down)],
        out_specs=[
            pl.BlockSpec((PAIR, width), lambda i: (jnp.minimum(i, half - 1), 0)),
            pl.BlockSpec((PAIR, width), lambda i: (jnp.maximum(i - half, 0), 0)),
        ],
        out_shape=[shape((rows // 2, width), BF16), shape((rows // 2, width), BF16)],
        compiler_params=params(),
        cost_estimate=cost(rows * width * local * 2, rows * width * 4),
        name="contract_rows",
    )(act, w_down)


def weight_kernel(pieces, *refs):
    left, right, out = refs[1 : 1 + pieces], refs[1 + pieces : 1 + 2 * pieces], refs[-1]
    total = mm(left[0][...], right[0][...], 0, 0)
    for a, b in zip(left[1:], right[1:]):
        total = total + mm(a[...], b[...], 0, 0)
    out[...] = total.astype(BF16)


def weight_grad(ids, lefts, rights, tiles, name):
    pieces = len(lefts)
    rows_out = lefts[0][0].shape[1]
    tile = rows_out // tiles
    cols = rights[0][0].shape[1]
    count = sum(size for _, size, _ in lefts)
    specs = [pl.BlockSpec((size, tile), lambda i, ids, at=at: (at(ids), i)) for _, size, at in lefts]
    specs += [pl.BlockSpec((size, cols), lambda i, ids, at=at: (at(ids), 0)) for _, size, at in rights]
    return pl.pallas_call(
        functools.partial(weight_kernel, pieces),
        grid_spec=pltpu.PrefetchScalarGridSpec(
            num_scalar_prefetch=1,
            grid=(tiles,),
            in_specs=specs,
            out_specs=pl.BlockSpec((tile, cols), lambda i, ids: (i, 0)),
        ),
        out_shape=shape((rows_out, cols), BF16),
        compiler_params=params(),
        cost_estimate=cost(2 * count * rows_out * cols, 2 * (count * (rows_out + cols) + rows_out * cols)),
        name=name,
    )(ids, *[a for a, _, _ in lefts], *[b for b, _, _ in rights])


def mid_back_kernel(pair, other, residual, cot, gain, grad_out, low_out, sums):
    i = pl.program_id(0)
    err = pair[...].astype(F32) + other[...].astype(F32)
    unit, scale = norm_stats(residual[...])
    top = cot[...].astype(F32)
    f = err * gain[...]
    f_mean = jnp.mean(f, axis=-1, keepdims=True)
    fx_mean = jnp.mean(f * unit, axis=-1, keepdims=True)
    grad = top + scale * (f - f_mean - unit * fx_mean)
    grad_out[...] = grad
    low_out[...] = grad.astype(BF16)

    @pl.when(i == 0)
    def _():
        sums[...] = jnp.zeros_like(sums)

    sums[0:1] += jnp.sum(err * unit, axis=0, keepdims=True)
    sums[1:2] += jnp.sum(err, axis=0, keepdims=True)
    sums[2:3] += jnp.sum(top, axis=0, keepdims=True)


def mid_back(chunk, chunks, ids, pair, other, residual, cot, gain):
    rows, width = residual.shape
    half = rows // PAIR
    row = pl.BlockSpec((PAIR, width), lambda i, ids: (i, 0))
    return pl.pallas_call(
        lambda ids, *refs: mid_back_kernel(*refs),
        grid_spec=pltpu.PrefetchScalarGridSpec(
            num_scalar_prefetch=1,
            grid=(half,),
            in_specs=[
                row, row, row,
                pl.BlockSpec((PAIR, width), lambda i, ids: (block_of(i + half, ids, chunk, half, chunks), 0)),
                whole(gain),
            ],
            out_specs=[row, row, pl.BlockSpec((8, width), lambda i, ids: (0, 0))],
        ),
        out_shape=[shape((rows, width), F32), shape((rows, width), BF16), shape((8, width), F32)],
        compiler_params=params(),
        cost_estimate=cost(rows * width * 20, rows * width * 16),
        name="mid_back",
    )(ids, pair, other, residual, cot, gain)


def attend_back_kernel(half, peer, own, q_ref, k_ref, v_ref, p_ref, wq, wk, wv, wo, send, keep, dq_out, dk_out, dv_out):
    i = pl.program_id(0)
    low = jnp.where(i < half, peer[...], own[...])
    grad_context = mm(low, wo[...], 1, 1).astype(BF16)
    q, k, v = q_ref[...], k_ref[...], v_ref[...]
    width = q.shape[1]
    head = lax.broadcasted_iota(jnp.int32, (1, width), 1) // HEAD_DIM
    zero = jnp.zeros_like(q)
    dq = dk = dv = jnp.zeros((PAIR, width), F32)
    for h in range(width // HEAD_DIM):
        mine = head == h
        gh = jnp.where(mine, grad_context, zero)
        weights = p_ref[0, h]
        grad_p = mm(gh, v, 1, 1)
        wide = weights.astype(F32)
        dot = jnp.sum(wide * grad_p, axis=-1, keepdims=True)
        grad_s = (wide * (grad_p - dot)).astype(BF16)
        dv = dv + mm(weights, gh, 0, 0)
        dq = dq + mm(grad_s, jnp.where(mine, k, zero), 1, 0)
        dk = dk + mm(grad_s, jnp.where(mine, q, zero), 0, 0)
    scale = HEAD_DIM**-0.5
    dq = (dq * scale).astype(BF16)
    dk = (dk * scale).astype(BF16)
    dv = dv.astype(BF16)
    dq_out[...] = dq
    dk_out[...] = dk
    dv_out[...] = dv
    part = (mm(dq, wq[...], 1, 1) + mm(dk, wk[...], 1, 1) + mm(dv, wv[...], 1, 1)).astype(BF16)

    @pl.when(i < half)
    def _():
        send[...] = part

    @pl.when(i >= half)
    def _():
        keep[...] = part


def attend_back(peer, own, q, k, v, p, wq, wk, wv, wo):
    rows, local = q.shape
    width = wo.shape[1]
    blocks = rows // PAIR
    half = blocks // 2
    heads = local // HEAD_DIM
    first = pl.BlockSpec((PAIR, width), lambda i: (jnp.minimum(i, half - 1), 0))
    second = pl.BlockSpec((PAIR, width), lambda i: (jnp.maximum(i - half, 0), 0))
    thin = pl.BlockSpec((PAIR, local), lambda i: (i, 0))
    return pl.pallas_call(
        functools.partial(attend_back_kernel, half),
        grid=(blocks,),
        in_specs=[
            first, second, thin, thin, thin,
            pl.BlockSpec((1, heads, PAIR, PAIR), lambda i: (i, 0, 0, 0)),
            whole(wq), whole(wk), whole(wv), whole(wo),
        ],
        out_specs=[first, second, thin, thin, thin],
        out_shape=[
            shape((rows // 2, width), BF16), shape((rows // 2, width), BF16),
            shape((rows, local), BF16), shape((rows, local), BF16), shape((rows, local), BF16),
        ],
        compiler_params=params(),
        cost_estimate=cost(rows * width * local * 8, rows * width * 10),
        name="attend_back",
    )(peer, own, q, k, v, p, wq, wk, wv, wo)


def last_kernel(pair, other, hidden, grad_residual, gain, low_out, sums, times):
    i = pl.program_id(0)
    err = pair[...].astype(F32) + other[...].astype(F32)
    unit, scale = norm_stats(hidden[...])
    f = err * gain[...]
    f_mean = jnp.mean(f, axis=-1, keepdims=True)
    fx_mean = jnp.mean(f * unit, axis=-1, keepdims=True)
    grad = grad_residual[...] + scale * (f - f_mean - unit * fx_mean)
    low_out[...] = grad.astype(BF16)

    @pl.when(i == 0)
    def _():
        sums[...] = jnp.zeros_like(sums)

    sums[0:1] += jnp.sum(err * unit, axis=0, keepdims=True)
    sums[1:2] += jnp.sum(err, axis=0, keepdims=True)
    times[0, 0:1] = jnp.sum(grad[:SHORT], axis=0, keepdims=True)
    times[0, 1:2] = jnp.sum(grad[SHORT:], axis=0, keepdims=True)


def last_back(pair, other, hidden, grad_residual, gain):
    rows, width = hidden.shape
    half = rows // PAIR
    row = pl.BlockSpec((PAIR, width), lambda i: (i, 0))
    return pl.pallas_call(
        last_kernel,
        grid=(half,),
        in_specs=[row, row, row, row, whole(gain)],
        out_specs=[
            row,
            pl.BlockSpec((8, width), lambda i: (0, 0)),
            pl.BlockSpec((1, 2, width), lambda i: (i, 0, 0)),
        ],
        out_shape=[shape((rows, width), BF16), shape((8, width), F32), shape((half, 2, width), F32)],
        compiler_params=params(),
        cost_estimate=cost(rows * width * 20, rows * width * 16),
        name="last_back",
    )(pair, other, hidden, grad_residual, gain)


def time_kernel(slots, ids, row_length, row_group, row_step, sums, out, at_ref):
    groups = at_ref.shape[0]
    rows = row_length.shape[0]
    out[...] = jnp.zeros_like(out)

    def clear(g, _):
        at_ref[g] = 0
        return 0

    lax.fori_loop(0, groups, clear, 0)

    def place(long):
        def one(r, _):
            @pl.when((row_length[r] > SHORT) == long)
            def _():
                g = row_group[r]
                at = at_ref[g]
                at_ref[g] = at + (2 if long else 1)
                base = (g ^ ids[1]) * slots + at
                value = sums[pl.ds(base, 1), :]
                if long:
                    value = value + sums[pl.ds(base + 1, 1), :]
                step = pl.ds(row_step[r], 1)
                out[step, :] = out[step, :] + value

            return 0

        lax.fori_loop(0, rows, one, 0)

    place(True)
    place(False)


def time_table_grad(scalars, sums, steps, slots):
    width = sums.shape[1]
    groups = sums.shape[0] // slots
    return pl.pallas_call(
        functools.partial(time_kernel, slots),
        grid_spec=pltpu.PrefetchScalarGridSpec(
            num_scalar_prefetch=4,
            grid=(1,),
            in_specs=[whole(sums)],
            out_specs=pl.BlockSpec((steps, width), lambda *_: (0, 0)),
            scratch_shapes=[pltpu.SMEM((groups,), jnp.int32)],
        ),
        out_shape=shape((steps, width), F32),
        compiler_params=params(),
        cost_estimate=cost(steps * width, steps * width * 4),
        name="time_table_grad",
    )(*scalars, sums)


def add_low(a, b):
    return (a.astype(F32) + b.astype(F32)).astype(BF16)


def share(send, keep):
    pair = add_low(keep, core_swap(send))
    return pair, chip_swap(pair)


def in_order(core, own, other):
    return jnp.where(
        core == 0,
        jnp.concatenate([own, other], axis=0),
        jnp.concatenate([other, own], axis=0),
    )


def shards(
    tokens, row_length, row_group, row_step, time_table, norm1_gain, norm1_bias, w_qkv, w_out,
    norm2_gain, norm2_bias, w_up, up_bias, w_down, down_bias, cotangent,
):
    count, width = tokens.shape
    chunks = CHUNKS
    n_dp = lax.axis_size("dp")
    dp = lax.axis_index("dp")
    part = lax.axis_index("tensor")
    core = lax.rem(part, 2)
    ids = jnp.stack([core, dp, part, dp]).astype(jnp.int32)
    scalars = (ids, row_length, row_group, row_step)
    local = w_out.shape[0]
    slots = count // SHORT
    gain1, bias1 = norm1_gain[None], norm1_bias[None]
    gain2, bias2 = norm2_gain[None], norm2_bias[None]
    up_b = up_bias[None]
    wq, wk, wv = w_qkv[:, 0], w_qkv[:, 1], w_qkv[:, 2]
    size = count // 2 // chunks
    each = range(chunks)

    ahead = [attend(c, chunks, scalars, tokens, time_table, gain1, bias1, wq, wk, wv, w_out) for c in each]
    residual, own2, peer2 = [], [], []
    for c in each:
        pair, other = share(ahead[c][0], ahead[c][1])
        r, n = mid_forward(ahead[c][2], pair, other, gain2, bias2)
        residual.append(r)
        own2.append(n)
        peer2.append(core_swap(n))
    grown = [expand(c, chunks, ids, peer2[c], own2[c], cotangent, w_up, up_b, w_down) for c in each]

    peer_rows = lambda c: (lambda ids: (1 - ids[0]) * chunks + c)
    own_rows = lambda c: (lambda ids: ids[0] * chunks + c)
    zero = lambda ids: 0
    one = lambda ids: 1
    cots = [(cotangent, size, f(c)) for c in each for f in (peer_rows, own_rows)]
    acts = [(grown[c][2], size, f) for c in each for f in (zero, one)]
    lows = [(grown[c][3], size, f) for c in each for f in (zero, one)]
    norms = [(a[c], size, zero) for c in each for a in (peer2, own2)]
    down_grad = weight_grad(ids, acts, cots, 2, "down_grad")
    up_grad = weight_grad(ids, norms, lows, 2, "up_grad")
    down_sum, up_sum = lax.psum((down_grad, up_grad), "dp")

    back = []
    for c in each:
        pair, other = share(grown[c][0], grown[c][1])
        back.append(mid_back(c, chunks, ids, pair, other, residual[c], cotangent, gain2))
    peer_low = [core_swap(back[c][1]) for c in each]
    attn = [
        attend_back(peer_low[c], back[c][1], *ahead[c][4:8], wq, wk, wv, w_out) for c in each
    ]
    ctxs = [(ahead[c][8], size, f) for c in each for f in (zero, one)]
    lows1 = [(a, size, zero) for c in each for a in (peer_low[c], back[c][1])]
    norms1 = [(ahead[c][3], size, f) for c in each for f in (zero, one)]
    out_grad = weight_grad(ids, ctxs, lows1, 1, "out_grad")
    qkv = [
        weight_grad(ids, norms1, [(attn[c][j], size, f) for c in each for f in (zero, one)], 2, "qkv_grad")
        for j in (2, 3, 4)
    ]
    qkv_sum, out_sum = lax.psum((jnp.stack(qkv), out_grad), "dp")

    low_in, vec1, times = [], [], []
    for c in each:
        pair, other = share(attn[c][0], attn[c][1])
        a, b, t = last_back(pair, other, ahead[c][2], back[c][0], gain1)
        low_in.append(a)
        vec1.append(b)
        times.append(t.reshape(-1, width))

    finals = []
    for c in each:
        send, keep = contract_rows(grown[c][2], w_down)
        pair, other = share(send, keep)
        finals.append((residual[c] + (pair.astype(F32) + other.astype(F32)) + down_bias).astype(BF16))
    final = jnp.concatenate(finals, axis=0)
    block_output = in_order(core, final, core_swap(final))
    low_grad = jnp.concatenate(low_in, axis=0)
    input_grad = in_order(core, low_grad, core_swap(low_grad))

    own_vec = jnp.concatenate([sum(b[2] for b in back)[:3], sum(vec1)[:2]], axis=0)
    own_time = jnp.concatenate(times, axis=0)
    other_vec, other_time = core_swap((own_vec, own_time))
    vec = jnp.concatenate([own_vec + other_vec, sum(g[4] for g in grown)], axis=0)
    table = in_order(core, own_time, other_time)
    table = lax.dynamic_slice_in_dim(table, part * local, local, 1)
    bit = 1
    while bit < n_dp:
        got_vec, got_table = dp_swap((vec, table), bit)
        vec = vec + got_vec
        table = jnp.concatenate([table, got_table], axis=0)
        bit *= 2
    time_grad = time_table_grad(scalars, table, time_table.shape[0], slots)

    return (
        block_output,
        input_grad,
        time_grad,
        vec[3],
        vec[4],
        jnp.transpose(qkv_sum, (1, 0, 2)).astype(F32),
        out_sum.astype(F32),
        vec[0],
        vec[1],
        up_sum.astype(F32),
        vec[5],
        down_sum.astype(F32),
        vec[2],
    )


def solution(mesh):
    in_specs = (
        P("dp", None), P(), P(), P(), P(), P(), P(), P(None, None, "tensor"), P("tensor", None), P(), P(),
        P(None, "tensor"), P("tensor"), P("tensor", None), P(), P("dp", None),
    )
    out_specs = (
        P("dp", None), P("dp", None), P(None, "tensor"), P(), P(), P(None, None, "tensor"), P("tensor", None),
        P(), P(), P(None, "tensor"), P("tensor"), P("tensor", None), P(),
    )
    return jax.shard_map(shards, mesh=mesh, in_specs=in_specs, out_specs=out_specs, check_vma=False)
```

```python
import functools

import jax
import jax.numpy as jnp
from jax import lax
from jax.experimental import pallas as pl
from jax.experimental.pallas import tpu as pltpu
from jax.sharding import PartitionSpec as P

HEAD_DIM = 64
SHORT = 128
PAIR = 256
EPS = 1e-05
NEG = -1000000000.0
SQRT_HALF = 0.7071067811865476
PHI_ZERO = 0.3989422804014327
VMEM_MB = 16
SMALL_MB = 8

F32 = jnp.float32
BF16 = jnp.bfloat16


def mm(left, right, left_dim, right_dim):
    return lax.dot_general(
        left, right, (((left_dim,), (right_dim,)), ((), ())), preferred_element_type=F32
    )


def params(dims=1):
    return pltpu.CompilerParams(
        dimension_semantics=("arbitrary",) * dims, vmem_limit_bytes=VMEM_MB << 20
    )


COST_SCALE = 0.0


def cost(micros):
    return pl.CostEstimate(flops=int(micros * COST_SCALE * 1e9), bytes_accessed=int(micros * COST_SCALE * 3e6) + 1, transcendentals=0)


def shape(dims, dtype):
    return jax.ShapeDtypeStruct(dims, dtype)


def whole(array):
    zeros = (0,) * array.ndim
    return pl.BlockSpec(array.shape, lambda *_: zeros)


def swap(value, axis, bit, name):
    pairs = [(i, i ^ bit) for i in range(lax.axis_size(axis))]
    with jax.named_scope(name):
        return lax.ppermute(value, axis, pairs)


def core_swap(value, name="core", pieces=1):
    return swap_pieces(value, 1, name, pieces)


def swap_pieces(value, bit, name, pieces):
    if pieces == 1:
        return swap(value, "tensor", bit, name)
    rows = value.shape[0] // pieces
    parts = [swap(value[i * rows : (i + 1) * rows], "tensor", bit, name) for i in range(pieces)]
    return jnp.concatenate(parts, axis=0)


def chip_swap(value, name="chip", pieces=1):
    return swap_pieces(value, 2, name, pieces)


def dp_swap(value, bit, name="dp"):
    return swap(value, "dp", bit, name)


def norm_stats(values):
    mean = jnp.mean(values, axis=-1, keepdims=True)
    centred = values - mean
    variance = jnp.mean(centred * centred, axis=-1, keepdims=True)
    scale = lax.rsqrt(variance + EPS)
    return centred * scale, scale


IDS = 8


def row_fields(info):
    rows = (info.shape[0] - IDS) // 3
    return rows, [lambda r, at=at: info[IDS + at * rows + r] for at in range(3)]


def fill_slots(slot_ref, info):
    group = info[1]
    rows, (row_length, row_group, row_step) = row_fields(info)

    def long_row(r, pos):
        step = row_step(r)
        slot_ref[pos] = step
        slot_ref[pos + 1] = step
        hit = (row_group(r) == group) & (row_length(r) > SHORT)
        return pos + jnp.where(hit, 2, 0)

    def short_row(r, pos):
        slot_ref[pos] = row_step(r)
        hit = (row_group(r) == group) & (row_length(r) <= SHORT)
        return pos + jnp.where(hit, 1, 0)

    long_slots = lax.fori_loop(0, rows, long_row, 0)
    lax.fori_loop(0, rows, short_row, long_slots)
    return long_slots


def block_of(i, ids, chunk, half, chunks):
    side = jnp.where(i < half, 1 - ids[0], ids[0])
    return side * (half * chunks) + chunk * half + lax.rem(i, half)


def add_low(a, b):
    return (a.astype(F32) + b.astype(F32)).astype(BF16)


def row_vector(ref):
    return ref[...].reshape(1, ref.shape[0])


VM = pl.BlockSpec(memory_space=pltpu.VMEM)
ANY = pl.BlockSpec(memory_space=pl.ANY)


def small_call(kernel, out_shape, operands, after, name):
    count = len(operands)
    return pl.pallas_call(
        lambda *refs: kernel(*refs[:count], *refs[count + len(after) :]),
        in_specs=[VM] * count + [ANY] * len(after),
        out_specs=[VM] * len(out_shape),
        out_shape=out_shape,
        compiler_params=pltpu.CompilerParams(vmem_limit_bytes=SMALL_MB << 20),
        cost_estimate=cost(0.2),
        name=name,
    )(*operands, *after)


def add_two(a, b, after, name):
    def kernel(a_ref, b_ref, out):
        out[...] = add_low(a_ref[...], b_ref[...])

    return small_call(kernel, [shape(a.shape, BF16)], [a, b], after, name)[0]


def attend_kernel(
    chunk, half, chunks, slots, ids,
    tokens, table, gain, bias, w_qkv, wo,
    send, keep, hidden_out, normed_out, q_out, k_out, v_out, p_out, c_out,
    slot_ref, rows_ref, sems,
):
    i = pl.program_id(0)

    def fetch(s):
        step = slot_ref[s]
        start = pl.multiple_of((step // 8) * 8, 8)
        return pltpu.make_async_copy(table.at[pl.ds(start, 8), :], rows_ref.at[s], sems.at[s])

    @pl.when(i == 0)
    def _():
        slot_ref[slots + 2] = fill_slots(slot_ref, ids)
        for s in range(slots):
            fetch(s).start()
        for s in range(slots):
            fetch(s).wait()

    block = block_of(i, ids, chunk, half, chunks)
    sub = lax.broadcasted_iota(jnp.int32, (8, 1), 0)

    def row_of(s):
        picked = sub == lax.rem(slot_ref[s], 8)
        return jnp.sum(jnp.where(picked, rows_ref[s].astype(F32), 0.0), axis=0, keepdims=True)

    low_half = lax.broadcasted_iota(jnp.int32, (PAIR, 1), 0) < SHORT
    step_row = jnp.where(low_half, row_of(2 * block), row_of(2 * block + 1))
    hidden = tokens[...].astype(F32) + step_row
    unit, _ = norm_stats(hidden)
    normed = (unit * row_vector(gain) + row_vector(bias)).astype(BF16)
    normed_out[...] = normed
    q = mm(normed, w_qkv[0], 1, 1).astype(BF16)
    k = mm(normed, w_qkv[1], 1, 1).astype(BF16)
    v = mm(normed, w_qkv[2], 1, 1).astype(BF16)
    q_out[...] = q
    k_out[...] = k
    v_out[...] = v
    split = (2 * block >= slot_ref[slots + 2]).astype(jnp.int32)
    row_half = lax.broadcasted_iota(jnp.int32, (PAIR, PAIR), 0) // SHORT
    col_half = lax.broadcasted_iota(jnp.int32, (PAIR, PAIR), 1) // SHORT
    allowed = ((row_half ^ col_half) * split) == 0
    width = q.shape[1]
    head = lax.broadcasted_iota(jnp.int32, (1, width), 1) // HEAD_DIM
    context = jnp.zeros((PAIR, width), F32)
    for h in range(width // HEAD_DIM):
        mine = head == h
        qh = jnp.where(mine, q, jnp.zeros_like(q))
        scores = mm(qh, k, 1, 1) * (HEAD_DIM**-0.5)
        scores = jnp.where(allowed, scores, NEG)
        top = jnp.max(scores, axis=-1, keepdims=True)
        powers = jnp.exp(scores - top)
        total = jnp.sum(powers, axis=-1, keepdims=True)
        weights = (powers * (1.0 / total)).astype(BF16)
        p_out[0, h] = weights
        context = context + mm(weights, jnp.where(mine, v, jnp.zeros_like(v)), 1, 0)
    low = context.astype(BF16)
    c_out[...] = low
    part = mm(low, wo[...], 1, 0).astype(BF16)

    @pl.when(i < half)
    def _():
        send[...] = part

    @pl.when(i >= half)
    def _():
        keep[...] = part
        hidden_out[...] = hidden


def attend(chunk, chunks, scalars, tokens, table, gain, bias, w_qkv, wo, after):
    count, width = tokens.shape
    local = wo.shape[0]
    blocks = count // PAIR // chunks
    half = blocks // 2
    rows = blocks * PAIR
    slots = count // SHORT
    own = rows // 2
    heads = local // HEAD_DIM
    first = lambda i, *_: (jnp.minimum(i, half - 1), 0)
    second = lambda i, *_: (jnp.maximum(i - half, 0), 0)
    step = lambda i, *_: (i, 0)
    row = pl.BlockSpec((PAIR, width), step)
    thin = pl.BlockSpec((PAIR, local), step)
    return pl.pallas_call(
        lambda *refs: attend_kernel(chunk, half, chunks, slots, *refs[:7], *refs[7 + len(after) :]),
        grid_spec=pltpu.PrefetchScalarGridSpec(
            num_scalar_prefetch=1,
            grid=(blocks,),
            in_specs=[
                pl.BlockSpec((PAIR, width), lambda i, ids, *_: (block_of(i, ids, chunk, half, chunks), 0)),
                pl.BlockSpec(memory_space=pltpu.HBM),
                whole(gain), whole(bias), whole(w_qkv), whole(wo),
            ]
            + [ANY] * len(after),
            out_specs=[
                pl.BlockSpec((PAIR, width), first),
                pl.BlockSpec((PAIR, width), second),
                pl.BlockSpec((PAIR, width), second),
                row, thin, thin, thin,
                pl.BlockSpec((1, heads, PAIR, PAIR), lambda i, *_: (i, 0, 0, 0)),
                thin,
            ],
            scratch_shapes=[
                pltpu.SMEM((slots + 4,), jnp.int32),
                pltpu.VMEM((slots, 8, width), BF16),
                pltpu.SemaphoreType.DMA((slots,)),
            ],
        ),
        out_shape=[
            shape((own, width), BF16), shape((own, width), BF16), shape((own, width), F32),
            shape((rows, width), BF16),
            shape((rows, local), BF16), shape((rows, local), BF16), shape((rows, local), BF16),
            shape((blocks, heads, PAIR, PAIR), BF16),
            shape((rows, local), BF16),
        ],
        compiler_params=params(),
        cost_estimate=cost(4.5),
        name="attend",
    )(scalars, tokens, table, gain, bias, w_qkv, wo, *after)


def mid_kernel(hidden, pair, other, gain, bias, residual_out, normed_out):
    residual = hidden[...] + (pair[...].astype(F32) + other[...].astype(F32))
    residual_out[...] = residual
    unit, _ = norm_stats(residual)
    normed_out[...] = (unit * row_vector(gain) + row_vector(bias)).astype(BF16)


def mid_forward(hidden, pair, other, gain, bias, after):
    rows, width = hidden.shape
    row = pl.BlockSpec((PAIR, width), lambda i: (i, 0))
    return pl.pallas_call(
        lambda *refs: mid_kernel(*refs[:5], *refs[5 + len(after) :]),
        grid=(rows // PAIR,),
        in_specs=[row, row, row, whole(gain), whole(bias)] + [ANY] * len(after),
        out_specs=[row, row],
        out_shape=[shape((rows, width), F32), shape((rows, width), BF16)],
        compiler_params=params(),
        cost_estimate=cost(0.4),
        name="mid_forward",
    )(hidden, pair, other, gain, bias, *after)


def expand_kernel(half, ids, peer, own, cot, w_up, up_bias, w_down, send, keep, act_out, low_out, bias_out):
    i = pl.program_id(0)
    normed = jnp.where(i < half, peer[...], own[...])
    pre = mm(normed, w_up[...], 1, 0) + row_vector(up_bias)
    grad_act = mm(cot[...], w_down[...], 1, 1)
    cdf = 0.5 * (1.0 + lax.erf(pre * SQRT_HALF))
    act_out[...] = (pre * cdf).astype(BF16)
    slope = cdf + pre * (PHI_ZERO * jnp.exp(-0.5 * (pre * pre)))
    grad_pre = grad_act * slope

    @pl.when(i == 0)
    def _():
        bias_out[...] = jnp.zeros_like(bias_out)

    bias_out[...] += jnp.sum(grad_pre, axis=0, keepdims=True)
    low = grad_pre.astype(BF16)
    low_out[...] = low
    part = mm(low, w_up[...], 1, 1).astype(BF16)

    @pl.when(i < half)
    def _():
        send[...] = part

    @pl.when(i >= half)
    def _():
        keep[...] = part


def expand(chunk, chunks, ids, peer, own, cot, w_up, up_bias, w_down, after):
    count, width = cot.shape
    local = w_up.shape[1]
    blocks = count // PAIR // chunks
    half = blocks // 2
    rows = blocks * PAIR
    first = lambda i, *_: (jnp.minimum(i, half - 1), 0)
    second = lambda i, *_: (jnp.maximum(i - half, 0), 0)
    step = lambda i, *_: (i, 0)
    return pl.pallas_call(
        lambda *refs: expand_kernel(half, *refs[:7], *refs[7 + len(after) :]),
        grid_spec=pltpu.PrefetchScalarGridSpec(
            num_scalar_prefetch=1,
            grid=(blocks,),
            in_specs=[
                pl.BlockSpec((PAIR, width), first),
                pl.BlockSpec((PAIR, width), second),
                pl.BlockSpec((PAIR, width), lambda i, ids: (block_of(i, ids, chunk, half, chunks), 0)),
                whole(w_up), whole(up_bias), whole(w_down),
            ]
            + [ANY] * len(after),
            out_specs=[
                pl.BlockSpec((PAIR, width), first),
                pl.BlockSpec((PAIR, width), second),
                pl.BlockSpec((PAIR, local), step),
                pl.BlockSpec((PAIR, local), step),
                pl.BlockSpec((1, local), lambda i, *_: (0, 0)),
            ],
        ),
        out_shape=[
            shape((rows // 2, width), BF16), shape((rows // 2, width), BF16),
            shape((rows, local), BF16), shape((rows, local), BF16),
            shape((1, local), F32),
        ],
        compiler_params=params(),
        cost_estimate=cost(3.7),
        name="expand",
    )(ids, peer, own, cot, w_up, up_bias, w_down, *after)


def contract_kernel(act, w_down, send, keep):
    i = pl.program_id(0)
    part = mm(act[...], w_down[...], 1, 0).astype(BF16)

    @pl.when(i < 2)
    def _():
        send[...] = part

    @pl.when(i >= 2)
    def _():
        keep[...] = part


def contract_rows(act, w_down, after):
    rows, local = act.shape
    width = w_down.shape[1]
    return pl.pallas_call(
        lambda *refs: contract_kernel(*refs[:2], *refs[2 + len(after) :]),
        grid=(rows // PAIR,),
        in_specs=[pl.BlockSpec((PAIR, local), lambda i: (i, 0)), whole(w_down)] + [ANY] * len(after),
        out_specs=[
            pl.BlockSpec((PAIR, width), lambda i: (jnp.minimum(i, 1), 0)),
            pl.BlockSpec((PAIR, width), lambda i: (jnp.maximum(i - 2, 0), 0)),
        ],
        out_shape=[shape((rows // 2, width), BF16), shape((rows // 2, width), BF16)],
        compiler_params=params(),
        cost_estimate=cost(2.1),
        name="contract_rows",
    )(act, w_down, *after)


def weight_kernel(order, groups, ids, *refs):
    count = sum(len(lefts) for lefts in groups)
    left, right = refs[:count], refs[count : 2 * count]
    send, keep, scratch = refs[2 * count : 2 * count + 3]
    i = pl.program_id(0)
    many = len(groups) > 1
    rows = send.shape[-2]
    at = 0
    for n, sizes in enumerate(groups):
        total = mm(left[at][...], right[at][...], 0, 0)
        for j in range(at + 1, at + len(sizes)):
            total = total + mm(left[j][...], right[j][...], 0, 0)
        at += len(sizes)
        scratch[n] = total

    def write(out):
        for r in range(4):
            start = pl.multiple_of((ids[order + 1] ^ r) * rows, 8)
            for n in range(len(groups)):
                value = scratch[n, pl.ds(start, rows), :].astype(BF16)
                if many:
                    out[r, n] = value
                else:
                    out[r] = value

    @pl.when(i == 0)
    def _():
        write(send)

    @pl.when(i == 1)
    def _():
        write(keep)


def weight_grad(ids, order, groups, after, name):
    rows_out = groups[0][0][0][0].shape[1]
    tile = rows_out // 2
    part = tile // 4
    cols = groups[0][0][1][0].shape[1]
    lefts = [left for pieces in groups for left, _ in pieces]
    rights = [right for pieces in groups for _, right in pieces]
    count = sum(size for _, size, _ in lefts)

    def column(i, ids):
        return jnp.where(i == 0, 1 - ids[order], ids[order])

    specs = [pl.BlockSpec((size, tile), lambda i, ids, at=at: (at(ids), column(i, ids))) for _, size, at in lefts]
    specs += [pl.BlockSpec((size, cols), lambda i, ids, at=at: (at(ids), 0)) for _, size, at in rights]
    dims = (4, part, cols) if len(groups) == 1 else (4, len(groups), part, cols)
    out = pl.BlockSpec(dims, lambda i, ids: (0,) * len(dims))
    kernel = functools.partial(weight_kernel, order, [[size for (_, size, _), _ in g] for g in groups])
    total = len(lefts)
    return list(pl.pallas_call(
        lambda ids, *refs: kernel(ids, *refs[: 2 * total], *refs[2 * total + len(after) :]),
        grid_spec=pltpu.PrefetchScalarGridSpec(
            num_scalar_prefetch=1,
            grid=(2,),
            in_specs=specs + [ANY] * len(after),
            out_specs=[out, out],
            scratch_shapes=[pltpu.VMEM((len(groups), tile, cols), F32)],
        ),
        out_shape=[shape(dims, BF16), shape(dims, BF16)],
        compiler_params=params(),
        cost_estimate=cost(2.5),
        name=name,
    )(ids, *[a for a, _, _ in lefts], *[b for b, _, _ in rights], *after))


def head_grad(ids, order, first, second, after, name):
    rows_out, cols = first[0][0].shape[1], first[0][1].shape[1]
    part = rows_out // 8
    pieces = [len(first), len(second)]
    flat = [x for pair in (*first, *second) for x in pair]

    def kernel(ids_ref, *refs):
        values = refs[: len(flat)]
        send, keep, scratch = refs[len(flat) + len(after) :]
        at = 0
        for n in range(2):
            total = jnp.zeros((rows_out, cols), F32)
            for _ in range(pieces[n]):
                total = total + mm(values[at][...], values[at + 1][...], 0, 0)
                at += 2
            scratch[n] = total
        for half, out in ((1 - ids_ref[order], send), (ids_ref[order], keep)):
            for r in range(4):
                start = pl.multiple_of((half * 4 + (ids_ref[order + 1] ^ r)) * part, 8)
                for n in range(2):
                    out[r, n] = scratch[n, pl.ds(start, part), :].astype(BF16)

    dims = (4, 2, part, cols)
    return pl.pallas_call(
        kernel,
        grid_spec=pltpu.PrefetchScalarGridSpec(
            num_scalar_prefetch=1,
            grid=(1,),
            in_specs=[VM] * len(flat) + [ANY] * len(after),
            out_specs=[VM, VM],
            scratch_shapes=[pltpu.VMEM((2, rows_out, cols), F32)],
        ),
        out_shape=[shape(dims, BF16), shape(dims, BF16)],
        compiler_params=params(),
        cost_estimate=cost(0.2),
        name=name,
    )(ids, *flat, *after)


class Dual:
    def __init__(self, bits, direct, name):
        self.bits, self.direct, self.name, self.level = bits, direct, name, 0
        self.halves, self.got = [None, None], [None, None]

    def begin(self, which, halves):
        self.halves[which] = list(halves)
        if self.direct:
            self.got[which] = dp_swap(halves[0], self.bits[which][0], f"{self.name}_start_{which}")

    def step(self, after):
        if not self.direct:
            return after
        (_, keep_a), (_, keep_b) = self.halves
        level, name = self.level, f"{self.name}_{self.level}"
        self.level += 1
        first, second = self.bits
        if level < 2:
            parts, rest = keep_a.shape[0], keep_a.shape[1:]
            half = parts // 2
            if level == 0:

                def kernel(ka, ga, kb, gb, sa, oa, sb, ob):
                    for k, g, send, out in ((ka, ga, sa, oa), (kb, gb, sb, ob)):
                        send[...] = add_low(k[half:], g[half:])
                        out[...] = add_low(k[:half], g[:half])

                out = [shape((half, *rest), BF16)] * 4
                sa, oa, sb, ob = small_call(kernel, out, [keep_a, self.got[0], keep_b, self.got[1]], [after], name)
                self.halves = [[sa, oa], [sb, ob]]
                self.got = [dp_swap(sa, first[1], name + "_a"), dp_swap(sb, second[1], name + "_b")]
                return oa

            def kernel(ka, ga, kb, gb, out):
                for n, (k, g) in enumerate(((ka, ga), (kb, gb))):
                    out[n] = add_low(k[...], g[...])

            out = [shape((2, parts, *rest), BF16)]
            both = small_call(kernel, out, [keep_a, self.got[0], keep_b, self.got[1]], [after], name)[0]
            self.halves = [[None, both], [None, both]]
            self.got = [dp_swap(both, first[2], name + "_far"), None]
            return both
        if level == 2:

            def kernel(k, g, oa, ob):
                for n, out in enumerate((oa, ob)):
                    for j in range(2):
                        out[j] = add_low(k[n, j], g[n, 1 - j])

            out = [shape(keep_a.shape[1:], BF16)] * 2
            oa, ob = small_call(kernel, out, [keep_a, self.got[0]], [after], name)
            self.halves = [[None, oa], [None, ob]]
            self.got = [dp_swap(oa, first[1], name + "_a"), dp_swap(ob, second[1], name + "_b")]
            return oa
        rest = keep_a.shape[1:]

        def kernel(ka, ga, kb, gb, oa, ob):
            for k, g, out in ((ka, ga, oa), (kb, gb, ob)):
                out[:2] = k[...]
                out[2:] = g[...]

        out = [shape((4, *rest), BF16)] * 2
        oa, ob = small_call(kernel, out, [keep_a, self.got[0], keep_b, self.got[1]], [after], name)
        self.halves = [[None, oa], [None, ob]]
        self.got = [dp_swap(oa, first[0], name + "_a"), dp_swap(ob, second[0], name + "_b")]
        return oa

    def collect(self, which):
        if not self.direct:
            send, keep = lax.psum(tuple(self.halves[which]), "dp")
            return keep, send
        return self.halves[which][1], self.got[which]


def place_half(ids, order, value, flip, base, after, name):
    _, part, cols = value.shape
    rows = 8 * part
    given = [] if base is None else [pltpu.with_memory_space_constraint(base, pltpu.HBM)]

    def kernel(ids_ref, value_ref, *refs):
        out = refs[-1]
        for r in range(4):
            start = pl.multiple_of((ids_ref[order + 1] ^ r) * part, 8)
            out[pl.ds(start, part), :] = value_ref[r].astype(F32)

    return pl.pallas_call(
        kernel,
        grid_spec=pltpu.PrefetchScalarGridSpec(
            num_scalar_prefetch=1,
            grid=(1,),
            in_specs=[VM] + [ANY] * (len(given) + len(after)),
            out_specs=pl.BlockSpec((4 * part, cols), lambda i, ids: (ids[order] ^ flip, 0)),
        ),
        out_shape=pltpu.HBM((rows, cols), F32),
        input_output_aliases={2: 0} if given else {},
        compiler_params=params(),
        cost_estimate=cost(1.6),
        name=name,
    )(ids, value, *given, *after)


def place_heads(ids, orders, a, b, after):
    _, _, part, cols = a[0].shape
    rows = 8 * part

    def kernel(ids_ref, near_a, far_a, near_b, far_b, *refs):
        qkv_out, proj_out = refs[len(after) :]
        for half in range(2):
            for n, (pick, order) in enumerate((((near_a, far_a), orders[0]), ((near_b, far_b), orders[1]))):
                for r in range(4):
                    at = (ids_ref[order] ^ half) * 4 + (ids_ref[order + 1] ^ r)
                    at = pl.ds(pl.multiple_of(at * part, 8), part)
                    if n == 0:
                        qkv_out[0, at, :] = pick[half][r, 0].astype(F32)
                        qkv_out[1, at, :] = pick[half][r, 1].astype(F32)
                    else:
                        qkv_out[2, at, :] = pick[half][r, 0].astype(F32)
                        proj_out[at, :] = pick[half][r, 1].astype(F32)

    return pl.pallas_call(
        kernel,
        grid_spec=pltpu.PrefetchScalarGridSpec(
            num_scalar_prefetch=1,
            grid=(1,),
            in_specs=[VM] * 4 + [ANY] * len(after),
            out_specs=[
                pl.BlockSpec((3, rows, cols), lambda *_: (0, 0, 0)),
                pl.BlockSpec((rows, cols), lambda *_: (0, 0)),
            ],
        ),
        out_shape=[pltpu.HBM((3, rows, cols), F32), pltpu.HBM((rows, cols), F32)],
        compiler_params=params(),
        cost_estimate=cost(2.1),
        name="place_heads",
    )(ids, *a, *b, *after)


def mid_back_kernel(pair, other, residual, cot, gain, grad_out, low_out, sums):
    i = pl.program_id(0)
    err = pair[...].astype(F32) + other[...].astype(F32)
    unit, scale = norm_stats(residual[...])
    top = cot[...].astype(F32)
    f = err * row_vector(gain)
    f_mean = jnp.mean(f, axis=-1, keepdims=True)
    fx_mean = jnp.mean(f * unit, axis=-1, keepdims=True)
    grad = top + scale * (f - f_mean - unit * fx_mean)
    grad_out[...] = grad
    low_out[...] = grad.astype(BF16)

    @pl.when(i == 0)
    def _():
        sums[...] = jnp.zeros_like(sums)

    sums[0:1] += jnp.sum(err * unit, axis=0, keepdims=True)
    sums[1:2] += jnp.sum(err, axis=0, keepdims=True)
    sums[2:3] += jnp.sum(top, axis=0, keepdims=True)


def mid_back(chunk, chunks, ids, pair, other, residual, cot, gain, after):
    rows, width = residual.shape
    half = rows // PAIR
    row = pl.BlockSpec((PAIR, width), lambda i, ids: (i, 0))
    return pl.pallas_call(
        lambda ids, *refs: mid_back_kernel(*refs[:5], *refs[5 + len(after) :]),
        grid_spec=pltpu.PrefetchScalarGridSpec(
            num_scalar_prefetch=1,
            grid=(half,),
            in_specs=[
                row, row, row,
                pl.BlockSpec((PAIR, width), lambda i, ids: (block_of(i + half, ids, chunk, half, chunks), 0)),
                whole(gain),
            ]
            + [ANY] * len(after),
            out_specs=[row, row, pl.BlockSpec((8, width), lambda i, ids: (0, 0))],
        ),
        out_shape=[shape((rows, width), F32), shape((rows, width), BF16), shape((8, width), F32)],
        compiler_params=params(),
        cost_estimate=cost(1.2),
        name="mid_back",
    )(ids, pair, other, residual, cot, gain, *after)


def attend_back_kernel(half, peer, own, q_ref, k_ref, v_ref, p_ref, w_qkv, wo, send, keep, dq_out, dk_out, dv_out):
    i = pl.program_id(0)
    low = jnp.where(i < half, peer[...], own[...])
    grad_context = mm(low, wo[...], 1, 1).astype(BF16)
    q, k, v = q_ref[...], k_ref[...], v_ref[...]
    width = q.shape[1]
    head = lax.broadcasted_iota(jnp.int32, (1, width), 1) // HEAD_DIM
    zero = jnp.zeros_like(q)
    dq = dk = dv = jnp.zeros((PAIR, width), F32)
    for h in range(width // HEAD_DIM):
        mine = head == h
        gh = jnp.where(mine, grad_context, zero)
        weights = p_ref[0, h]
        grad_p = mm(gh, v, 1, 1)
        wide = weights.astype(F32)
        dot = jnp.sum(wide * grad_p, axis=-1, keepdims=True)
        grad_s = (wide * (grad_p - dot)).astype(BF16)
        dv = dv + mm(weights, gh, 0, 0)
        dq = dq + mm(grad_s, jnp.where(mine, k, zero), 1, 0)
        dk = dk + mm(grad_s, jnp.where(mine, q, zero), 0, 0)
    scale = HEAD_DIM**-0.5
    dq = (dq * scale).astype(BF16)
    dk = (dk * scale).astype(BF16)
    dv = dv.astype(BF16)
    dq_out[...] = dq
    dk_out[...] = dk
    dv_out[...] = dv
    part = (mm(dq, w_qkv[0], 1, 0) + mm(dk, w_qkv[1], 1, 0) + mm(dv, w_qkv[2], 1, 0)).astype(BF16)

    @pl.when(i < half)
    def _():
        send[...] = part

    @pl.when(i >= half)
    def _():
        keep[...] = part


def attend_back(peer, own, q, k, v, p, w_qkv, wo, after):
    rows, local = q.shape
    width = wo.shape[1]
    blocks = rows // PAIR
    half = blocks // 2
    heads = local // HEAD_DIM
    first = pl.BlockSpec((PAIR, width), lambda i: (jnp.minimum(i, half - 1), 0))
    second = pl.BlockSpec((PAIR, width), lambda i: (jnp.maximum(i - half, 0), 0))
    thin = pl.BlockSpec((PAIR, local), lambda i: (i, 0))
    return pl.pallas_call(
        lambda *refs: attend_back_kernel(half, *refs[:8], *refs[8 + len(after) :]),
        grid=(blocks,),
        in_specs=[
            first, second, thin, thin, thin,
            pl.BlockSpec((1, heads, PAIR, PAIR), lambda i: (i, 0, 0, 0)),
            whole(w_qkv), whole(wo),
        ]
        + [ANY] * len(after),
        out_specs=[first, second, thin, thin, thin],
        out_shape=[
            shape((rows // 2, width), BF16), shape((rows // 2, width), BF16),
            shape((rows, local), BF16), shape((rows, local), BF16), shape((rows, local), BF16),
        ],
        compiler_params=params(),
        cost_estimate=cost(3.5),
        name="attend_back",
    )(peer, own, q, k, v, p, w_qkv, wo, *after)


def last_kernel(pair, other, hidden, grad_residual, gain, low_out, sums, times):
    i = pl.program_id(0)
    err = pair[...].astype(F32) + other[...].astype(F32)
    unit, scale = norm_stats(hidden[...])
    f = err * row_vector(gain)
    f_mean = jnp.mean(f, axis=-1, keepdims=True)
    fx_mean = jnp.mean(f * unit, axis=-1, keepdims=True)
    grad = grad_residual[...] + scale * (f - f_mean - unit * fx_mean)
    low_out[...] = grad.astype(BF16)

    @pl.when(i == 0)
    def _():
        sums[...] = jnp.zeros_like(sums)

    sums[0:1] += jnp.sum(err * unit, axis=0, keepdims=True)
    sums[1:2] += jnp.sum(err, axis=0, keepdims=True)
    times[0, 0:1] = jnp.sum(grad[:SHORT], axis=0, keepdims=True)
    times[0, 1:2] = jnp.sum(grad[SHORT:], axis=0, keepdims=True)


def last_back(pair, other, hidden, grad_residual, gain, after):
    rows, width = hidden.shape
    half = rows // PAIR
    row = pl.BlockSpec((PAIR, width), lambda i: (i, 0))
    return pl.pallas_call(
        lambda *refs: last_kernel(*refs[:5], *refs[5 + len(after) :]),
        grid=(half,),
        in_specs=[row, row, row, row, whole(gain)] + [ANY] * len(after),
        out_specs=[
            row,
            pl.BlockSpec((8, width), lambda i: (0, 0)),
            pl.BlockSpec((1, 2, width), lambda i: (i, 0, 0)),
        ],
        out_shape=[shape((rows, width), BF16), shape((8, width), F32), shape((half, 2, width), F32)],
        compiler_params=params(),
        cost_estimate=cost(0.7),
        name="last_back",
    )(pair, other, hidden, grad_residual, gain, *after)


def pack_sums(vec2, vec1, up, times, after):
    pairs, _, width = times.shape

    def kernel(v2, v1, u, t, out):
        out[0:3] = v2[0:3]
        out[3:5] = v1[0:2]
        out[5:6] = u[...]
        out[6:8] = jnp.zeros((2, width), F32)
        for n in range(pairs):
            out[8 + 2 * n : 10 + 2 * n] = t[n]

    return small_call(kernel, [shape((8 + 2 * pairs, width), F32)], [vec2, vec1, up, times], after, "pack_sums")[0]


def join_sums(a, b, after, name):
    rows, width = a.shape
    more = rows - 8

    def kernel(a_ref, b_ref, out):
        out[0:8] = a_ref[0:8] + b_ref[0:8]
        out[8 : 8 + more] = a_ref[8:]
        out[8 + more :] = b_ref[8:]

    return small_call(kernel, [shape((8 + 2 * more, width), F32)], [a, b], after, name)[0]


def table_kernel(slots, steps, ids, own, other, vec_out, out, table, acc, at_ref):
    groups = at_ref.shape[0]
    rows, (row_length, row_group, row_step) = row_fields(ids)
    local = table.shape[2]
    half = slots // 2
    vec_out[...] = own[0:8] + other[0:8]
    vec_out[5:6] = own[5:6]
    for p in range(own.shape[1] // local):

        @pl.when(ids[2] == p)
        def _():
            table[0] = own[8:, p * local : (p + 1) * local]
            table[1] = other[8:, p * local : (p + 1) * local]

    acc[...] = jnp.zeros_like(acc)

    def clear(g, _):
        at_ref[g] = 0
        return 0

    lax.fori_loop(0, groups, clear, 0)

    def place(long):
        def one(r, _):
            @pl.when((row_length(r) > SHORT) == long)
            def _():
                g = row_group(r)
                at = at_ref[g]
                at_ref[g] = at + (2 if long else 1)
                which = (at // half) ^ ids[0]
                base = (g ^ ids[1]) * half + lax.rem(at, half)
                value = table[which, pl.ds(base, 1), :]
                if long:
                    value = value + table[which, pl.ds(base + 1, 1), :]
                step = pl.ds(row_step(r), 1)
                acc[step, :] = acc[step, :] + value

            return 0

        lax.fori_loop(0, rows, one, 0)

    place(True)
    place(False)
    out[...] = jnp.transpose(acc[...])[:, :steps]


def table_grad(scalars, own, other, steps, local, slots, after):
    rows, width = own.shape
    groups = (rows - 8) * 2 // slots
    return pl.pallas_call(
        lambda *refs: table_kernel(slots, steps, *refs[:3], *refs[3 + len(after) :]),
        grid_spec=pltpu.PrefetchScalarGridSpec(
            num_scalar_prefetch=1,
            grid=(1,),
            in_specs=[VM, VM] + [ANY] * len(after),
            out_specs=[pl.BlockSpec((8, width), lambda *_: (0, 0)), pl.BlockSpec((local, steps), lambda *_: (0, 0))],
            scratch_shapes=[
                pltpu.VMEM((2, rows - 8, local), F32),
                pltpu.VMEM((pl.cdiv(steps, 128) * 128, local), F32),
                pltpu.SMEM((groups,), jnp.int32),
            ],
        ),
        out_shape=[shape((8, width), F32), pltpu.HBM((local, steps), F32)],
        compiler_params=params(),
        cost_estimate=cost(3.9),
        name="table_grad",
    )(scalars, own, other, *after)


def finish(residuals, pair, other, bias, after):
    rows, width = pair.shape
    part = rows // len(residuals)

    def kernel(*refs):
        res = refs[: len(residuals)]
        pair_ref, other_ref, bias_ref = refs[len(residuals) : len(residuals) + 3]
        out = refs[-1]
        for n, r in enumerate(res):
            at = slice(n * part, (n + 1) * part)
            total = r[...] + (pair_ref[at].astype(F32) + other_ref[at].astype(F32))
            out[at] = (total + row_vector(bias_ref)).astype(BF16)

    return small_call(kernel, [shape((rows, width), BF16)], [*residuals, pair, other, bias], after, "finish")[0]


def order_rows(ids, own, other, after, name):
    count = len(own)
    part, width = own[0].shape

    def kernel(ids_ref, *refs):
        out = refs[-1]
        i = pl.program_id(0)
        for n in range(2 * count):

            @pl.when(i == n)
            def _():
                out[...] = refs[n][...]

    return pl.pallas_call(
        kernel,
        grid_spec=pltpu.PrefetchScalarGridSpec(
            num_scalar_prefetch=1,
            grid=(2 * count,),
            in_specs=[VM] * (2 * count) + [ANY] * len(after),
            out_specs=pl.BlockSpec(
                (part, width), lambda i, ids: ((ids[0] ^ (i // count)) * count + lax.rem(i, count), 0)
            ),
        ),
        out_shape=pltpu.HBM((2 * count * part, width), BF16),
        compiler_params=params(),
        cost_estimate=cost(2.0),
        name=name,
    )(ids, *own, *other, *after)


def shards(
    tokens, row_length, row_group, row_step, time_table, norm1_gain, norm1_bias, w_qkv, w_out,
    norm2_gain, norm2_bias, w_up, up_bias, w_down, down_bias, cotangent,
):
    count, width = tokens.shape
    n_dp = lax.axis_size("dp")
    dp = lax.axis_index("dp")
    part = lax.axis_index("tensor")
    core = lax.rem(part, 2)
    direct = n_dp == 8
    low_bit, mid_bit, top_bit = dp & 1, (dp >> 1) & 1, (dp >> 2) & 1
    if direct:
        orders = [low_bit, 2 * mid_bit + top_bit, mid_bit, 2 * low_bit + top_bit]
    else:
        orders = [1, 0, 1, 0]
    ids = jnp.stack([core, dp, part, *[jnp.int32(o) for o in orders], jnp.int32(0)]).astype(jnp.int32)
    scalars = jnp.concatenate([ids, row_length, row_group, row_step])
    order_a, order_b = 3, 5
    bits = ((1, 2, 4), (2, 1, 4))
    local = w_out.shape[0]
    slots = count // SHORT
    heads = jnp.transpose(w_qkv, (1, 2, 0))
    far = lambda x: pltpu.with_memory_space_constraint(x, pltpu.HBM)
    size = count // 2
    peer_rows = lambda ids: 1 - ids[0]
    own_rows = lambda ids: ids[0]
    zero = lambda ids: 0
    one = lambda ids: 1

    send, keep, hidden, normed, q, k, v, p, ctx = attend(
        0, 1, scalars, *[far(x) for x in (tokens, time_table, norm1_gain, norm1_bias, heads, w_out)], []
    )
    pair = add_two(keep, core_swap(send, "core_one"), [], "pair_one")
    residual, own2 = mid_forward(hidden, pair, chip_swap(pair, "chip_one"), norm2_gain, norm2_bias, [])
    peer2 = core_swap(own2, "core_norm")
    send, keep, act, low, up_sum = expand(0, 1, ids, peer2, own2, far(cotangent), far(w_up), up_bias, far(w_down), [])
    got = core_swap(send, "core_two")
    cots = [(cotangent, size, f) for f in (peer_rows, own_rows)]
    acts = [(act, size, f) for f in (zero, one)]
    lows = [(low, size, f) for f in (zero, one)]
    norms = [(peer2, size, zero), (own2, size, zero)]
    down = weight_grad(ids, order_a, [list(zip(acts, cots))], [keep], "down_grad")
    mlp = Dual(bits, direct, "mlp")
    mlp.begin(0, down)
    pair = add_two(keep, got, [down[1]], "pair_two")
    other = chip_swap(pair, "chip_two")
    up = weight_grad(ids, order_b, [list(zip(norms, lows))], [pair], "up_grad")
    mlp.begin(1, up)
    send_e, keep_e = contract_rows(act, w_down, [up[1]])
    got_e = core_swap(send_e, "core_out", 4)
    mark = mlp.step(keep_e)
    grad_residual, low_own, vec2 = mid_back(0, 1, ids, pair, other, residual, cotangent, norm2_gain, [mark])
    low_peer = core_swap(low_own, "core_low", 4)
    send, keep, dq, dk, dv = attend_back(low_peer, low_own, q, k, v, p, heads, w_out, [])
    got = core_swap(send, "core_three", 4)
    heads_sum = Dual(bits, direct, "heads")
    mark = mlp.step(keep)
    qk = head_grad(ids, order_a, [(dq, normed)], [(dk, normed)], [mark], "qk_grad")
    heads_sum.begin(0, qk)
    pair = add_two(keep, got, [qk[1]], "pair_three")
    other = chip_swap(pair, "chip_three", 2)
    mark = pair
    lows1 = jnp.concatenate([low_peer, low_own], axis=0)
    vo = head_grad(ids, order_b, [(dv, normed)], [(ctx, lows1)], [mark], "vo_grad")
    heads_sum.begin(1, vo)
    mark = heads_sum.step(vo[1])
    low_in, vec1, times = last_back(pair, other, hidden, grad_residual, norm1_gain, [mark])
    low_got = core_swap(low_in, "core_input", 4)
    sums = pack_sums(vec2, vec1, up_sum, times, [low_in])
    sums_got = dp_swap(sums, 1, "sums_0")
    mark = heads_sum.step(sums)
    pair_e = add_two(keep_e, got_e, [mark], "pair_out")
    other_e = chip_swap(pair_e, "chip_out", 2)
    mark = mlp.step(pair_e)
    sums = join_sums(sums, sums_got, [mark], "join_sums_0")
    sums_got = dp_swap(sums, 2, "sums_1")
    input_grad = order_rows(ids, [low_in], [low_got], [sums], "order_input")
    sums = join_sums(sums, sums_got, [far(input_grad)], "join_sums_1")
    sums_got = dp_swap(sums, 4, "sums_2")
    mark = heads_sum.step(sums)
    mark = mlp.step(mark)
    near_down, far_down = mlp.collect(0)
    near_up, far_up = mlp.collect(1)
    down_out = place_half(ids, order_a, near_down, 0, None, [mark], "place_down_0")
    up_out = place_half(ids, order_b, near_up, 0, None, [far(down_out)], "place_up_0")
    sums = join_sums(sums, sums_got, [far(up_out)], "join_sums_2")
    bit = 8
    while bit < n_dp:
        sums = join_sums(sums, dp_swap(sums, bit), [], f"join_sums_{bit}")
        bit *= 2
    sums_peer = core_swap(sums, "core_sums")
    mark = heads_sum.step(sums)
    final = finish([residual], pair_e, other_e, down_bias, [mark])
    final_got = core_swap(final, "core_final", 4)
    vec, time_grad = table_grad(scalars, sums, sums_peer, time_table.shape[0], local, slots, [final])
    down_out = place_half(ids, order_a, far_down, 1, down_out, [vec], "place_down_1")
    up_out = place_half(ids, order_b, far_up, 1, up_out, [far(down_out)], "place_up_1")
    qkv_out, proj_out = place_heads(ids, (order_a, order_b), heads_sum.collect(0), heads_sum.collect(1), [far(up_out)])
    block_output = order_rows(ids, [final], [final_got], [far(proj_out)], "order_output")

    return (
        block_output,
        input_grad,
        time_grad.T,
        vec[3],
        vec[4],
        jnp.transpose(qkv_out, (2, 0, 1)),
        proj_out,
        vec[0],
        vec[1],
        up_out,
        vec[5],
        down_out,
        vec[2],
    )


def solution(mesh):
    in_specs = (
        P("dp", None), P(), P(), P(), P(), P(), P(), P(None, None, "tensor"), P("tensor", None), P(), P(),
        P(None, "tensor"), P("tensor"), P("tensor", None), P(), P("dp", None),
    )
    out_specs = (
        P("dp", None), P("dp", None), P(None, "tensor"), P(), P(), P(None, None, "tensor"), P("tensor", None),
        P(), P(), P(None, "tensor"), P("tensor"), P("tensor", None), P(),
    )
    return jax.shard_map(shards, mesh=mesh, in_specs=in_specs, out_specs=out_specs, check_vma=False)
```

```python
import functools
import types

import jax
import jax.numpy as jnp
from jax import lax
from jax.experimental import pallas as pl
from jax.experimental.pallas import tpu as pltpu
from jax.sharding import PartitionSpec as P

HEAD_DIM = 64
SHORT = 128
PAIR = 256
EPS = 1e-05
NEG = -1000000000.0
SQRT_HALF = 0.7071067811865476
PHI_ZERO = 0.3989422804014327
VMEM_MB = 16
LOW_PIECES = 2
PART_PIECES = 4

SMALL_MB = 8

F32 = jnp.float32
BF16 = jnp.bfloat16


def mm(left, right, left_dim, right_dim):
    return lax.dot_general(
        left, right, (((left_dim,), (right_dim,)), ((), ())), preferred_element_type=F32
    )


def params(dims=1):
    return pltpu.CompilerParams(
        dimension_semantics=("arbitrary",) * dims, vmem_limit_bytes=VMEM_MB << 20
    )


COSTS = {"expand": 1, "finish": 0.5, "order_input": 0.5}


def cost(name):
    return pl.CostEstimate(flops=int(COSTS.get(name, 0) * 1e9), bytes_accessed=1, transcendentals=0)


def shape(dims, dtype):
    return jax.ShapeDtypeStruct(dims, dtype)


def whole(array):
    zeros = (0,) * array.ndim
    return pl.BlockSpec(array.shape, lambda *_: zeros)


def swap(value, axis, bit):
    return lax.ppermute(value, axis, [(i, i ^ bit) for i in range(lax.axis_size(axis))])


def core_swap(value):
    return swap(value, "tensor", 1)


def chip_swap(value):
    return swap(value, "tensor", 2)


def dp_swap(value, bit):
    return swap(value, "dp", bit)


def norm_stats(values):
    mean = jnp.mean(values, axis=-1, keepdims=True)
    centred = values - mean
    variance = jnp.mean(centred * centred, axis=-1, keepdims=True)
    scale = lax.rsqrt(variance + EPS)
    return centred * scale, scale


IDS = 8


def row_fields(info):
    rows = (info.shape[0] - IDS) // 3
    return rows, [lambda r, at=at: info[IDS + at * rows + r] for at in range(3)]


def fill_slots(slot_ref, info):
    group = info[1]
    rows, (row_length, row_group, row_step) = row_fields(info)

    def long_row(r, pos):
        step = row_step(r)
        slot_ref[pos] = step
        slot_ref[pos + 1] = step
        hit = (row_group(r) == group) & (row_length(r) > SHORT)
        return pos + jnp.where(hit, 2, 0)

    def short_row(r, pos):
        slot_ref[pos] = row_step(r)
        hit = (row_group(r) == group) & (row_length(r) <= SHORT)
        return pos + jnp.where(hit, 1, 0)

    long_slots = lax.fori_loop(0, rows, long_row, 0)
    lax.fori_loop(0, rows, short_row, long_slots)
    return long_slots


def block_of(i, ids, chunk, half, chunks):
    side = jnp.where(i < half, 1 - ids[0], ids[0])
    return side * (half * chunks) + chunk * half + lax.rem(i, half)


def add_low(a, b):
    return (a.astype(F32) + b.astype(F32)).astype(BF16)


def row_vector(ref):
    return ref[...].reshape(1, ref.shape[0])


VM = pl.BlockSpec(memory_space=pltpu.VMEM)
ANY = pl.BlockSpec(memory_space=pl.ANY)


def small_call(kernel, out_shape, operands, after, name):
    count = len(operands)
    return pl.pallas_call(
        lambda *refs: kernel(*refs[:count], *refs[count + len(after) :]),
        in_specs=[VM] * count + [ANY] * len(after),
        out_specs=[VM] * len(out_shape),
        out_shape=out_shape,
        compiler_params=pltpu.CompilerParams(vmem_limit_bytes=SMALL_MB << 20),
        cost_estimate=cost(name),
        name=name,
    )(*operands, *after)


def stage(arrays, after):
    count = len(arrays)

    def kernel(*refs):
        out, sems = refs[count + len(after) : -1], refs[-1]
        copies = [pltpu.make_async_copy(refs[n], out[n], sems.at[n]) for n in range(count)]
        for copy in copies:
            copy.start()
        for copy in copies:
            copy.wait()

    return pl.pallas_call(
        kernel,
        in_specs=[pl.BlockSpec(memory_space=pltpu.HBM)] * count + [ANY] * len(after),
        out_specs=[VM] * count,
        out_shape=[pltpu.VMEM(a.shape, a.dtype) for a in arrays],
        scratch_shapes=[pltpu.SemaphoreType.DMA((count,))],
        compiler_params=pltpu.CompilerParams(vmem_limit_bytes=SMALL_MB << 20),
        cost_estimate=cost("stage"),
        name="stage",
    )(*arrays, *after)


def add_two(a, b, after, name):
    def kernel(a_ref, b_ref, out):
        out[...] = add_low(a_ref[...], b_ref[...])

    return small_call(kernel, [shape(a.shape, BF16)], [a, b], after, name)[0]


def attend_kernel(
    chunk, half, chunks, slots, ids,
    tokens, table, gain, bias, w_qkv, wo,
    send, keep, hidden_out, normed_out, q_out, k_out, v_out, p_out, c_out,
    slot_ref, rows_ref, sems,
):
    i = pl.program_id(0)

    def fetch(s):
        step = slot_ref[s]
        start = pl.multiple_of((step // 8) * 8, 8)
        return pltpu.make_async_copy(table.at[pl.ds(start, 8), :], rows_ref.at[s], sems.at[s])

    @pl.when(i == 0)
    def _():
        slot_ref[slots + 2] = fill_slots(slot_ref, ids)
        for s in range(slots):
            fetch(s).start()
        for s in range(slots):
            fetch(s).wait()

    block = block_of(i, ids, chunk, half, chunks)
    sub = lax.broadcasted_iota(jnp.int32, (8, 1), 0)

    def row_of(s):
        picked = sub == lax.rem(slot_ref[s], 8)
        return jnp.sum(jnp.where(picked, rows_ref[s].astype(F32), 0.0), axis=0, keepdims=True)

    low_half = lax.broadcasted_iota(jnp.int32, (PAIR, 1), 0) < SHORT
    step_row = jnp.where(low_half, row_of(2 * block), row_of(2 * block + 1))
    hidden = tokens[...].astype(F32) + step_row
    unit, _ = norm_stats(hidden)
    normed = (unit * row_vector(gain) + row_vector(bias)).astype(BF16)
    normed_out[...] = normed
    q = mm(normed, w_qkv[0], 1, 1).astype(BF16)
    k = mm(normed, w_qkv[1], 1, 1).astype(BF16)
    v = mm(normed, w_qkv[2], 1, 1).astype(BF16)
    q_out[...] = q
    k_out[...] = k
    v_out[...] = v
    split = (2 * block >= slot_ref[slots + 2]).astype(jnp.int32)
    row_half = lax.broadcasted_iota(jnp.int32, (PAIR, PAIR), 0) // SHORT
    col_half = lax.broadcasted_iota(jnp.int32, (PAIR, PAIR), 1) // SHORT
    allowed = ((row_half ^ col_half) * split) == 0
    width = q.shape[1]
    head = lax.broadcasted_iota(jnp.int32, (1, width), 1) // HEAD_DIM
    context = jnp.zeros((PAIR, width), F32)
    for h in range(width // HEAD_DIM):
        mine = head == h
        qh = jnp.where(mine, q, jnp.zeros_like(q))
        scores = mm(qh, k, 1, 1) * (HEAD_DIM**-0.5)
        scores = jnp.where(allowed, scores, NEG)
        top = jnp.max(scores, axis=-1, keepdims=True)
        powers = jnp.exp(scores - top)
        total = jnp.sum(powers, axis=-1, keepdims=True)
        weights = (powers * (1.0 / total)).astype(BF16)
        p_out[0, h] = weights
        context = context + mm(weights, jnp.where(mine, v, jnp.zeros_like(v)), 1, 0)
    low = context.astype(BF16)
    c_out[...] = low
    part = mm(low, wo[...], 1, 0).astype(BF16)

    @pl.when(i < half)
    def _():
        send[...] = part

    @pl.when(i >= half)
    def _():
        keep[...] = part
        hidden_out[...] = hidden


def attend(chunk, chunks, scalars, tokens, table, gain, bias, w_qkv, wo, after):
    count, width = tokens.shape
    local = wo.shape[0]
    blocks = count // PAIR // chunks
    half = blocks // 2
    rows = blocks * PAIR
    slots = count // SHORT
    own = rows // 2
    heads = local // HEAD_DIM
    first = lambda i, *_: (jnp.minimum(i, half - 1), 0)
    second = lambda i, *_: (jnp.maximum(i - half, 0), 0)
    step = lambda i, *_: (i, 0)
    row = pl.BlockSpec((PAIR, width), step)
    thin = pl.BlockSpec((PAIR, local), step)
    return pl.pallas_call(
        lambda *refs: attend_kernel(chunk, half, chunks, slots, *refs[:7], *refs[7 + len(after) :]),
        grid_spec=pltpu.PrefetchScalarGridSpec(
            num_scalar_prefetch=1,
            grid=(blocks,),
            in_specs=[
                pl.BlockSpec((PAIR, width), lambda i, ids, *_: (block_of(i, ids, chunk, half, chunks), 0)),
                pl.BlockSpec(memory_space=pltpu.HBM),
                whole(gain), whole(bias), whole(w_qkv), whole(wo),
            ]
            + [ANY] * len(after),
            out_specs=[
                pl.BlockSpec((PAIR, width), first),
                pl.BlockSpec((PAIR, width), second),
                pl.BlockSpec((PAIR, width), second),
                row, thin, thin, thin,
                pl.BlockSpec((1, heads, PAIR, PAIR), lambda i, *_: (i, 0, 0, 0)),
                thin,
            ],
            scratch_shapes=[
                pltpu.SMEM((slots + 4,), jnp.int32),
                pltpu.VMEM((slots, 8, width), BF16),
                pltpu.SemaphoreType.DMA((slots,)),
            ],
        ),
        out_shape=[
            shape((own, width), BF16), shape((own, width), BF16), shape((own, width), F32),
            shape((rows, width), BF16),
            shape((rows, local), BF16), shape((rows, local), BF16), shape((rows, local), BF16),
            shape((blocks, heads, PAIR, PAIR), BF16),
            shape((rows, local), BF16),
        ],
        compiler_params=params(),
        cost_estimate=cost("attend"),
        name="attend",
    )(scalars, tokens, table, gain, bias, w_qkv, wo, *after)


def mid_kernel(hidden, pair, other, gain, bias, residual_out, normed_out):
    residual = hidden[...] + (pair[...].astype(F32) + other[...].astype(F32))
    residual_out[...] = residual
    unit, _ = norm_stats(residual)
    normed_out[...] = (unit * row_vector(gain) + row_vector(bias)).astype(BF16)


def mid_forward(hidden, pair, other, gain, bias, after):
    rows, width = hidden.shape
    row = pl.BlockSpec((PAIR, width), lambda i: (i, 0))
    return pl.pallas_call(
        lambda *refs: mid_kernel(*refs[:5], *refs[5 + len(after) :]),
        grid=(rows // PAIR,),
        in_specs=[row, row, row, whole(gain), whole(bias)] + [ANY] * len(after),
        out_specs=[row, row],
        out_shape=[shape((rows, width), F32), shape((rows, width), BF16)],
        compiler_params=params(),
        cost_estimate=cost("mid_forward"),
        name="mid_forward",
    )(hidden, pair, other, gain, bias, *after)


def act_grad(cot, w_down):
    rows, width = cot.shape
    local = w_down.shape[0]

    def kernel(cot_ref, w_ref, out):
        out[...] = mm(cot_ref[...], w_ref[...], 1, 1)

    return pl.pallas_call(
        kernel,
        grid=(rows // PAIR,),
        in_specs=[pl.BlockSpec((PAIR, width), lambda i: (i, 0)), VM],
        out_specs=pl.BlockSpec((PAIR, local), lambda i: (i, 0)),
        out_shape=shape((rows, local), F32),
        compiler_params=params(),
        cost_estimate=cost("act_grad"),
        name="act_grad",
    )(cot, w_down)


def expand_kernel(half, ids, peer, own, grad_act, w_up, up_bias, send, keep, act_out, low_out, bias_out):
    i = pl.program_id(0)
    normed = jnp.where(i < half, peer[...], own[...])
    pre = mm(normed, w_up[...], 1, 0) + row_vector(up_bias)
    cdf = 0.5 * (1.0 + lax.erf(pre * SQRT_HALF))
    act_out[...] = (pre * cdf).astype(BF16)
    slope = cdf + pre * (PHI_ZERO * jnp.exp(-0.5 * (pre * pre)))
    grad_pre = grad_act[...] * slope

    @pl.when(i == 0)
    def _():
        bias_out[...] = jnp.zeros_like(bias_out)

    bias_out[...] += jnp.sum(grad_pre, axis=0, keepdims=True)
    low = grad_pre.astype(BF16)
    low_out[...] = low
    part = mm(low, w_up[...], 1, 1).astype(BF16)

    @pl.when(i < half)
    def _():
        send[...] = part

    @pl.when(i >= half)
    def _():
        keep[...] = part


def expand(chunk, chunks, ids, peer, own, grad_act, w_up, up_bias, after):
    count, width = grad_act.shape[0], peer.shape[1]
    local = w_up.shape[1]
    blocks = count // PAIR // chunks
    half = blocks // 2
    rows = blocks * PAIR
    first = lambda i, *_: (jnp.minimum(i, half - 1), 0)
    second = lambda i, *_: (jnp.maximum(i - half, 0), 0)
    step = lambda i, *_: (i, 0)
    return pl.pallas_call(
        lambda *refs: expand_kernel(half, *refs[:6], *refs[6 + len(after) :]),
        grid_spec=pltpu.PrefetchScalarGridSpec(
            num_scalar_prefetch=1,
            grid=(blocks,),
            in_specs=[
                pl.BlockSpec((PAIR, width), first),
                pl.BlockSpec((PAIR, width), second),
                pl.BlockSpec((PAIR, local), lambda i, ids: (block_of(i, ids, chunk, half, chunks), 0)),
                VM, whole(up_bias),
            ]
            + [ANY] * len(after),
            out_specs=[
                pl.BlockSpec((PAIR, width), first),
                pl.BlockSpec((PAIR, width), second),
                pl.BlockSpec((PAIR, local), step),
                pl.BlockSpec((PAIR, local), step),
                pl.BlockSpec((1, local), lambda i, *_: (0, 0)),
            ],
        ),
        out_shape=[
            shape((rows // 2, width), BF16), shape((rows // 2, width), BF16),
            shape((rows, local), BF16), shape((rows, local), BF16),
            shape((1, local), F32),
        ],
        compiler_params=params(),
        cost_estimate=cost("expand"),
        name="expand",
    )(ids, peer, own, grad_act, w_up, up_bias, *after)


def contract_kernel(act, w_down, send, keep):
    i = pl.program_id(0)
    part = mm(act[...], w_down[...], 1, 0).astype(BF16)

    @pl.when(i < 2)
    def _():
        send[...] = part

    @pl.when(i >= 2)
    def _():
        keep[...] = part


def contract_rows(act, w_down, after):
    rows, local = act.shape
    width = w_down.shape[1]
    return pl.pallas_call(
        lambda *refs: contract_kernel(*refs[:2], *refs[2 + len(after) :]),
        grid=(rows // PAIR,),
        in_specs=[pl.BlockSpec((PAIR, local), lambda i: (i, 0)), VM] + [ANY] * len(after),
        out_specs=[
            pl.BlockSpec((PAIR, width), lambda i: (jnp.minimum(i, 1), 0)),
            pl.BlockSpec((PAIR, width), lambda i: (jnp.maximum(i - 2, 0), 0)),
        ],
        out_shape=[shape((rows // 2, width), BF16), shape((rows // 2, width), BF16)],
        compiler_params=params(),
        cost_estimate=cost("contract_rows"),
        name="contract_rows",
    )(act, w_down, *after)


def weight_kernel(order, groups, ids, *refs):
    count = sum(len(lefts) for lefts in groups)
    left, right = refs[:count], refs[count : 2 * count]
    send, keep, scratch = refs[2 * count : 2 * count + 3]
    i = pl.program_id(0)
    many = len(groups) > 1
    rows = send.shape[-2]
    at = 0
    for n, sizes in enumerate(groups):
        total = mm(left[at][...], right[at][...], 0, 0)
        for j in range(at + 1, at + len(sizes)):
            total = total + mm(left[j][...], right[j][...], 0, 0)
        at += len(sizes)
        scratch[n] = total

    def write(out):
        for r in range(4):
            start = pl.multiple_of((ids[order + 1] ^ r) * rows, 8)
            for n in range(len(groups)):
                value = scratch[n, pl.ds(start, rows), :].astype(BF16)
                if many:
                    out[r, n] = value
                else:
                    out[r] = value

    @pl.when(i == 0)
    def _():
        write(send)

    @pl.when(i == 1)
    def _():
        write(keep)


def weight_grad(ids, order, groups, after, name):
    rows_out = groups[0][0][0][0].shape[1]
    tile = rows_out // 2
    part = tile // 4
    cols = groups[0][0][1][0].shape[1]
    lefts = [left for pieces in groups for left, _ in pieces]
    rights = [right for pieces in groups for _, right in pieces]
    count = sum(size for _, size, _ in lefts)

    def column(i, ids):
        return jnp.where(i == 0, 1 - ids[order], ids[order])

    specs = [pl.BlockSpec((size, tile), lambda i, ids, at=at: (at(ids), column(i, ids))) for _, size, at in lefts]
    specs += [pl.BlockSpec((size, cols), lambda i, ids, at=at: (at(ids), 0)) for _, size, at in rights]
    dims = (4, part, cols) if len(groups) == 1 else (4, len(groups), part, cols)
    out = pl.BlockSpec(dims, lambda i, ids: (0,) * len(dims))
    kernel = functools.partial(weight_kernel, order, [[size for (_, size, _), _ in g] for g in groups])
    total = len(lefts)
    return list(pl.pallas_call(
        lambda ids, *refs: kernel(ids, *refs[: 2 * total], *refs[2 * total + len(after) :]),
        grid_spec=pltpu.PrefetchScalarGridSpec(
            num_scalar_prefetch=1,
            grid=(2,),
            in_specs=specs + [ANY] * len(after),
            out_specs=[out, out],
            scratch_shapes=[pltpu.VMEM((len(groups), tile, cols), F32)],
        ),
        out_shape=[shape(dims, BF16), shape(dims, BF16)],
        compiler_params=params(),
        cost_estimate=cost(name),
        name=name,
    )(ids, *[a for a, _, _ in lefts], *[b for b, _, _ in rights], *after))


def head_grad(ids, order, first, second, after, name):
    rows_out, cols = first[0].shape[1], first[1][0].shape[1]
    part = rows_out // 8
    flat = [first[0], *first[1], second[0], *second[1]]

    def kernel(ids_ref, *refs):
        values = refs[: len(flat)]
        send, keep, scratch = refs[len(flat) + len(after) :]
        at = 0
        for n, (_, pieces) in enumerate((first, second)):
            rights = [values[at + 1 + j][...] for j in range(len(pieces))]
            right = rights[0] if len(rights) == 1 else jnp.concatenate(rights, axis=0)
            scratch[n] = mm(values[at][...], right, 0, 0)
            at += 1 + len(pieces)
        for half, out in ((1 - ids_ref[order], send), (ids_ref[order], keep)):
            for r in range(4):
                start = pl.multiple_of((half * 4 + (ids_ref[order + 1] ^ r)) * part, 8)
                for n in range(2):
                    out[r, n] = scratch[n, pl.ds(start, part), :].astype(BF16)

    dims = (4, 2, part, cols)
    return pl.pallas_call(
        kernel,
        grid_spec=pltpu.PrefetchScalarGridSpec(
            num_scalar_prefetch=1,
            grid=(1,),
            in_specs=[VM] * len(flat) + [ANY] * len(after),
            out_specs=[VM, VM],
            scratch_shapes=[pltpu.VMEM((2, rows_out, cols), F32)],
        ),
        out_shape=[shape(dims, BF16), shape(dims, BF16)],
        compiler_params=params(),
        cost_estimate=cost(name),
        name=name,
    )(ids, *flat, *after)


def add_pieces(a, b, pieces, after, name):
    rows, width = a.shape
    size, out_size = rows // len(b), rows // pieces
    step = min(size, out_size)

    def kernel(a_ref, *refs):
        given, out = refs[: len(b)], refs[len(b) :]
        for at in range(0, rows, step):
            got = given[at // size][at % size : at % size + step]
            out[at // out_size][at % out_size : at % out_size + step] = add_low(a_ref[at : at + step], got)

    return list(small_call(kernel, [shape((out_size, width), BF16)] * pieces, [a, *b], after, name))


class Dual:
    def __init__(self, bits, direct):
        self.bits, self.direct, self.level = bits, direct, 0
        self.summed = [None, None]
        self.halves, self.got = [None, None], [None, None]

    def begin(self, which, halves):
        self.halves[which] = list(halves)
        if self.direct:
            self.got[which] = dp_swap(halves[0], self.bits[which][0])

    def step(self, after):
        if not self.direct:
            return after
        (_, keep_a), (_, keep_b) = self.halves
        level, name = self.level, "exchange"
        self.level += 1
        first, second = self.bits
        if level < 2:
            parts, rest = keep_a.shape[0], keep_a.shape[1:]
            half = parts // 2
            if level == 0:

                def kernel(ka, ga, kb, gb, sa, oa, sb, ob):
                    for k, g, send, out in ((ka, ga, sa, oa), (kb, gb, sb, ob)):
                        send[...] = add_low(k[half:], g[half:])
                        out[...] = add_low(k[:half], g[:half])

                out = [shape((half, *rest), BF16)] * 4
                sa, oa, sb, ob = small_call(kernel, out, [keep_a, self.got[0], keep_b, self.got[1]], [after], name)
                self.halves = [[sa, oa], [sb, ob]]
                self.got = [dp_swap(sa, first[1]), dp_swap(sb, second[1])]
                return oa

            def kernel(ka, ga, kb, gb, out):
                for n, (k, g) in enumerate(((ka, ga), (kb, gb))):
                    out[n] = add_low(k[...], g[...])

            out = [shape((2, parts, *rest), BF16)]
            both = small_call(kernel, out, [keep_a, self.got[0], keep_b, self.got[1]], [after], name)[0]
            self.halves = [[None, both], [None, both]]
            self.got = [dp_swap(both, first[2]), None]
            return both
        if level == 2:

            def kernel(k, g, oa, ob):
                for n, out in enumerate((oa, ob)):
                    for j in range(2):
                        out[j] = add_low(k[n, j], g[n, 1 - j])

            out = [shape(keep_a.shape[1:], BF16)] * 2
            oa, ob = small_call(kernel, out, [keep_a, self.got[0]], [after], name)
            self.halves = [[None, oa], [None, ob]]
            self.got = [dp_swap(oa, first[1]), dp_swap(ob, second[1])]
            return oa
        rest = keep_a.shape[1:]

        def kernel(ka, ga, kb, gb, oa, ob):
            for k, g, out in ((ka, ga, oa), (kb, gb, ob)):
                out[:2] = k[...]
                out[2:] = g[...]

        out = [shape((4, *rest), BF16)] * 2
        oa, ob = small_call(kernel, out, [keep_a, self.got[0], keep_b, self.got[1]], [after], name)
        self.halves = [[None, oa], [None, ob]]
        self.got = [dp_swap(oa, first[0]), dp_swap(ob, second[0])]
        return oa

    def collect(self, which):
        if not self.direct:
            if self.summed[which] is None:
                send, keep = lax.psum(tuple(self.halves[which]), "dp")
                self.summed[which] = keep, send
            return self.summed[which]
        return self.halves[which][1], self.got[which]


HB = pl.BlockSpec(memory_space=pltpu.HBM)


def place_half(ids, order, value, flip, base, after, name):
    _, part, cols = value.shape
    given = [] if base is None else [pltpu.with_memory_space_constraint(base, pltpu.HBM)]

    def kernel(ids_ref, value_ref, *refs):
        out, wide, sems = refs[-3:]
        copies = []
        for r in range(4):
            start = ((ids_ref[order] ^ flip) * 4 + (ids_ref[order + 1] ^ r)) * part
            wide[r] = value_ref[r].astype(F32)
            rows = out.at[pl.ds(pl.multiple_of(start, 8), part), :]
            copies.append(pltpu.make_async_copy(wide.at[r], rows, sems.at[r]))
            copies[-1].start()
        for copy in copies:
            copy.wait()

    return pl.pallas_call(
        kernel,
        grid_spec=pltpu.PrefetchScalarGridSpec(
            num_scalar_prefetch=1,
            grid=(1,),
            in_specs=[VM] + [HB] * len(given) + [ANY] * len(after),
            out_specs=HB,
            scratch_shapes=[pltpu.VMEM((4, part, cols), F32), pltpu.SemaphoreType.DMA((4,))],
        ),
        out_shape=pltpu.HBM((8 * part, cols), F32),
        input_output_aliases={2: 0} if given else {},
        compiler_params=params(),
        cost_estimate=cost(name),
        name=name,
    )(ids, value, *given, *after)


def place_heads(ids, orders, a, b, flip, bases, after, name):
    _, _, part, cols = a.shape
    rows = 8 * part
    given = [pltpu.with_memory_space_constraint(x, pltpu.HBM) for x in bases]

    def kernel(ids_ref, a_ref, b_ref, *refs):
        qkv_out, proj_out, wide, sems = refs[-4:]
        copies = []
        for n, (pick, order) in enumerate(((a_ref, orders[0]), (b_ref, orders[1]))):
            for r in range(4):
                at = (ids_ref[order] ^ flip) * 4 + (ids_ref[order + 1] ^ r)
                at = pl.ds(pl.multiple_of(at * part, 8), part)
                for j in range(2):
                    k = len(copies)
                    wide[k] = pick[r, j].astype(F32)
                    out = proj_out.at[at, :] if n + j == 2 else qkv_out.at[2 * n + j, at, :]
                    copies.append(pltpu.make_async_copy(wide.at[k], out, sems.at[k]))
                    copies[-1].start()
        for copy in copies:
            copy.wait()

    return list(
        pl.pallas_call(
            kernel,
            grid_spec=pltpu.PrefetchScalarGridSpec(
                num_scalar_prefetch=1,
                grid=(1,),
                in_specs=[VM, VM] + [HB] * len(given) + [ANY] * len(after),
                out_specs=[HB, HB],
                scratch_shapes=[pltpu.VMEM((16, part, cols), F32), pltpu.SemaphoreType.DMA((16,))],
            ),
            out_shape=[pltpu.HBM((3, rows, cols), F32), pltpu.HBM((rows, cols), F32)],
            input_output_aliases={3: 0, 4: 1} if given else {},
            compiler_params=params(),
            cost_estimate=cost(name),
            name=name,
        )(ids, a, b, *given, *after)
    )


def mid_back_kernel(pair, other, residual, cot, gain, grad_out, *refs):
    low_out, sums = refs[:-1], refs[-1]
    i = pl.program_id(0)
    err = pair[...].astype(F32) + other[...].astype(F32)
    unit, scale = norm_stats(residual[...])
    top = cot[...].astype(F32)
    f = err * row_vector(gain)
    f_mean = jnp.mean(f, axis=-1, keepdims=True)
    fx_mean = jnp.mean(f * unit, axis=-1, keepdims=True)
    grad = top + scale * (f - f_mean - unit * fx_mean)
    grad_out[...] = grad
    low = grad.astype(BF16)
    per = PAIR // low_out[0].shape[0]
    for n, piece in enumerate(low_out):

        @pl.when(i == n // per)
        def _():
            rows = piece.shape[0]
            piece[...] = low[(n % per) * rows : (n % per + 1) * rows]

    @pl.when(i == 0)
    def _():
        sums[...] = jnp.zeros_like(sums)

    sums[0:1] += jnp.sum(err * unit, axis=0, keepdims=True)
    sums[1:2] += jnp.sum(err, axis=0, keepdims=True)
    sums[2:3] += jnp.sum(top, axis=0, keepdims=True)


def mid_back(chunk, chunks, ids, pair, other, residual, cot, gain, pieces, after):
    rows, width = residual.shape
    half = rows // PAIR
    row = pl.BlockSpec((PAIR, width), lambda i, ids: (i, 0))
    return pl.pallas_call(
        lambda ids, *refs: mid_back_kernel(*refs[:5], *refs[5 + len(after) :]),
        grid_spec=pltpu.PrefetchScalarGridSpec(
            num_scalar_prefetch=1,
            grid=(half,),
            in_specs=[
                row, row, row,
                pl.BlockSpec((PAIR, width), lambda i, ids: (block_of(i + half, ids, chunk, half, chunks), 0)),
                whole(gain),
            ]
            + [ANY] * len(after),
            out_specs=[row] + [VM] * pieces + [pl.BlockSpec((8, width), lambda i, ids: (0, 0))],
        ),
        out_shape=[shape((rows, width), F32)] + [shape((rows // pieces, width), BF16)] * pieces + [shape((8, width), F32)],
        compiler_params=params(),
        cost_estimate=cost("mid_back"),
        name="mid_back",
    )(ids, pair, other, residual, cot, gain, *after)


def attend_back_kernel(count, blocks, *refs):
    peers, owns = refs[:count], refs[count : 2 * count]
    q_ref, k_ref, v_ref, p_ref, w_qkv, wo = refs[2 * count : 2 * count + 6]
    sends, (keep, dq_out, dk_out, dv_out, low_ref, part_ref) = refs[2 * count + 6 : -6], refs[-6:]
    i = pl.program_id(0)
    half = blocks // 2
    rows = peers[0].shape[0]

    @pl.when(i == 0)
    def _():
        for n, piece in enumerate((*peers, *owns)):
            low_ref[n * rows : (n + 1) * rows] = piece[...]

    low = low_ref[pl.ds(pl.multiple_of(i * PAIR, PAIR), PAIR), :]
    grad_context = mm(low, wo[...], 1, 1).astype(BF16)
    q, k, v = q_ref[...], k_ref[...], v_ref[...]
    width = q.shape[1]
    head = lax.broadcasted_iota(jnp.int32, (1, width), 1) // HEAD_DIM
    zero = jnp.zeros_like(q)
    dq = dk = dv = jnp.zeros((PAIR, width), F32)
    for h in range(width // HEAD_DIM):
        mine = head == h
        gh = jnp.where(mine, grad_context, zero)
        weights = p_ref[0, h]
        grad_p = mm(gh, v, 1, 1)
        wide = weights.astype(F32)
        dot = jnp.sum(wide * grad_p, axis=-1, keepdims=True)
        grad_s = (wide * (grad_p - dot)).astype(BF16)
        dv = dv + mm(weights, gh, 0, 0)
        dq = dq + mm(grad_s, jnp.where(mine, k, zero), 1, 0)
        dk = dk + mm(grad_s, jnp.where(mine, q, zero), 0, 0)
    scale = HEAD_DIM**-0.5
    dq = (dq * scale).astype(BF16)
    dk = (dk * scale).astype(BF16)
    dv = dv.astype(BF16)
    dq_out[...] = dq
    dk_out[...] = dk
    dv_out[...] = dv
    part = (mm(dq, w_qkv[0], 1, 0) + mm(dk, w_qkv[1], 1, 0) + mm(dv, w_qkv[2], 1, 0)).astype(BF16)
    part_ref[...] = part
    per = PAIR // sends[0].shape[0]
    for n, piece in enumerate(sends):

        @pl.when(i == n // per)
        def _():
            size = piece.shape[0]
            piece[...] = part_ref[(n % per) * size : (n % per + 1) * size]

    @pl.when(i >= half)
    def _():
        keep[...] = part


def attend_back(peers, owns, q, k, v, p, w_qkv, wo, pieces, after):
    rows, local = q.shape
    width = wo.shape[1]
    blocks = rows // PAIR
    half = blocks // 2
    heads = local // HEAD_DIM
    count = len(peers)
    ins = 2 * count + 6
    second = pl.BlockSpec((PAIR, width), lambda i: (jnp.maximum(i - half, 0), 0))
    thin = pl.BlockSpec((PAIR, local), lambda i: (i, 0))
    return pl.pallas_call(
        lambda *refs: attend_back_kernel(count, blocks, *refs[:ins], *refs[ins + len(after) :]),
        grid=(blocks,),
        in_specs=[VM] * (2 * count)
        + [
            thin, thin, thin,
            pl.BlockSpec((1, heads, PAIR, PAIR), lambda i: (i, 0, 0, 0)),
            whole(w_qkv), whole(wo),
        ]
        + [ANY] * len(after),
        out_specs=[VM] * pieces + [second, thin, thin, thin],
        out_shape=[shape((rows // 2 // pieces, width), BF16)] * pieces
        + [shape((rows // 2, width), BF16)]
        + [shape((rows, local), BF16)] * 3,
        scratch_shapes=[pltpu.VMEM((rows, width), BF16), pltpu.VMEM((PAIR, width), BF16)],
        compiler_params=params(),
        cost_estimate=cost("attend_back"),
        name="attend_back",
    )(*peers, *owns, q, k, v, p, w_qkv, wo, *after)


def last_kernel(count, *refs):
    pairs, others = refs[:count], refs[count : 2 * count]
    hidden, grad_residual, gain, low_out, sums, times = refs[2 * count :]
    i = pl.program_id(0)
    pair = jnp.where(i == 0, pairs[0][...], pairs[1][...])
    other = jnp.where(i == 0, others[0][...], others[1][...])
    err = pair.astype(F32) + other.astype(F32)
    unit, scale = norm_stats(hidden[...])
    f = err * row_vector(gain)
    f_mean = jnp.mean(f, axis=-1, keepdims=True)
    fx_mean = jnp.mean(f * unit, axis=-1, keepdims=True)
    grad = grad_residual[...] + scale * (f - f_mean - unit * fx_mean)
    low_out[...] = grad.astype(BF16)

    @pl.when(i == 0)
    def _():
        sums[...] = jnp.zeros_like(sums)

    sums[0:1] += jnp.sum(err * unit, axis=0, keepdims=True)
    sums[1:2] += jnp.sum(err, axis=0, keepdims=True)
    times[0, 0:1] = jnp.sum(grad[:SHORT], axis=0, keepdims=True)
    times[0, 1:2] = jnp.sum(grad[SHORT:], axis=0, keepdims=True)


def last_back(pair, other, hidden, grad_residual, gain, after):
    rows, width = hidden.shape
    half = rows // PAIR
    row = pl.BlockSpec((PAIR, width), lambda i: (i, 0))
    return pl.pallas_call(
        lambda *refs: last_kernel(2, *refs[:7], *refs[7 + len(after) :]),
        grid=(half,),
        in_specs=[VM] * 4 + [row, row, whole(gain)] + [ANY] * len(after),
        out_specs=[
            row,
            pl.BlockSpec((8, width), lambda i: (0, 0)),
            pl.BlockSpec((1, 2, width), lambda i: (i, 0, 0)),
        ],
        out_shape=[shape((rows, width), BF16), shape((8, width), F32), shape((half, 2, width), F32)],
        compiler_params=params(),
        cost_estimate=cost("last_back"),
        name="last_back",
    )(*pair, *other, hidden, grad_residual, gain, *after)


def pack_sums(vec2, vec1, up, times, after):
    pairs, _, width = times.shape

    def kernel(v2, v1, u, t, out):
        out[0:3] = v2[0:3]
        out[3:5] = v1[0:2]
        out[5:6] = u[...]
        out[6:8] = jnp.zeros((2, width), F32)
        for n in range(pairs):
            out[8 + 2 * n : 10 + 2 * n] = t[n]

    return small_call(kernel, [shape((8 + 2 * pairs, width), F32)], [vec2, vec1, up, times], after, "pack_sums")[0]


def join_sums(a, b, after, name):
    rows, width = a.shape
    more = rows - 8

    def kernel(a_ref, b_ref, out):
        out[0:8] = a_ref[0:8] + b_ref[0:8]
        out[8 : 8 + more] = a_ref[8:]
        out[8 + more :] = b_ref[8:]

    return small_call(kernel, [shape((8 + 2 * more, width), F32)], [a, b], after, name)[0]


def table_kernel(slots, steps, ids, own, other, *refs):
    vec_out, (out, table, acc, at_ref) = refs[:6], refs[6:]
    groups = at_ref.shape[0]
    rows, (row_length, row_group, row_step) = row_fields(ids)
    local = table.shape[2]
    half = slots // 2
    for n, vec in enumerate(vec_out):
        row = own[n : n + 1] + (other[n : n + 1] if n < 5 else 0.0)
        vec[...] = row.reshape(row.shape[1])
    for p in range(own.shape[1] // local):

        @pl.when(ids[2] == p)
        def _():
            table[0] = own[8:, p * local : (p + 1) * local]
            table[1] = other[8:, p * local : (p + 1) * local]

    acc[...] = jnp.zeros_like(acc)

    def clear(g, _):
        at_ref[g] = 0
        return 0

    lax.fori_loop(0, groups, clear, 0)

    def place(long):
        def one(r, _):
            @pl.when((row_length(r) > SHORT) == long)
            def _():
                g = row_group(r)
                at = at_ref[g]
                at_ref[g] = at + (2 if long else 1)
                which = (at // half) ^ ids[0]
                base = (g ^ ids[1]) * half + lax.rem(at, half)
                value = table[which, pl.ds(base, 1), :]
                if long:
                    value = value + table[which, pl.ds(base + 1, 1), :]
                step = pl.ds(row_step(r), 1)
                acc[step, :] = acc[step, :] + value

            return 0

        lax.fori_loop(0, rows, one, 0)

    place(True)
    place(False)
    out[...] = jnp.transpose(acc[...])[:, :steps]


def table_grad(scalars, own, other, steps, local, slots, after):
    rows, width = own.shape
    groups = (rows - 8) * 2 // slots
    return pl.pallas_call(
        lambda *refs: table_kernel(slots, steps, *refs[:3], *refs[3 + len(after) :]),
        grid_spec=pltpu.PrefetchScalarGridSpec(
            num_scalar_prefetch=1,
            grid=(1,),
            in_specs=[VM, VM] + [ANY] * len(after),
            out_specs=[pl.BlockSpec((width,), lambda *_: (0,))] * 6 + [pl.BlockSpec((local, steps), lambda *_: (0, 0))],
            scratch_shapes=[
                pltpu.VMEM((2, rows - 8, local), F32),
                pltpu.VMEM((pl.cdiv(steps, 128) * 128, local), F32),
                pltpu.SMEM((groups,), jnp.int32),
            ],
        ),
        out_shape=[pltpu.HBM((width,), F32)] * 6 + [pltpu.HBM((local, steps), F32)],
        compiler_params=params(),
        cost_estimate=cost("table_grad"),
        name="table_grad",
    )(scalars, own, other, *after)


def finish(residuals, pair, other, bias, after):
    rows, width = pair.shape
    part = rows // len(residuals)

    def kernel(*refs):
        res = refs[: len(residuals)]
        pair_ref, other_ref, bias_ref = refs[len(residuals) : len(residuals) + 3]
        out = refs[-1]
        for n, r in enumerate(res):
            at = slice(n * part, (n + 1) * part)
            total = r[...] + (pair_ref[at].astype(F32) + other_ref[at].astype(F32))
            out[at] = (total + row_vector(bias_ref)).astype(BF16)

    return small_call(kernel, [shape((rows, width), BF16)], [*residuals, pair, other, bias], after, "finish")[0]


def order_rows(ids, own, other, after, name):
    part, width = own.shape

    def kernel(ids_ref, own_ref, other_ref, *refs):
        out, sems = refs[len(after) :]
        copies = []
        for n, ref in enumerate((own_ref, other_ref)):
            start = pl.multiple_of((ids_ref[0] ^ n) * part, 16)
            copies.append(pltpu.make_async_copy(ref, out.at[pl.ds(start, part), :], sems.at[n]))
            copies[-1].start()
        for copy in copies:
            copy.wait()

    return pl.pallas_call(
        kernel,
        grid_spec=pltpu.PrefetchScalarGridSpec(
            num_scalar_prefetch=1,
            grid=(1,),
            in_specs=[VM, VM] + [ANY] * len(after),
            out_specs=HB,
            scratch_shapes=[pltpu.SemaphoreType.DMA((2,))],
        ),
        out_shape=pltpu.HBM((2 * part, width), BF16),
        compiler_params=params(),
        cost_estimate=cost(name),
        name=name,
    )(ids, own, other, *after)


def shards(
    tokens, row_length, row_group, row_step, time_table, norm1_gain, norm1_bias, w_qkv, w_out,
    norm2_gain, norm2_bias, w_up, up_bias, w_down, down_bias, cotangent,
):
    count, width = tokens.shape
    n_dp = lax.axis_size("dp")
    dp = lax.axis_index("dp")
    part = lax.axis_index("tensor")
    core = lax.rem(part, 2)
    direct = n_dp == 8
    low_bit, mid_bit, top_bit = dp & 1, (dp >> 1) & 1, (dp >> 2) & 1
    if direct:
        orders = [low_bit, 2 * mid_bit + top_bit, mid_bit, 2 * low_bit + top_bit]
    else:
        orders = [1, 0, 1, 0]
    own = jnp.stack([core, dp, part, *[jnp.int32(o) for o in orders], jnp.int32(0)]).astype(jnp.int32)
    ids = jnp.concatenate([own, row_length, row_group, row_step])
    scalars = ids
    order_a, order_b = 3, 5
    bits = ((1, 2, 4), (2, 1, 4))
    local = w_out.shape[0]
    slots = count // SHORT
    heads = jnp.transpose(w_qkv, (1, 2, 0))
    far = lambda x: pltpu.with_memory_space_constraint(x, pltpu.HBM)
    size = count // 2
    peer_rows = lambda ids: 1 - ids[0]
    own_rows = lambda ids: ids[0]
    zero = lambda ids: 0
    one = lambda ids: 1

    send, keep, hidden, normed, q, k, v, p, ctx = attend(
        0, 1, scalars, *[far(x) for x in (tokens, time_table, norm1_gain, norm1_bias, heads, w_out)], []
    )
    pair = add_two(keep, core_swap(send), [], "pair_one")
    other = chip_swap(pair)
    w_up, w_down, cotangent = stage([far(x) for x in (w_up, w_down, cotangent)], [pair])
    grad_act = act_grad(cotangent, w_down)
    residual, own2 = mid_forward(hidden, pair, other, norm2_gain, norm2_bias, [grad_act])
    peer2 = core_swap(own2)
    send, keep, act, low, up_sum = expand(0, 1, ids, peer2, own2, grad_act, w_up, up_bias, [])
    got_two = core_swap(send)
    first_keep = keep
    cots = [(cotangent, size, f) for f in (peer_rows, own_rows)]
    acts = [(act, size, f) for f in (zero, one)]
    lows = [(low, size, f) for f in (zero, one)]
    norms = [(peer2, size, zero), (own2, size, zero)]
    mlp = Dual(bits, direct)
    heads_sum = Dual(bits, direct)
    it = types.SimpleNamespace(attn=[])
    placed = [None, None]

    def down_grad(after):
        halves = weight_grad(ids, order_a, [list(zip(acts, cots))], after, "down_grad")
        mlp.begin(0, halves)
        return halves[1]

    def up_grad(after):
        halves = weight_grad(ids, order_b, [list(zip(norms, lows))], after, "up_grad")
        mlp.begin(1, halves)
        return halves[1]

    def pair_two(after):
        it.pair2 = add_two(first_keep, got_two, after, "pair_two")
        it.other2 = chip_swap(it.pair2)
        return it.pair2

    def contract(after):
        send, it.keep_e = contract_rows(act, w_down, after)
        it.got_e = core_swap(send)
        return it.keep_e

    def mid(after):
        it.grad_res, *it.low_own, it.vec2 = mid_back(
            0, 1, ids, it.pair2, it.other2, residual, cotangent, norm2_gain, LOW_PIECES, after
        )
        it.low_peer = [core_swap(x) for x in it.low_own]
        return it.low_own[0]

    def attend_grad(after):
        *send, it.keep3, it.dq, it.dk, it.dv = attend_back(
            it.low_peer, it.low_own, q, k, v, p, heads, w_out, PART_PIECES, after
        )
        it.got3 = [core_swap(x) for x in send]
        return it.keep3

    def qk_grad(after):
        halves = head_grad(ids, order_a, (it.dq, [normed]), (it.dk, [normed]), after, "qk_grad")
        heads_sum.begin(0, halves)
        return halves[1]

    def vo_grad(after):
        lows = [*it.low_peer, *it.low_own]
        halves = head_grad(ids, order_b, (it.dv, [normed]), (ctx, lows), after, "vo_grad")
        heads_sum.begin(1, halves)
        return halves[1]

    def pair_three(after):
        it.pair3 = add_pieces(it.keep3, it.got3, 2, after, "pair_three")
        it.other3 = [chip_swap(x) for x in it.pair3]
        return it.pair3[0]

    def pair_out(after):
        it.pair_e = add_two(it.keep_e, it.got_e, after, "pair_out")
        it.other_e = chip_swap(it.pair_e)
        return it.pair_e

    def last(after):
        it.low_in, it.vec1, it.times = last_back(
            it.pair3, it.other3, hidden, it.grad_res, norm1_gain, after
        )
        it.low_got = core_swap(it.low_in)
        return it.low_in

    def pack(after):
        it.sums = pack_sums(it.vec2, it.vec1, up_sum, it.times, after)
        it.sums_got = dp_swap(it.sums, 1)
        return it.sums

    def join(level):
        def run(after):
            bit = 2 << level
            sums = join_sums(it.sums, it.sums_got, after, "join_sums")
            while level == 2 and bit < n_dp:
                sums = join_sums(sums, dp_swap(sums, bit), [], "join_sums")
                bit *= 2
            it.sums = sums
            if level < 2:
                it.sums_got = dp_swap(sums, bit)
            else:
                it.sums_peer = core_swap(sums)
            return sums

        return run

    def input_rows(after):
        it.input_grad = order_rows(ids, it.low_in, it.low_got, after, "order_input")
        return far(it.input_grad)

    def final(after):
        it.final = finish([residual], it.pair_e, it.other_e, down_bias, after)
        it.final_got = core_swap(it.final)
        return it.final

    def output_rows(after):
        it.block_output = order_rows(ids, it.final, it.final_got, after, "order_output")
        return far(it.block_output)

    def table(after):
        *it.vec, it.time_grad = table_grad(
            scalars, it.sums, it.sums_peer, time_table.shape[0], local, slots, after
        )
        return far(it.vec[0])

    def place(which, half):
        def run(after):
            order, value = (order_a, order_b)[which], mlp.collect(which)[half]
            placed[which] = place_half(ids, order, value, half, placed[which], after, ("place_down", "place_up")[which])
            return far(placed[which])

        return run

    def place_attn(half):
        def run(after):
            a, b = heads_sum.collect(0)[half], heads_sum.collect(1)[half]
            it.attn = place_heads(ids, (order_a, order_b), a, b, half, it.attn, after, "place_heads")
            return far(it.attn[1])

        return run

    def sum_step(group):
        return lambda after: group.step(after[0])

    order = (
        down_grad, pair_two, up_grad, contract, mid, sum_step(mlp), attend_grad, sum_step(mlp), pair_out,
        vo_grad, pair_three, qk_grad, sum_step(heads_sum), last, sum_step(heads_sum), pack, sum_step(mlp),
        join(0), sum_step(heads_sum), join(1), sum_step(mlp), place(0, 0), sum_step(heads_sum), place(1, 0),
        join(2), final, input_rows, output_rows, table, place_attn(0), place(1, 1), place(0, 1), place_attn(1),
    )
    mark = first_keep
    for step in order:
        mark = step([mark])
    vec, time_grad = it.vec, it.time_grad
    block_output, input_grad = it.block_output, it.input_grad
    down_out, up_out = placed
    qkv_out, proj_out = it.attn

    return (
        block_output,
        input_grad,
        time_grad.T,
        vec[3],
        vec[4],
        jnp.transpose(qkv_out, (2, 0, 1)),
        proj_out,
        vec[0],
        vec[1],
        up_out,
        vec[5],
        down_out,
        vec[2],
    )


def solution(mesh):
    in_specs = (
        P("dp", None), P(), P(), P(), P(), P(), P(), P(None, None, "tensor"), P("tensor", None), P(), P(),
        P(None, "tensor"), P("tensor"), P("tensor", None), P(), P("dp", None),
    )
    out_specs = (
        P("dp", None), P("dp", None), P(None, "tensor"), P(), P(), P(None, None, "tensor"), P("tensor", None),
        P(), P(), P(None, "tensor"), P("tensor"), P("tensor", None), P(),
    )
    return jax.shard_map(shards, mesh=mesh, in_specs=in_specs, out_specs=out_specs, check_vma=False)
```

```python
import functools
import types

import jax
import jax.numpy as jnp
from jax import lax
from jax.experimental import pallas as pl
from jax.experimental.pallas import tpu as pltpu
from jax.sharding import PartitionSpec as P

HEAD_DIM = 64
SHORT = 128
PAIR = 256
EPS = 1e-05
NEG = -1000000000.0
SQRT_HALF = 0.7071067811865476
PHI_ZERO = 0.3989422804014327
VMEM_MB = 16
LOW_PIECES = 2
PART_PIECES = 4

SMALL_MB = 8

F32 = jnp.float32
BF16 = jnp.bfloat16


def mm(left, right, left_dim, right_dim):
    return lax.dot_general(
        left, right, (((left_dim,), (right_dim,)), ((), ())), preferred_element_type=F32
    )


def params(dims=1):
    return pltpu.CompilerParams(
        dimension_semantics=("arbitrary",) * dims, vmem_limit_bytes=VMEM_MB << 20
    )


COSTS = {"finish": 0.5, "up_grad": 1}


def cost(name):
    return pl.CostEstimate(flops=int(COSTS.get(name, 0) * 1e9), bytes_accessed=1, transcendentals=0)


def shape(dims, dtype):
    return jax.ShapeDtypeStruct(dims, dtype)


def whole(array):
    zeros = (0,) * array.ndim
    return pl.BlockSpec(array.shape, lambda *_: zeros)


def swap(value, axis, bit):
    return lax.ppermute(value, axis, [(i, i ^ bit) for i in range(lax.axis_size(axis))])


def core_swap(value):
    return swap(value, "tensor", 1)


def chip_swap(value):
    return swap(value, "tensor", 2)


def dp_swap(value, bit):
    return swap(value, "dp", bit)


def norm_stats(values):
    mean = jnp.mean(values, axis=-1, keepdims=True)
    centred = values - mean
    variance = jnp.mean(centred * centred, axis=-1, keepdims=True)
    scale = lax.rsqrt(variance + EPS)
    return centred * scale, scale


IDS = 8


def row_fields(info):
    rows = (info.shape[0] - IDS) // 3
    return rows, [lambda r, at=at: info[IDS + at * rows + r] for at in range(3)]


def fill_slots(slot_ref, info):
    group = info[1]
    rows, (row_length, row_group, row_step) = row_fields(info)

    def long_row(r, pos):
        step = row_step(r)
        slot_ref[pos] = step
        slot_ref[pos + 1] = step
        hit = (row_group(r) == group) & (row_length(r) > SHORT)
        return pos + jnp.where(hit, 2, 0)

    def short_row(r, pos):
        slot_ref[pos] = row_step(r)
        hit = (row_group(r) == group) & (row_length(r) <= SHORT)
        return pos + jnp.where(hit, 1, 0)

    long_slots = lax.fori_loop(0, rows, long_row, 0)
    lax.fori_loop(0, rows, short_row, long_slots)
    return long_slots


def block_of(i, ids, chunk, half, chunks):
    side = jnp.where(i < half, 1 - ids[0], ids[0])
    return side * (half * chunks) + chunk * half + lax.rem(i, half)


def add_low(a, b):
    return (a.astype(F32) + b.astype(F32)).astype(BF16)


def row_vector(ref):
    return ref[...].reshape(1, ref.shape[0])


VM = pl.BlockSpec(memory_space=pltpu.VMEM)
ANY = pl.BlockSpec(memory_space=pl.ANY)


def small_call(kernel, out_shape, operands, after, name):
    count = len(operands)
    return pl.pallas_call(
        lambda *refs: kernel(*refs[:count], *refs[count + len(after) :]),
        in_specs=[VM] * count + [ANY] * len(after),
        out_specs=[VM] * len(out_shape),
        out_shape=out_shape,
        compiler_params=pltpu.CompilerParams(vmem_limit_bytes=SMALL_MB << 20),
        cost_estimate=cost(name),
        name=name,
    )(*operands, *after)


def stage(arrays, after):
    count = len(arrays)

    def kernel(*refs):
        out, sems = refs[count + len(after) : -1], refs[-1]
        copies = [pltpu.make_async_copy(refs[n], out[n], sems.at[n]) for n in range(count)]
        for copy in copies:
            copy.start()
        for copy in copies:
            copy.wait()

    return pl.pallas_call(
        kernel,
        in_specs=[pl.BlockSpec(memory_space=pltpu.HBM)] * count + [ANY] * len(after),
        out_specs=[VM] * count,
        out_shape=[pltpu.VMEM(a.shape, a.dtype) for a in arrays],
        scratch_shapes=[pltpu.SemaphoreType.DMA((count,))],
        compiler_params=pltpu.CompilerParams(vmem_limit_bytes=SMALL_MB << 20),
        cost_estimate=cost("stage"),
        name="stage",
    )(*arrays, *after)


def add_two(a, b, after, name):
    def kernel(a_ref, b_ref, out):
        out[...] = add_low(a_ref[...], b_ref[...])

    return small_call(kernel, [shape(a.shape, BF16)], [a, b], after, name)[0]


def attend_kernel(
    chunk, half, chunks, slots, ids,
    tokens, table, gain, bias, w_qkv, wo,
    send, keep, hidden_out, normed_out, q_out, k_out, v_out, p_out, c_out,
    slot_ref, rows_ref, sems,
):
    i = pl.program_id(0)

    def fetch(s):
        step = slot_ref[s]
        start = pl.multiple_of((step // 8) * 8, 8)
        return pltpu.make_async_copy(table.at[pl.ds(start, 8), :], rows_ref.at[s], sems.at[s])

    @pl.when(i == 0)
    def _():
        slot_ref[slots + 2] = fill_slots(slot_ref, ids)
        for s in range(slots):
            fetch(s).start()
        for s in range(slots):
            fetch(s).wait()

    block = block_of(i, ids, chunk, half, chunks)
    sub = lax.broadcasted_iota(jnp.int32, (8, 1), 0)

    def row_of(s):
        picked = sub == lax.rem(slot_ref[s], 8)
        return jnp.sum(jnp.where(picked, rows_ref[s].astype(F32), 0.0), axis=0, keepdims=True)

    low_half = lax.broadcasted_iota(jnp.int32, (PAIR, 1), 0) < SHORT
    step_row = jnp.where(low_half, row_of(2 * block), row_of(2 * block + 1))
    hidden = tokens[...].astype(F32) + step_row
    unit, _ = norm_stats(hidden)
    normed = (unit * row_vector(gain) + row_vector(bias)).astype(BF16)
    normed_out[...] = normed
    q = mm(normed, w_qkv[0], 1, 1).astype(BF16)
    k = mm(normed, w_qkv[1], 1, 1).astype(BF16)
    v = mm(normed, w_qkv[2], 1, 1).astype(BF16)
    q_out[...] = q
    k_out[...] = k
    v_out[...] = v
    split = (2 * block >= slot_ref[slots + 2]).astype(jnp.int32)
    row_half = lax.broadcasted_iota(jnp.int32, (PAIR, PAIR), 0) // SHORT
    col_half = lax.broadcasted_iota(jnp.int32, (PAIR, PAIR), 1) // SHORT
    allowed = ((row_half ^ col_half) * split) == 0
    width = q.shape[1]
    head = lax.broadcasted_iota(jnp.int32, (1, width), 1) // HEAD_DIM
    context = jnp.zeros((PAIR, width), F32)
    for h in range(width // HEAD_DIM):
        mine = head == h
        qh = jnp.where(mine, q, jnp.zeros_like(q))
        scores = mm(qh, k, 1, 1) * (HEAD_DIM**-0.5)
        scores = jnp.where(allowed, scores, NEG)
        top = jnp.max(scores, axis=-1, keepdims=True)
        powers = jnp.exp(scores - top)
        total = jnp.sum(powers, axis=-1, keepdims=True)
        weights = (powers * (1.0 / total)).astype(BF16)
        p_out[0, h] = weights
        context = context + mm(weights, jnp.where(mine, v, jnp.zeros_like(v)), 1, 0)
    low = context.astype(BF16)
    c_out[...] = low
    part = mm(low, wo[...], 1, 0).astype(BF16)

    @pl.when(i < half)
    def _():
        send[...] = part

    @pl.when(i >= half)
    def _():
        keep[...] = part
        hidden_out[...] = hidden


def attend(chunk, chunks, scalars, tokens, table, gain, bias, w_qkv, wo, after):
    count, width = tokens.shape
    local = wo.shape[0]
    blocks = count // PAIR // chunks
    half = blocks // 2
    rows = blocks * PAIR
    slots = count // SHORT
    own = rows // 2
    heads = local // HEAD_DIM
    first = lambda i, *_: (jnp.minimum(i, half - 1), 0)
    second = lambda i, *_: (jnp.maximum(i - half, 0), 0)
    step = lambda i, *_: (i, 0)
    row = pl.BlockSpec((PAIR, width), step)
    thin = pl.BlockSpec((PAIR, local), step)
    return pl.pallas_call(
        lambda *refs: attend_kernel(chunk, half, chunks, slots, *refs[:7], *refs[7 + len(after) :]),
        grid_spec=pltpu.PrefetchScalarGridSpec(
            num_scalar_prefetch=1,
            grid=(blocks,),
            in_specs=[
                pl.BlockSpec((PAIR, width), lambda i, ids, *_: (block_of(i, ids, chunk, half, chunks), 0)),
                pl.BlockSpec(memory_space=pltpu.HBM),
                whole(gain), whole(bias), whole(w_qkv), whole(wo),
            ]
            + [ANY] * len(after),
            out_specs=[
                pl.BlockSpec((PAIR, width), first),
                pl.BlockSpec((PAIR, width), second),
                pl.BlockSpec((PAIR, width), second),
                row, thin, thin, thin,
                pl.BlockSpec((1, heads, PAIR, PAIR), lambda i, *_: (i, 0, 0, 0)),
                thin,
            ],
            scratch_shapes=[
                pltpu.SMEM((slots + 4,), jnp.int32),
                pltpu.VMEM((slots, 8, width), BF16),
                pltpu.SemaphoreType.DMA((slots,)),
            ],
        ),
        out_shape=[
            shape((own, width), BF16), shape((own, width), BF16), shape((own, width), F32),
            shape((rows, width), BF16),
            shape((rows, local), BF16), shape((rows, local), BF16), shape((rows, local), BF16),
            shape((blocks, heads, PAIR, PAIR), BF16),
            shape((rows, local), BF16),
        ],
        compiler_params=params(),
        cost_estimate=cost("attend"),
        name="attend",
    )(scalars, tokens, table, gain, bias, w_qkv, wo, *after)


def mid_kernel(hidden, pair, other, gain, bias, residual_out, normed_out):
    residual = hidden[...] + (pair[...].astype(F32) + other[...].astype(F32))
    residual_out[...] = residual
    unit, _ = norm_stats(residual)
    normed_out[...] = (unit * row_vector(gain) + row_vector(bias)).astype(BF16)


def mid_forward(hidden, pair, other, gain, bias, after):
    rows, width = hidden.shape
    row = pl.BlockSpec((PAIR, width), lambda i: (i, 0))
    return pl.pallas_call(
        lambda *refs: mid_kernel(*refs[:5], *refs[5 + len(after) :]),
        grid=(rows // PAIR,),
        in_specs=[row, row, row, whole(gain), whole(bias)] + [ANY] * len(after),
        out_specs=[row, row],
        out_shape=[shape((rows, width), F32), shape((rows, width), BF16)],
        compiler_params=params(),
        cost_estimate=cost("mid_forward"),
        name="mid_forward",
    )(hidden, pair, other, gain, bias, *after)


def act_grad(cot, w_down):
    rows, width = cot.shape
    local = w_down.shape[0]

    def kernel(cot_ref, w_ref, out):
        out[...] = mm(cot_ref[...], w_ref[...], 1, 1)

    return pl.pallas_call(
        kernel,
        grid=(rows // PAIR,),
        in_specs=[pl.BlockSpec((PAIR, width), lambda i: (i, 0)), VM],
        out_specs=pl.BlockSpec((PAIR, local), lambda i: (i, 0)),
        out_shape=shape((rows, local), F32),
        compiler_params=params(),
        cost_estimate=cost("act_grad"),
        name="act_grad",
    )(cot, w_down)


def expand_kernel(half, ids, peer, own, grad_act, w_up, up_bias, send, keep, act_out, low_out, bias_out):
    i = pl.program_id(0)
    normed = jnp.where(i < half, peer[...], own[...])
    pre = mm(normed, w_up[...], 1, 0) + row_vector(up_bias)
    cdf = 0.5 * (1.0 + lax.erf(pre * SQRT_HALF))
    act_out[...] = (pre * cdf).astype(BF16)
    slope = cdf + pre * (PHI_ZERO * jnp.exp(-0.5 * (pre * pre)))
    grad_pre = grad_act[...] * slope

    @pl.when(i == 0)
    def _():
        bias_out[...] = jnp.zeros_like(bias_out)

    bias_out[...] += jnp.sum(grad_pre, axis=0, keepdims=True)
    low = grad_pre.astype(BF16)
    low_out[...] = low
    part = mm(low, w_up[...], 1, 1).astype(BF16)

    @pl.when(i < half)
    def _():
        send[...] = part

    @pl.when(i >= half)
    def _():
        keep[...] = part


def expand(chunk, chunks, ids, peer, own, grad_act, w_up, up_bias, after):
    count, width = grad_act.shape[0], peer.shape[1]
    local = w_up.shape[1]
    blocks = count // PAIR // chunks
    half = blocks // 2
    rows = blocks * PAIR
    first = lambda i, *_: (jnp.minimum(i, half - 1), 0)
    second = lambda i, *_: (jnp.maximum(i - half, 0), 0)
    step = lambda i, *_: (i, 0)
    return pl.pallas_call(
        lambda *refs: expand_kernel(half, *refs[:6], *refs[6 + len(after) :]),
        grid_spec=pltpu.PrefetchScalarGridSpec(
            num_scalar_prefetch=1,
            grid=(blocks,),
            in_specs=[
                pl.BlockSpec((PAIR, width), first),
                pl.BlockSpec((PAIR, width), second),
                pl.BlockSpec((PAIR, local), lambda i, ids: (block_of(i, ids, chunk, half, chunks), 0)),
                VM, whole(up_bias),
            ]
            + [ANY] * len(after),
            out_specs=[
                pl.BlockSpec((PAIR, width), first),
                pl.BlockSpec((PAIR, width), second),
                pl.BlockSpec((PAIR, local), step),
                pl.BlockSpec((PAIR, local), step),
                pl.BlockSpec((1, local), lambda i, *_: (0, 0)),
            ],
        ),
        out_shape=[
            shape((rows // 2, width), BF16), shape((rows // 2, width), BF16),
            shape((rows, local), BF16), shape((rows, local), BF16),
            shape((1, local), F32),
        ],
        compiler_params=params(),
        cost_estimate=cost("expand"),
        name="expand",
    )(ids, peer, own, grad_act, w_up, up_bias, *after)


def contract_kernel(act, w_down, send, keep):
    i = pl.program_id(0)
    part = mm(act[...], w_down[...], 1, 0).astype(BF16)

    @pl.when(i < 2)
    def _():
        send[...] = part

    @pl.when(i >= 2)
    def _():
        keep[...] = part


def contract_rows(act, w_down, after):
    rows, local = act.shape
    width = w_down.shape[1]
    return pl.pallas_call(
        lambda *refs: contract_kernel(*refs[:2], *refs[2 + len(after) :]),
        grid=(rows // PAIR,),
        in_specs=[pl.BlockSpec((PAIR, local), lambda i: (i, 0)), VM] + [ANY] * len(after),
        out_specs=[
            pl.BlockSpec((PAIR, width), lambda i: (jnp.minimum(i, 1), 0)),
            pl.BlockSpec((PAIR, width), lambda i: (jnp.maximum(i - 2, 0), 0)),
        ],
        out_shape=[shape((rows // 2, width), BF16), shape((rows // 2, width), BF16)],
        compiler_params=params(),
        cost_estimate=cost("contract_rows"),
        name="contract_rows",
    )(act, w_down, *after)


def weight_kernel(order, groups, ids, *refs):
    count = sum(len(lefts) for lefts in groups)
    left, right = refs[:count], refs[count : 2 * count]
    send, keep, scratch = refs[2 * count : 2 * count + 3]
    i = pl.program_id(0)
    many = len(groups) > 1
    rows = send.shape[-2]
    at = 0
    for n, sizes in enumerate(groups):
        total = mm(left[at][...], right[at][...], 0, 0)
        for j in range(at + 1, at + len(sizes)):
            total = total + mm(left[j][...], right[j][...], 0, 0)
        at += len(sizes)
        scratch[n] = total

    def write(out):
        for r in range(4):
            start = pl.multiple_of((ids[order + 1] ^ r) * rows, 8)
            for n in range(len(groups)):
                value = scratch[n, pl.ds(start, rows), :].astype(BF16)
                if many:
                    out[r, n] = value
                else:
                    out[r] = value

    @pl.when(i == 0)
    def _():
        write(send)

    @pl.when(i == 1)
    def _():
        write(keep)


def weight_grad(ids, order, groups, after, name):
    rows_out = groups[0][0][0][0].shape[1]
    tile = rows_out // 2
    part = tile // 4
    cols = groups[0][0][1][0].shape[1]
    lefts = [left for pieces in groups for left, _ in pieces]
    rights = [right for pieces in groups for _, right in pieces]
    count = sum(size for _, size, _ in lefts)

    def column(i, ids):
        return jnp.where(i == 0, 1 - ids[order], ids[order])

    specs = [pl.BlockSpec((size, tile), lambda i, ids, at=at: (at(ids), column(i, ids))) for _, size, at in lefts]
    specs += [pl.BlockSpec((size, cols), lambda i, ids, at=at: (at(ids), 0)) for _, size, at in rights]
    dims = (4, part, cols) if len(groups) == 1 else (4, len(groups), part, cols)
    out = pl.BlockSpec(dims, lambda i, ids: (0,) * len(dims))
    kernel = functools.partial(weight_kernel, order, [[size for (_, size, _), _ in g] for g in groups])
    total = len(lefts)
    return list(pl.pallas_call(
        lambda ids, *refs: kernel(ids, *refs[: 2 * total], *refs[2 * total + len(after) :]),
        grid_spec=pltpu.PrefetchScalarGridSpec(
            num_scalar_prefetch=1,
            grid=(2,),
            in_specs=specs + [ANY] * len(after),
            out_specs=[out, out],
            scratch_shapes=[pltpu.VMEM((len(groups), tile, cols), F32)],
        ),
        out_shape=[shape(dims, BF16), shape(dims, BF16)],
        compiler_params=params(),
        cost_estimate=cost(name),
        name=name,
    )(ids, *[a for a, _, _ in lefts], *[b for b, _, _ in rights], *after))


def head_grad(ids, order, first, second, after, name):
    rows_out, cols = first[0].shape[1], first[1][0].shape[1]
    part = rows_out // 8
    flat = [first[0], *first[1], second[0], *second[1]]

    def kernel(ids_ref, *refs):
        values = refs[: len(flat)]
        send, keep, scratch = refs[len(flat) + len(after) :]
        at = 0
        for n, (_, pieces) in enumerate((first, second)):
            rights = [values[at + 1 + j][...] for j in range(len(pieces))]
            right = rights[0] if len(rights) == 1 else jnp.concatenate(rights, axis=0)
            scratch[n] = mm(values[at][...], right, 0, 0)
            at += 1 + len(pieces)
        for half, out in ((1 - ids_ref[order], send), (ids_ref[order], keep)):
            for r in range(4):
                start = pl.multiple_of((half * 4 + (ids_ref[order + 1] ^ r)) * part, 8)
                for n in range(2):
                    out[r, n] = scratch[n, pl.ds(start, part), :].astype(BF16)

    dims = (4, 2, part, cols)
    return pl.pallas_call(
        kernel,
        grid_spec=pltpu.PrefetchScalarGridSpec(
            num_scalar_prefetch=1,
            grid=(1,),
            in_specs=[VM] * len(flat) + [ANY] * len(after),
            out_specs=[VM, VM],
            scratch_shapes=[pltpu.VMEM((2, rows_out, cols), F32)],
        ),
        out_shape=[shape(dims, BF16), shape(dims, BF16)],
        compiler_params=params(),
        cost_estimate=cost(name),
        name=name,
    )(ids, *flat, *after)


def add_pieces(a, b, pieces, after, name):
    rows, width = a.shape
    size, out_size = rows // len(b), rows // pieces
    step = min(size, out_size)

    def kernel(a_ref, *refs):
        given, out = refs[: len(b)], refs[len(b) :]
        for at in range(0, rows, step):
            got = given[at // size][at % size : at % size + step]
            out[at // out_size][at % out_size : at % out_size + step] = add_low(a_ref[at : at + step], got)

    return list(small_call(kernel, [shape((out_size, width), BF16)] * pieces, [a, *b], after, name))


class Dual:
    def __init__(self, bits, direct):
        self.bits, self.direct, self.level = bits, direct, 0
        self.summed = [None, None]
        self.halves, self.got = [None, None], [None, None]

    def begin(self, which, halves):
        self.halves[which] = list(halves)
        if self.direct:
            self.got[which] = dp_swap(halves[0], self.bits[which][0])

    def step(self, after):
        if not self.direct:
            return after
        (_, keep_a), (_, keep_b) = self.halves
        level, name = self.level, "exchange"
        self.level += 1
        first, second = self.bits
        if level < 2:
            parts, rest = keep_a.shape[0], keep_a.shape[1:]
            half = parts // 2
            if level == 0:

                def kernel(ka, ga, kb, gb, sa, oa, sb, ob):
                    for k, g, send, out in ((ka, ga, sa, oa), (kb, gb, sb, ob)):
                        send[...] = add_low(k[half:], g[half:])
                        out[...] = add_low(k[:half], g[:half])

                out = [shape((half, *rest), BF16)] * 4
                sa, oa, sb, ob = small_call(kernel, out, [keep_a, self.got[0], keep_b, self.got[1]], [after], name)
                self.halves = [[sa, oa], [sb, ob]]
                self.got = [dp_swap(sa, first[1]), dp_swap(sb, second[1])]
                return oa

            def kernel(ka, ga, kb, gb, out):
                for n, (k, g) in enumerate(((ka, ga), (kb, gb))):
                    out[n] = add_low(k[...], g[...])

            out = [shape((2, parts, *rest), BF16)]
            both = small_call(kernel, out, [keep_a, self.got[0], keep_b, self.got[1]], [after], name)[0]
            self.halves = [[None, both], [None, both]]
            self.got = [dp_swap(both, first[2]), None]
            return both
        if level == 2:

            def kernel(k, g, oa, ob):
                for n, out in enumerate((oa, ob)):
                    for j in range(2):
                        out[j] = add_low(k[n, j], g[n, 1 - j])

            out = [shape(keep_a.shape[1:], BF16)] * 2
            oa, ob = small_call(kernel, out, [keep_a, self.got[0]], [after], name)
            self.halves = [[None, oa], [None, ob]]
            self.got = [dp_swap(oa, first[1]), dp_swap(ob, second[1])]
            return oa
        rest = keep_a.shape[1:]

        def kernel(ka, ga, kb, gb, oa, ob):
            for k, g, out in ((ka, ga, oa), (kb, gb, ob)):
                out[:2] = k[...]
                out[2:] = g[...]

        out = [shape((4, *rest), BF16)] * 2
        oa, ob = small_call(kernel, out, [keep_a, self.got[0], keep_b, self.got[1]], [after], name)
        self.halves = [[None, oa], [None, ob]]
        self.got = [dp_swap(oa, first[0]), dp_swap(ob, second[0])]
        return oa

    def collect(self, which):
        if not self.direct:
            if self.summed[which] is None:
                send, keep = lax.psum(tuple(self.halves[which]), "dp")
                self.summed[which] = keep, send
            return self.summed[which]
        return self.halves[which][1], self.got[which]


HB = pl.BlockSpec(memory_space=pltpu.HBM)


def place_half(ids, order, value, flip, base, after, name):
    _, part, cols = value.shape
    given = [] if base is None else [pltpu.with_memory_space_constraint(base, pltpu.HBM)]

    def kernel(ids_ref, value_ref, *refs):
        out, wide, sems = refs[-3:]
        copies = []
        for r in range(4):
            start = ((ids_ref[order] ^ flip) * 4 + (ids_ref[order + 1] ^ r)) * part
            wide[r] = value_ref[r].astype(F32)
            rows = out.at[pl.ds(pl.multiple_of(start, 8), part), :]
            copies.append(pltpu.make_async_copy(wide.at[r], rows, sems.at[r]))
            copies[-1].start()
        for copy in copies:
            copy.wait()

    return pl.pallas_call(
        kernel,
        grid_spec=pltpu.PrefetchScalarGridSpec(
            num_scalar_prefetch=1,
            grid=(1,),
            in_specs=[VM] + [HB] * len(given) + [ANY] * len(after),
            out_specs=HB,
            scratch_shapes=[pltpu.VMEM((4, part, cols), F32), pltpu.SemaphoreType.DMA((4,))],
        ),
        out_shape=pltpu.HBM((8 * part, cols), F32),
        input_output_aliases={2: 0} if given else {},
        compiler_params=params(),
        cost_estimate=cost(name),
        name=name,
    )(ids, value, *given, *after)


def place_heads(ids, orders, a, b, flip, bases, after, name):
    _, _, part, cols = a.shape
    rows = 8 * part
    given = [pltpu.with_memory_space_constraint(x, pltpu.HBM) for x in bases]

    def kernel(ids_ref, a_ref, b_ref, *refs):
        qkv_out, proj_out, wide, sems = refs[-4:]
        copies = []
        for n, (pick, order) in enumerate(((a_ref, orders[0]), (b_ref, orders[1]))):
            for r in range(4):
                at = (ids_ref[order] ^ flip) * 4 + (ids_ref[order + 1] ^ r)
                at = pl.ds(pl.multiple_of(at * part, 8), part)
                for j in range(2):
                    k = len(copies)
                    wide[k] = pick[r, j].astype(F32)
                    out = proj_out.at[at, :] if n + j == 2 else qkv_out.at[2 * n + j, at, :]
                    copies.append(pltpu.make_async_copy(wide.at[k], out, sems.at[k]))
                    copies[-1].start()
        for copy in copies:
            copy.wait()

    return list(
        pl.pallas_call(
            kernel,
            grid_spec=pltpu.PrefetchScalarGridSpec(
                num_scalar_prefetch=1,
                grid=(1,),
                in_specs=[VM, VM] + [HB] * len(given) + [ANY] * len(after),
                out_specs=[HB, HB],
                scratch_shapes=[pltpu.VMEM((16, part, cols), F32), pltpu.SemaphoreType.DMA((16,))],
            ),
            out_shape=[pltpu.HBM((3, rows, cols), F32), pltpu.HBM((rows, cols), F32)],
            input_output_aliases={3: 0, 4: 1} if given else {},
            compiler_params=params(),
            cost_estimate=cost(name),
            name=name,
        )(ids, a, b, *given, *after)
    )


def mid_back_kernel(pair, other, residual, cot, gain, grad_out, *refs):
    low_out, sums = refs[:-1], refs[-1]
    i = pl.program_id(0)
    err = pair[...].astype(F32) + other[...].astype(F32)
    unit, scale = norm_stats(residual[...])
    top = cot[...].astype(F32)
    f = err * row_vector(gain)
    f_mean = jnp.mean(f, axis=-1, keepdims=True)
    fx_mean = jnp.mean(f * unit, axis=-1, keepdims=True)
    grad = top + scale * (f - f_mean - unit * fx_mean)
    grad_out[...] = grad
    low = grad.astype(BF16)
    per = PAIR // low_out[0].shape[0]
    for n, piece in enumerate(low_out):

        @pl.when(i == n // per)
        def _():
            rows = piece.shape[0]
            piece[...] = low[(n % per) * rows : (n % per + 1) * rows]

    @pl.when(i == 0)
    def _():
        sums[...] = jnp.zeros_like(sums)

    sums[0:1] += jnp.sum(err * unit, axis=0, keepdims=True)
    sums[1:2] += jnp.sum(err, axis=0, keepdims=True)
    sums[2:3] += jnp.sum(top, axis=0, keepdims=True)


def mid_back(chunk, chunks, ids, pair, other, residual, cot, gain, pieces, after):
    rows, width = residual.shape
    half = rows // PAIR
    row = pl.BlockSpec((PAIR, width), lambda i, ids: (i, 0))
    return pl.pallas_call(
        lambda ids, *refs: mid_back_kernel(*refs[:5], *refs[5 + len(after) :]),
        grid_spec=pltpu.PrefetchScalarGridSpec(
            num_scalar_prefetch=1,
            grid=(half,),
            in_specs=[
                row, row, row,
                pl.BlockSpec((PAIR, width), lambda i, ids: (block_of(i + half, ids, chunk, half, chunks), 0)),
                whole(gain),
            ]
            + [ANY] * len(after),
            out_specs=[row] + [VM] * pieces + [pl.BlockSpec((8, width), lambda i, ids: (0, 0))],
        ),
        out_shape=[shape((rows, width), F32)] + [shape((rows // pieces, width), BF16)] * pieces + [shape((8, width), F32)],
        compiler_params=params(),
        cost_estimate=cost("mid_back"),
        name="mid_back",
    )(ids, pair, other, residual, cot, gain, *after)


def attend_back_kernel(count, blocks, *refs):
    peers, owns = refs[:count], refs[count : 2 * count]
    q_ref, k_ref, v_ref, p_ref, w_qkv, wo = refs[2 * count : 2 * count + 6]
    sends, (keep, dq_out, dk_out, dv_out, low_ref, part_ref) = refs[2 * count + 6 : -6], refs[-6:]
    i = pl.program_id(0)
    half = blocks // 2
    rows = peers[0].shape[0]

    @pl.when(i == 0)
    def _():
        for n, piece in enumerate((*peers, *owns)):
            low_ref[n * rows : (n + 1) * rows] = piece[...]

    low = low_ref[pl.ds(pl.multiple_of(i * PAIR, PAIR), PAIR), :]
    grad_context = mm(low, wo[...], 1, 1).astype(BF16)
    q, k, v = q_ref[...], k_ref[...], v_ref[...]
    width = q.shape[1]
    head = lax.broadcasted_iota(jnp.int32, (1, width), 1) // HEAD_DIM
    zero = jnp.zeros_like(q)
    dq = dk = dv = jnp.zeros((PAIR, width), F32)
    for h in range(width // HEAD_DIM):
        mine = head == h
        gh = jnp.where(mine, grad_context, zero)
        weights = p_ref[0, h]
        grad_p = mm(gh, v, 1, 1)
        wide = weights.astype(F32)
        dot = jnp.sum(wide * grad_p, axis=-1, keepdims=True)
        grad_s = (wide * (grad_p - dot)).astype(BF16)
        dv = dv + mm(weights, gh, 0, 0)
        dq = dq + mm(grad_s, jnp.where(mine, k, zero), 1, 0)
        dk = dk + mm(grad_s, jnp.where(mine, q, zero), 0, 0)
    scale = HEAD_DIM**-0.5
    dq = (dq * scale).astype(BF16)
    dk = (dk * scale).astype(BF16)
    dv = dv.astype(BF16)
    dq_out[...] = dq
    dk_out[...] = dk
    dv_out[...] = dv
    part = (mm(dq, w_qkv[0], 1, 0) + mm(dk, w_qkv[1], 1, 0) + mm(dv, w_qkv[2], 1, 0)).astype(BF16)
    part_ref[...] = part
    per = PAIR // sends[0].shape[0]
    for n, piece in enumerate(sends):

        @pl.when(i == n // per)
        def _():
            size = piece.shape[0]
            piece[...] = part_ref[(n % per) * size : (n % per + 1) * size]

    @pl.when(i >= half)
    def _():
        keep[...] = part


def attend_back(peers, owns, q, k, v, p, w_qkv, wo, pieces, after):
    rows, local = q.shape
    width = wo.shape[1]
    blocks = rows // PAIR
    half = blocks // 2
    heads = local // HEAD_DIM
    count = len(peers)
    ins = 2 * count + 6
    second = pl.BlockSpec((PAIR, width), lambda i: (jnp.maximum(i - half, 0), 0))
    thin = pl.BlockSpec((PAIR, local), lambda i: (i, 0))
    return pl.pallas_call(
        lambda *refs: attend_back_kernel(count, blocks, *refs[:ins], *refs[ins + len(after) :]),
        grid=(blocks,),
        in_specs=[VM] * (2 * count)
        + [
            thin, thin, thin,
            pl.BlockSpec((1, heads, PAIR, PAIR), lambda i: (i, 0, 0, 0)),
            whole(w_qkv), whole(wo),
        ]
        + [ANY] * len(after),
        out_specs=[VM] * pieces + [second, thin, thin, thin],
        out_shape=[shape((rows // 2 // pieces, width), BF16)] * pieces
        + [shape((rows // 2, width), BF16)]
        + [shape((rows, local), BF16)] * 3,
        scratch_shapes=[pltpu.VMEM((rows, width), BF16), pltpu.VMEM((PAIR, width), BF16)],
        compiler_params=params(),
        cost_estimate=cost("attend_back"),
        name="attend_back",
    )(*peers, *owns, q, k, v, p, w_qkv, wo, *after)


def last_kernel(count, *refs):
    pairs, others = refs[:count], refs[count : 2 * count]
    hidden, grad_residual, gain, low_out, sums, times = refs[2 * count :]
    i = pl.program_id(0)
    pair = jnp.where(i == 0, pairs[0][...], pairs[1][...])
    other = jnp.where(i == 0, others[0][...], others[1][...])
    err = pair.astype(F32) + other.astype(F32)
    unit, scale = norm_stats(hidden[...])
    f = err * row_vector(gain)
    f_mean = jnp.mean(f, axis=-1, keepdims=True)
    fx_mean = jnp.mean(f * unit, axis=-1, keepdims=True)
    grad = grad_residual[...] + scale * (f - f_mean - unit * fx_mean)
    low_out[...] = grad.astype(BF16)

    @pl.when(i == 0)
    def _():
        sums[...] = jnp.zeros_like(sums)

    sums[0:1] += jnp.sum(err * unit, axis=0, keepdims=True)
    sums[1:2] += jnp.sum(err, axis=0, keepdims=True)
    times[0, 0:1] = jnp.sum(grad[:SHORT], axis=0, keepdims=True)
    times[0, 1:2] = jnp.sum(grad[SHORT:], axis=0, keepdims=True)


def last_back(pair, other, hidden, grad_residual, gain, after):
    rows, width = hidden.shape
    half = rows // PAIR
    row = pl.BlockSpec((PAIR, width), lambda i: (i, 0))
    return pl.pallas_call(
        lambda *refs: last_kernel(2, *refs[:7], *refs[7 + len(after) :]),
        grid=(half,),
        in_specs=[VM] * 4 + [row, row, whole(gain)] + [ANY] * len(after),
        out_specs=[
            row,
            pl.BlockSpec((8, width), lambda i: (0, 0)),
            pl.BlockSpec((1, 2, width), lambda i: (i, 0, 0)),
        ],
        out_shape=[shape((rows, width), BF16), shape((8, width), F32), shape((half, 2, width), F32)],
        compiler_params=params(),
        cost_estimate=cost("last_back"),
        name="last_back",
    )(*pair, *other, hidden, grad_residual, gain, *after)


def pack_sums(vec2, vec1, up, times, after):
    pairs, _, width = times.shape

    def kernel(v2, v1, u, t, out):
        out[0:3] = v2[0:3]
        out[3:5] = v1[0:2]
        out[5:6] = u[...]
        out[6:8] = jnp.zeros((2, width), F32)
        for n in range(pairs):
            out[8 + 2 * n : 10 + 2 * n] = t[n]

    return small_call(kernel, [shape((8 + 2 * pairs, width), F32)], [vec2, vec1, up, times], after, "pack_sums")[0]


def join_sums(a, b, after, name):
    rows, width = a.shape
    more = rows - 8

    def kernel(a_ref, b_ref, out):
        out[0:8] = a_ref[0:8] + b_ref[0:8]
        out[8 : 8 + more] = a_ref[8:]
        out[8 + more :] = b_ref[8:]

    return small_call(kernel, [shape((8 + 2 * more, width), F32)], [a, b], after, name)[0]


def table_kernel(slots, steps, ids, own, other, *refs):
    vec_out, (out, table, acc, at_ref) = refs[:6], refs[6:]
    groups = at_ref.shape[0]
    rows, (row_length, row_group, row_step) = row_fields(ids)
    local = table.shape[2]
    half = slots // 2
    for n, vec in enumerate(vec_out):
        row = own[n : n + 1] + (other[n : n + 1] if n < 5 else 0.0)
        vec[...] = row.reshape(row.shape[1])
    for p in range(own.shape[1] // local):

        @pl.when(ids[2] == p)
        def _():
            table[0] = own[8:, p * local : (p + 1) * local]
            table[1] = other[8:, p * local : (p + 1) * local]

    acc[...] = jnp.zeros_like(acc)

    def clear(g, _):
        at_ref[g] = 0
        return 0

    lax.fori_loop(0, groups, clear, 0)

    def place(long):
        def one(r, _):
            @pl.when((row_length(r) > SHORT) == long)
            def _():
                g = row_group(r)
                at = at_ref[g]
                at_ref[g] = at + (2 if long else 1)
                which = (at // half) ^ ids[0]
                base = (g ^ ids[1]) * half + lax.rem(at, half)
                value = table[which, pl.ds(base, 1), :]
                if long:
                    value = value + table[which, pl.ds(base + 1, 1), :]
                step = pl.ds(row_step(r), 1)
                acc[step, :] = acc[step, :] + value

            return 0

        lax.fori_loop(0, rows, one, 0)

    place(True)
    place(False)
    out[...] = jnp.transpose(acc[...])[:, :steps]


def table_grad(scalars, own, other, steps, local, slots, after):
    rows, width = own.shape
    groups = (rows - 8) * 2 // slots
    return pl.pallas_call(
        lambda *refs: table_kernel(slots, steps, *refs[:3], *refs[3 + len(after) :]),
        grid_spec=pltpu.PrefetchScalarGridSpec(
            num_scalar_prefetch=1,
            grid=(1,),
            in_specs=[VM, VM] + [ANY] * len(after),
            out_specs=[pl.BlockSpec((width,), lambda *_: (0,))] * 6 + [pl.BlockSpec((local, steps), lambda *_: (0, 0))],
            scratch_shapes=[
                pltpu.VMEM((2, rows - 8, local), F32),
                pltpu.VMEM((pl.cdiv(steps, 128) * 128, local), F32),
                pltpu.SMEM((groups,), jnp.int32),
            ],
        ),
        out_shape=[pltpu.HBM((width,), F32)] * 6 + [pltpu.HBM((local, steps), F32)],
        compiler_params=params(),
        cost_estimate=cost("table_grad"),
        name="table_grad",
    )(scalars, own, other, *after)


def finish(residuals, pair, other, bias, after):
    rows, width = pair.shape
    part = rows // len(residuals)

    def kernel(*refs):
        res = refs[: len(residuals)]
        pair_ref, other_ref, bias_ref = refs[len(residuals) : len(residuals) + 3]
        out = refs[-1]
        for n, r in enumerate(res):
            at = slice(n * part, (n + 1) * part)
            total = r[...] + (pair_ref[at].astype(F32) + other_ref[at].astype(F32))
            out[at] = (total + row_vector(bias_ref)).astype(BF16)

    return small_call(kernel, [shape((rows, width), BF16)], [*residuals, pair, other, bias], after, "finish")[0]


def order_rows(ids, own, other, after, name):
    part, width = own.shape

    def kernel(ids_ref, own_ref, other_ref, *refs):
        out, sems = refs[len(after) :]
        copies = []
        for n, ref in enumerate((own_ref, other_ref)):
            start = pl.multiple_of((ids_ref[0] ^ n) * part, 16)
            copies.append(pltpu.make_async_copy(ref, out.at[pl.ds(start, part), :], sems.at[n]))
            copies[-1].start()
        for copy in copies:
            copy.wait()

    return pl.pallas_call(
        kernel,
        grid_spec=pltpu.PrefetchScalarGridSpec(
            num_scalar_prefetch=1,
            grid=(1,),
            in_specs=[VM, VM] + [ANY] * len(after),
            out_specs=HB,
            scratch_shapes=[pltpu.SemaphoreType.DMA((2,))],
        ),
        out_shape=pltpu.HBM((2 * part, width), BF16),
        compiler_params=params(),
        cost_estimate=cost(name),
        name=name,
    )(ids, own, other, *after)


def shards(
    tokens, row_length, row_group, row_step, time_table, norm1_gain, norm1_bias, w_qkv, w_out,
    norm2_gain, norm2_bias, w_up, up_bias, w_down, down_bias, cotangent,
):
    count, width = tokens.shape
    n_dp = lax.axis_size("dp")
    dp = lax.axis_index("dp")
    part = lax.axis_index("tensor")
    core = lax.rem(part, 2)
    direct = n_dp == 8
    low_bit, top_bit = dp & 1, (dp >> 2) & 1
    mid_bit = ((dp >> 1) & 1) ^ top_bit
    if direct:
        orders = [low_bit, 2 * mid_bit + top_bit, mid_bit, 2 * low_bit + top_bit]
    else:
        orders = [1, 0, 1, 0]
    own = jnp.stack([core, dp, part, *[jnp.int32(o) for o in orders], jnp.int32(0)]).astype(jnp.int32)
    ids = jnp.concatenate([own, row_length, row_group, row_step])
    scalars = ids
    order_a, order_b = 3, 5
    bits = ((1, 2, 6), (2, 1, 6))
    local = w_out.shape[0]
    slots = count // SHORT
    heads = jnp.transpose(w_qkv, (1, 2, 0))
    far = lambda x: pltpu.with_memory_space_constraint(x, pltpu.HBM)
    size = count // 2
    peer_rows = lambda ids: 1 - ids[0]
    own_rows = lambda ids: ids[0]
    zero = lambda ids: 0
    one = lambda ids: 1

    send, keep, hidden, normed, q, k, v, p, ctx = attend(
        0, 1, scalars, *[far(x) for x in (tokens, time_table, norm1_gain, norm1_bias, heads, w_out)], []
    )
    pair = add_two(keep, core_swap(send), [], "pair_one")
    other = chip_swap(pair)
    w_up, w_down, cotangent = stage([far(x) for x in (w_up, w_down, cotangent)], [pair])
    grad_act = act_grad(cotangent, w_down)
    residual, own2 = mid_forward(hidden, pair, other, norm2_gain, norm2_bias, [grad_act])
    peer2 = core_swap(own2)
    send, keep, act, low, up_sum = expand(0, 1, ids, peer2, own2, grad_act, w_up, up_bias, [])
    got_two = core_swap(send)
    first_keep = keep
    cots = [(cotangent, size, f) for f in (peer_rows, own_rows)]
    acts = [(act, size, f) for f in (zero, one)]
    lows = [(low, size, f) for f in (zero, one)]
    norms = [(peer2, size, zero), (own2, size, zero)]
    mlp = Dual(bits, direct)
    heads_sum = Dual(bits, direct)
    it = types.SimpleNamespace(attn=[])
    placed = [None, None]

    def down_grad(after):
        halves = weight_grad(ids, order_a, [list(zip(acts, cots))], after, "down_grad")
        mlp.begin(0, halves)
        return halves[1]

    def up_grad(after):
        halves = weight_grad(ids, order_b, [list(zip(norms, lows))], after, "up_grad")
        mlp.begin(1, halves)
        return halves[1]

    def pair_two(after):
        it.pair2 = add_two(first_keep, got_two, after, "pair_two")
        it.other2 = chip_swap(it.pair2)
        return it.pair2

    def contract(after):
        send, it.keep_e = contract_rows(act, w_down, after)
        it.got_e = core_swap(send)
        return it.keep_e

    def mid(after):
        it.grad_res, *it.low_own, it.vec2 = mid_back(
            0, 1, ids, it.pair2, it.other2, residual, cotangent, norm2_gain, LOW_PIECES, after
        )
        it.low_peer = [core_swap(x) for x in it.low_own]
        return it.low_own[0]

    def attend_grad(after):
        *send, it.keep3, it.dq, it.dk, it.dv = attend_back(
            it.low_peer, it.low_own, q, k, v, p, heads, w_out, PART_PIECES, after
        )
        it.got3 = [core_swap(x) for x in send]
        return it.keep3

    def qk_grad(after):
        halves = head_grad(ids, order_a, (it.dq, [normed]), (it.dk, [normed]), after, "qk_grad")
        heads_sum.begin(0, halves)
        return halves[1]

    def vo_grad(after):
        lows = [*it.low_peer, *it.low_own]
        halves = head_grad(ids, order_b, (it.dv, [normed]), (ctx, lows), after, "vo_grad")
        heads_sum.begin(1, halves)
        return halves[1]

    def pair_three(after):
        it.pair3 = add_pieces(it.keep3, it.got3, 2, after, "pair_three")
        it.other3 = [chip_swap(x) for x in it.pair3]
        return it.pair3[0]

    def pair_out(after):
        it.pair_e = add_two(it.keep_e, it.got_e, after, "pair_out")
        it.other_e = chip_swap(it.pair_e)
        return it.pair_e

    def last(after):
        it.low_in, it.vec1, it.times = last_back(
            it.pair3, it.other3, hidden, it.grad_res, norm1_gain, after
        )
        it.low_got = core_swap(it.low_in)
        return it.low_in

    def pack(after):
        it.sums = pack_sums(it.vec2, it.vec1, up_sum, it.times, after)
        it.sums_got = dp_swap(it.sums, 1)
        return it.sums

    def join(level):
        def run(after):
            bit = 2 << level
            sums = join_sums(it.sums, it.sums_got, after, "join_sums")
            while level == 2 and bit < n_dp:
                sums = join_sums(sums, dp_swap(sums, bit), [], "join_sums")
                bit *= 2
            it.sums = sums
            if level < 2:
                it.sums_got = dp_swap(sums, bit)
            else:
                it.sums_peer = core_swap(sums)
            return sums

        return run

    def input_rows(after):
        it.input_grad = order_rows(ids, it.low_in, it.low_got, after, "order_input")
        return far(it.input_grad)

    def final(after):
        it.final = finish([residual], it.pair_e, it.other_e, down_bias, after)
        it.final_got = core_swap(it.final)
        return it.final

    def output_rows(after):
        it.block_output = order_rows(ids, it.final, it.final_got, after, "order_output")
        return far(it.block_output)

    def table(after):
        *it.vec, it.time_grad = table_grad(
            scalars, it.sums, it.sums_peer, time_table.shape[0], local, slots, after
        )
        return far(it.vec[0])

    def place(which, half):
        def run(after):
            order, value = (order_a, order_b)[which], mlp.collect(which)[half]
            placed[which] = place_half(ids, order, value, half, placed[which], after, ("place_down", "place_up")[which])
            return far(placed[which])

        return run

    def place_attn(half):
        def run(after):
            a, b = heads_sum.collect(0)[half], heads_sum.collect(1)[half]
            it.attn = place_heads(ids, (order_a, order_b), a, b, half, it.attn, after, "place_heads")
            return far(it.attn[1])

        return run

    def sum_step(group):
        return lambda after: group.step(after[0])

    order = (
        down_grad, pair_two, up_grad, contract, mid, sum_step(mlp), attend_grad, sum_step(mlp), vo_grad,
        pair_out, pair_three, qk_grad, sum_step(heads_sum), last, sum_step(heads_sum), pack, sum_step(mlp),
        sum_step(heads_sum), join(0), join(1), sum_step(mlp), sum_step(heads_sum), place_attn(0), join(2),
        final, place(0, 0), place(1, 0), input_rows, output_rows, table, place(1, 1), place(0, 1),
        place_attn(1),
    )
    mark = first_keep
    for step in order:
        mark = step([mark])
    vec, time_grad = it.vec, it.time_grad
    block_output, input_grad = it.block_output, it.input_grad
    down_out, up_out = placed
    qkv_out, proj_out = it.attn

    return (
        block_output,
        input_grad,
        time_grad.T,
        vec[3],
        vec[4],
        jnp.transpose(qkv_out, (2, 0, 1)),
        proj_out,
        vec[0],
        vec[1],
        up_out,
        vec[5],
        down_out,
        vec[2],
    )


def solution(mesh):
    in_specs = (
        P("dp", None), P(), P(), P(), P(), P(), P(), P(None, None, "tensor"), P("tensor", None), P(), P(),
        P(None, "tensor"), P("tensor"), P("tensor", None), P(), P("dp", None),
    )
    out_specs = (
        P("dp", None), P("dp", None), P(None, "tensor"), P(), P(), P(None, None, "tensor"), P("tensor", None),
        P(), P(), P(None, "tensor"), P("tensor"), P("tensor", None), P(),
    )
    return jax.shard_map(shards, mesh=mesh, in_specs=in_specs, out_specs=out_specs, check_vma=False)
```

```python
import functools
import types

import jax
import jax.numpy as jnp
from jax import lax
from jax.experimental import pallas as pl
from jax.experimental.pallas import tpu as pltpu
from jax.sharding import PartitionSpec as P

HEAD_DIM = 64
SHORT = 128
PAIR = 256
EPS = 1e-05
NEG = -1000000000.0
SQRT_HALF = 0.7071067811865476
PHI_ZERO = 0.3989422804014327
VMEM_MB = 16
LOW_PIECES = 2
PART_PIECES = 4

SMALL_MB = 8

F32 = jnp.float32
BF16 = jnp.bfloat16


def mm(left, right, left_dim, right_dim):
    return lax.dot_general(
        left, right, (((left_dim,), (right_dim,)), ((), ())), preferred_element_type=F32
    )


def params(dims=1):
    return pltpu.CompilerParams(
        dimension_semantics=("arbitrary",) * dims, vmem_limit_bytes=VMEM_MB << 20
    )


COSTS = {"finish": 0.5, "up_grad": 1}


def cost(name):
    return pl.CostEstimate(flops=int(COSTS.get(name, 0) * 1e9), bytes_accessed=1, transcendentals=0)


def shape(dims, dtype):
    return jax.ShapeDtypeStruct(dims, dtype)


def whole(array):
    zeros = (0,) * array.ndim
    return pl.BlockSpec(array.shape, lambda *_: zeros)


def swap(value, axis, bit):
    return lax.ppermute(value, axis, [(i, i ^ bit) for i in range(lax.axis_size(axis))])


def core_swap(value):
    return swap(value, "tensor", 1)


def chip_swap(value):
    return swap(value, "tensor", 2)


def dp_swap(value, bit):
    return swap(value, "dp", bit)


def norm_stats(values):
    mean = jnp.mean(values, axis=-1, keepdims=True)
    centred = values - mean
    variance = jnp.mean(centred * centred, axis=-1, keepdims=True)
    scale = lax.rsqrt(variance + EPS)
    return centred * scale, scale


IDS = 8


def row_fields(info):
    rows = (info.shape[0] - IDS) // 3
    return rows, [lambda r, at=at: info[IDS + at * rows + r] for at in range(3)]


def fill_slots(slot_ref, info):
    group = info[1]
    rows, (row_length, row_group, row_step) = row_fields(info)

    def long_row(r, pos):
        step = row_step(r)
        slot_ref[pos] = step
        slot_ref[pos + 1] = step
        hit = (row_group(r) == group) & (row_length(r) > SHORT)
        return pos + jnp.where(hit, 2, 0)

    def short_row(r, pos):
        slot_ref[pos] = row_step(r)
        hit = (row_group(r) == group) & (row_length(r) <= SHORT)
        return pos + jnp.where(hit, 1, 0)

    long_slots = lax.fori_loop(0, rows, long_row, 0)
    lax.fori_loop(0, rows, short_row, long_slots)
    return long_slots


def block_of(i, ids, chunk, half, chunks):
    side = jnp.where(i < half, 1 - ids[0], ids[0])
    return side * (half * chunks) + chunk * half + lax.rem(i, half)


def add_low(a, b):
    return (a.astype(F32) + b.astype(F32)).astype(BF16)


def row_vector(ref):
    return ref[...].reshape(1, ref.shape[0])


VM = pl.BlockSpec(memory_space=pltpu.VMEM)
ANY = pl.BlockSpec(memory_space=pl.ANY)


def small_call(kernel, out_shape, operands, after, name):
    count = len(operands)
    return pl.pallas_call(
        lambda *refs: kernel(*refs[:count], *refs[count + len(after) :]),
        in_specs=[VM] * count + [ANY] * len(after),
        out_specs=[VM] * len(out_shape),
        out_shape=out_shape,
        compiler_params=pltpu.CompilerParams(vmem_limit_bytes=SMALL_MB << 20),
        cost_estimate=cost(name),
        name=name,
    )(*operands, *after)


def stage(arrays, after):
    count = len(arrays)

    def kernel(*refs):
        out, sems = refs[count + len(after) : -1], refs[-1]
        copies = [pltpu.make_async_copy(refs[n], out[n], sems.at[n]) for n in range(count)]
        for copy in copies:
            copy.start()
        for copy in copies:
            copy.wait()

    return pl.pallas_call(
        kernel,
        in_specs=[pl.BlockSpec(memory_space=pltpu.HBM)] * count + [ANY] * len(after),
        out_specs=[VM] * count,
        out_shape=[pltpu.VMEM(a.shape, a.dtype) for a in arrays],
        scratch_shapes=[pltpu.SemaphoreType.DMA((count,))],
        compiler_params=pltpu.CompilerParams(vmem_limit_bytes=SMALL_MB << 20),
        cost_estimate=cost("stage"),
        name="stage",
    )(*arrays, *after)


def add_two(a, b, after, name):
    def kernel(a_ref, b_ref, out):
        out[...] = add_low(a_ref[...], b_ref[...])

    return small_call(kernel, [shape(a.shape, BF16)], [a, b], after, name)[0]


def attend_kernel(
    chunk, half, chunks, slots, ids,
    tokens, table, gain, bias, w_qkv, wo,
    send, keep, hidden_out, normed_out, q_out, k_out, v_out, p_out, c_out,
    slot_ref, rows_ref, sems,
):
    i = pl.program_id(0)

    def fetch(s):
        step = slot_ref[s]
        start = pl.multiple_of((step // 8) * 8, 8)
        return pltpu.make_async_copy(table.at[pl.ds(start, 8), :], rows_ref.at[s], sems.at[s])

    @pl.when(i == 0)
    def _():
        slot_ref[slots + 2] = fill_slots(slot_ref, ids)
        for s in range(slots):
            fetch(s).start()
        for s in range(slots):
            fetch(s).wait()

    block = block_of(i, ids, chunk, half, chunks)
    sub = lax.broadcasted_iota(jnp.int32, (8, 1), 0)

    def row_of(s):
        picked = sub == lax.rem(slot_ref[s], 8)
        return jnp.sum(jnp.where(picked, rows_ref[s].astype(F32), 0.0), axis=0, keepdims=True)

    low_half = lax.broadcasted_iota(jnp.int32, (PAIR, 1), 0) < SHORT
    step_row = jnp.where(low_half, row_of(2 * block), row_of(2 * block + 1))
    hidden = tokens[...].astype(F32) + step_row
    unit, _ = norm_stats(hidden)
    normed = (unit * row_vector(gain) + row_vector(bias)).astype(BF16)
    normed_out[...] = normed
    q = mm(normed, w_qkv[0], 1, 1).astype(BF16)
    k = mm(normed, w_qkv[1], 1, 1).astype(BF16)
    v = mm(normed, w_qkv[2], 1, 1).astype(BF16)
    q_out[...] = q
    k_out[...] = k
    v_out[...] = v
    split = (2 * block >= slot_ref[slots + 2]).astype(jnp.int32)
    row_half = lax.broadcasted_iota(jnp.int32, (PAIR, PAIR), 0) // SHORT
    col_half = lax.broadcasted_iota(jnp.int32, (PAIR, PAIR), 1) // SHORT
    allowed = ((row_half ^ col_half) * split) == 0
    width = q.shape[1]
    head = lax.broadcasted_iota(jnp.int32, (1, width), 1) // HEAD_DIM
    context = jnp.zeros((PAIR, width), F32)
    for h in range(width // HEAD_DIM):
        mine = head == h
        qh = jnp.where(mine, q, jnp.zeros_like(q))
        scores = mm(qh, k, 1, 1) * (HEAD_DIM**-0.5)
        scores = jnp.where(allowed, scores, NEG)
        top = jnp.max(scores, axis=-1, keepdims=True)
        powers = jnp.exp(scores - top)
        total = jnp.sum(powers, axis=-1, keepdims=True)
        weights = (powers * (1.0 / total)).astype(BF16)
        p_out[0, h] = weights
        context = context + mm(weights, jnp.where(mine, v, jnp.zeros_like(v)), 1, 0)
    low = context.astype(BF16)
    c_out[...] = low
    part = mm(low, wo[...], 1, 0).astype(BF16)

    @pl.when(i < half)
    def _():
        send[...] = part

    @pl.when(i >= half)
    def _():
        keep[...] = part
        hidden_out[...] = hidden


def attend(chunk, chunks, scalars, tokens, table, gain, bias, w_qkv, wo, after):
    count, width = tokens.shape
    local = wo.shape[0]
    blocks = count // PAIR // chunks
    half = blocks // 2
    rows = blocks * PAIR
    slots = count // SHORT
    own = rows // 2
    heads = local // HEAD_DIM
    first = lambda i, *_: (jnp.minimum(i, half - 1), 0)
    second = lambda i, *_: (jnp.maximum(i - half, 0), 0)
    step = lambda i, *_: (i, 0)
    row = pl.BlockSpec((PAIR, width), step)
    thin = pl.BlockSpec((PAIR, local), step)
    return pl.pallas_call(
        lambda *refs: attend_kernel(chunk, half, chunks, slots, *refs[:7], *refs[7 + len(after) :]),
        grid_spec=pltpu.PrefetchScalarGridSpec(
            num_scalar_prefetch=1,
            grid=(blocks,),
            in_specs=[
                pl.BlockSpec((PAIR, width), lambda i, ids, *_: (block_of(i, ids, chunk, half, chunks), 0)),
                pl.BlockSpec(memory_space=pltpu.HBM),
                whole(gain), whole(bias), whole(w_qkv), whole(wo),
            ]
            + [ANY] * len(after),
            out_specs=[
                pl.BlockSpec((PAIR, width), first),
                pl.BlockSpec((PAIR, width), second),
                pl.BlockSpec((PAIR, width), second),
                row, thin, thin, thin,
                pl.BlockSpec((1, heads, PAIR, PAIR), lambda i, *_: (i, 0, 0, 0)),
                thin,
            ],
            scratch_shapes=[
                pltpu.SMEM((slots + 4,), jnp.int32),
                pltpu.VMEM((slots, 8, width), BF16),
                pltpu.SemaphoreType.DMA((slots,)),
            ],
        ),
        out_shape=[
            shape((own, width), BF16), shape((own, width), BF16), shape((own, width), F32),
            shape((rows, width), BF16),
            shape((rows, local), BF16), shape((rows, local), BF16), shape((rows, local), BF16),
            shape((blocks, heads, PAIR, PAIR), BF16),
            shape((rows, local), BF16),
        ],
        compiler_params=params(),
        cost_estimate=cost("attend"),
        name="attend",
    )(scalars, tokens, table, gain, bias, w_qkv, wo, *after)


def mid_kernel(hidden, pair, other, gain, bias, residual_out, normed_out):
    residual = hidden[...] + (pair[...].astype(F32) + other[...].astype(F32))
    residual_out[...] = residual
    unit, _ = norm_stats(residual)
    normed_out[...] = (unit * row_vector(gain) + row_vector(bias)).astype(BF16)


def mid_forward(hidden, pair, other, gain, bias, after):
    rows, width = hidden.shape
    row = pl.BlockSpec((PAIR, width), lambda i: (i, 0))
    return pl.pallas_call(
        lambda *refs: mid_kernel(*refs[:5], *refs[5 + len(after) :]),
        grid=(rows // PAIR,),
        in_specs=[row, row, row, whole(gain), whole(bias)] + [ANY] * len(after),
        out_specs=[row, row],
        out_shape=[shape((rows, width), F32), shape((rows, width), BF16)],
        compiler_params=params(),
        cost_estimate=cost("mid_forward"),
        name="mid_forward",
    )(hidden, pair, other, gain, bias, *after)


def act_grad(cot, w_down):
    rows, width = cot.shape
    local = w_down.shape[0]

    def kernel(cot_ref, w_ref, out):
        out[...] = mm(cot_ref[...], w_ref[...], 1, 1)

    return pl.pallas_call(
        kernel,
        grid=(rows // PAIR,),
        in_specs=[pl.BlockSpec((PAIR, width), lambda i: (i, 0)), VM],
        out_specs=pl.BlockSpec((PAIR, local), lambda i: (i, 0)),
        out_shape=shape((rows, local), F32),
        compiler_params=params(),
        cost_estimate=cost("act_grad"),
        name="act_grad",
    )(cot, w_down)


def expand_kernel(ids, normed, grad_act, w_up, up_bias, part_out, act_out, low_out, bias_out):
    pre = mm(normed[...], w_up[...], 1, 0) + row_vector(up_bias)
    cdf = 0.5 * (1.0 + lax.erf(pre * SQRT_HALF))
    act_out[...] = (pre * cdf).astype(BF16)
    slope = cdf + pre * (PHI_ZERO * jnp.exp(-0.5 * (pre * pre)))
    grad_pre = grad_act[...] * slope

    @pl.when(pl.program_id(0) == 0)
    def _():
        bias_out[...] = jnp.zeros_like(bias_out)

    bias_out[...] += jnp.sum(grad_pre, axis=0, keepdims=True)
    low = grad_pre.astype(BF16)
    low_out[...] = low
    part_out[...] = mm(low, w_up[...], 1, 1).astype(BF16)


def expand(ids, own, normed, grad_act, w_up, up_bias, after):
    rows, width = normed.shape
    local = w_up.shape[1]
    blocks = rows // PAIR
    side = 0 if own else 1
    row = pl.BlockSpec((PAIR, width), lambda i, *_: (i, 0))
    thin = pl.BlockSpec((PAIR, local), lambda i, *_: (i, 0))
    return pl.pallas_call(
        lambda *refs: expand_kernel(*refs[:5], *refs[5 + len(after) :]),
        grid_spec=pltpu.PrefetchScalarGridSpec(
            num_scalar_prefetch=1,
            grid=(blocks,),
            in_specs=[
                row,
                pl.BlockSpec((PAIR, local), lambda i, ids: ((ids[0] ^ side) * blocks + i, 0)),
                VM, whole(up_bias),
            ]
            + [ANY] * len(after),
            out_specs=[row, thin, thin, pl.BlockSpec((1, local), lambda i, *_: (0, 0))],
        ),
        out_shape=[
            shape((rows, width), BF16), shape((rows, local), BF16), shape((rows, local), BF16),
            shape((1, local), F32),
        ],
        compiler_params=params(),
        cost_estimate=cost("expand"),
        name="expand",
    )(ids, normed, grad_act, w_up, up_bias, *after)


def contract_kernel(a, b, w_down, send, keep):
    i = pl.program_id(0)
    act = jnp.where(i < 2, a[...], b[...])
    part = mm(act, w_down[...], 1, 0).astype(BF16)

    @pl.when(i < 2)
    def _():
        send[...] = part

    @pl.when(i >= 2)
    def _():
        keep[...] = part


def contract_rows(peer, own, w_down, after):
    rows, local = peer.shape
    width = w_down.shape[1]
    first = lambda i: (jnp.minimum(i, 1), 0)
    second = lambda i: (jnp.maximum(i - 2, 0), 0)
    return pl.pallas_call(
        lambda *refs: contract_kernel(*refs[:3], *refs[3 + len(after) :]),
        grid=(2 * rows // PAIR,),
        in_specs=[pl.BlockSpec((PAIR, local), first), pl.BlockSpec((PAIR, local), second), VM] + [ANY] * len(after),
        out_specs=[pl.BlockSpec((PAIR, width), first), pl.BlockSpec((PAIR, width), second)],
        out_shape=[shape((rows, width), BF16), shape((rows, width), BF16)],
        compiler_params=params(),
        cost_estimate=cost("contract_rows"),
        name="contract_rows",
    )(peer, own, w_down, *after)


def weight_kernel(order, groups, ids, *refs):
    count = sum(len(lefts) for lefts in groups)
    left, right = refs[:count], refs[count : 2 * count]
    send, keep, scratch = refs[2 * count : 2 * count + 3]
    i = pl.program_id(0)
    many = len(groups) > 1
    rows = send.shape[-2]
    at = 0
    for n, sizes in enumerate(groups):
        total = mm(left[at][...], right[at][...], 0, 0)
        for j in range(at + 1, at + len(sizes)):
            total = total + mm(left[j][...], right[j][...], 0, 0)
        at += len(sizes)
        scratch[n] = total

    def write(out):
        for r in range(4):
            start = pl.multiple_of((ids[order + 1] ^ r) * rows, 8)
            for n in range(len(groups)):
                value = scratch[n, pl.ds(start, rows), :].astype(BF16)
                if many:
                    out[r, n] = value
                else:
                    out[r] = value

    @pl.when(i == 0)
    def _():
        write(send)

    @pl.when(i == 1)
    def _():
        write(keep)


def weight_grad(ids, order, groups, after, name):
    rows_out = groups[0][0][0][0].shape[1]
    tile = rows_out // 2
    part = tile // 4
    cols = groups[0][0][1][0].shape[1]
    lefts = [left for pieces in groups for left, _ in pieces]
    rights = [right for pieces in groups for _, right in pieces]
    count = sum(size for _, size, _ in lefts)

    def column(i, ids):
        return jnp.where(i == 0, 1 - ids[order], ids[order])

    specs = [pl.BlockSpec((size, tile), lambda i, ids, at=at: (at(ids), column(i, ids))) for _, size, at in lefts]
    specs += [pl.BlockSpec((size, cols), lambda i, ids, at=at: (at(ids), 0)) for _, size, at in rights]
    dims = (4, part, cols) if len(groups) == 1 else (4, len(groups), part, cols)
    out = pl.BlockSpec(dims, lambda i, ids: (0,) * len(dims))
    kernel = functools.partial(weight_kernel, order, [[size for (_, size, _), _ in g] for g in groups])
    total = len(lefts)
    return list(pl.pallas_call(
        lambda ids, *refs: kernel(ids, *refs[: 2 * total], *refs[2 * total + len(after) :]),
        grid_spec=pltpu.PrefetchScalarGridSpec(
            num_scalar_prefetch=1,
            grid=(2,),
            in_specs=specs + [ANY] * len(after),
            out_specs=[out, out],
            scratch_shapes=[pltpu.VMEM((len(groups), tile, cols), F32)],
        ),
        out_shape=[shape(dims, BF16), shape(dims, BF16)],
        compiler_params=params(),
        cost_estimate=cost(name),
        name=name,
    )(ids, *[a for a, _, _ in lefts], *[b for b, _, _ in rights], *after))


def head_grad(ids, order, first, second, after, name):
    rows_out, cols = first[0].shape[1], first[1][0].shape[1]
    part = rows_out // 8
    flat = [first[0], *first[1], second[0], *second[1]]

    def kernel(ids_ref, *refs):
        values = refs[: len(flat)]
        send, keep, scratch = refs[len(flat) + len(after) :]
        at = 0
        for n, (_, pieces) in enumerate((first, second)):
            rights = [values[at + 1 + j][...] for j in range(len(pieces))]
            right = rights[0] if len(rights) == 1 else jnp.concatenate(rights, axis=0)
            scratch[n] = mm(values[at][...], right, 0, 0)
            at += 1 + len(pieces)
        for half, out in ((1 - ids_ref[order], send), (ids_ref[order], keep)):
            for r in range(4):
                start = pl.multiple_of((half * 4 + (ids_ref[order + 1] ^ r)) * part, 8)
                for n in range(2):
                    out[r, n] = scratch[n, pl.ds(start, part), :].astype(BF16)

    dims = (4, 2, part, cols)
    return pl.pallas_call(
        kernel,
        grid_spec=pltpu.PrefetchScalarGridSpec(
            num_scalar_prefetch=1,
            grid=(1,),
            in_specs=[VM] * len(flat) + [ANY] * len(after),
            out_specs=[VM, VM],
            scratch_shapes=[pltpu.VMEM((2, rows_out, cols), F32)],
        ),
        out_shape=[shape(dims, BF16), shape(dims, BF16)],
        compiler_params=params(),
        cost_estimate=cost(name),
        name=name,
    )(ids, *flat, *after)


def add_pieces(a, b, pieces, after, name):
    rows, width = a.shape
    size, out_size = rows // len(b), rows // pieces
    step = min(size, out_size)

    def kernel(a_ref, *refs):
        given, out = refs[: len(b)], refs[len(b) :]
        for at in range(0, rows, step):
            got = given[at // size][at % size : at % size + step]
            out[at // out_size][at % out_size : at % out_size + step] = add_low(a_ref[at : at + step], got)

    return list(small_call(kernel, [shape((out_size, width), BF16)] * pieces, [a, *b], after, name))


class Dual:
    def __init__(self, bits, direct):
        self.bits, self.direct, self.level = bits, direct, 0
        self.summed = [None, None]
        self.halves, self.got = [None, None], [None, None]

    def begin(self, which, halves):
        self.halves[which] = list(halves)
        if self.direct:
            self.got[which] = dp_swap(halves[0], self.bits[which][0])

    def step(self, after):
        if not self.direct:
            return after
        (_, keep_a), (_, keep_b) = self.halves
        level, name = self.level, "exchange"
        self.level += 1
        first, second = self.bits
        if level < 2:
            parts, rest = keep_a.shape[0], keep_a.shape[1:]
            half = parts // 2
            if level == 0:

                def kernel(ka, ga, kb, gb, sa, oa, sb, ob):
                    for k, g, send, out in ((ka, ga, sa, oa), (kb, gb, sb, ob)):
                        send[...] = add_low(k[half:], g[half:])
                        out[...] = add_low(k[:half], g[:half])

                out = [shape((half, *rest), BF16)] * 4
                sa, oa, sb, ob = small_call(kernel, out, [keep_a, self.got[0], keep_b, self.got[1]], [after], name)
                self.halves = [[sa, oa], [sb, ob]]
                self.got = [dp_swap(sa, first[1]), dp_swap(sb, second[1])]
                return oa

            def kernel(ka, ga, kb, gb, out):
                for n, (k, g) in enumerate(((ka, ga), (kb, gb))):
                    out[n] = add_low(k[...], g[...])

            out = [shape((2, parts, *rest), BF16)]
            both = small_call(kernel, out, [keep_a, self.got[0], keep_b, self.got[1]], [after], name)[0]
            self.halves = [[None, both], [None, both]]
            self.got = [dp_swap(both, first[2]), None]
            return both
        if level == 2:

            def kernel(k, g, oa, ob):
                for n, out in enumerate((oa, ob)):
                    for j in range(2):
                        out[j] = add_low(k[n, j], g[n, 1 - j])

            out = [shape(keep_a.shape[1:], BF16)] * 2
            oa, ob = small_call(kernel, out, [keep_a, self.got[0]], [after], name)
            self.halves = [[None, oa], [None, ob]]
            self.got = [dp_swap(oa, first[1]), dp_swap(ob, second[1])]
            return oa
        rest = keep_a.shape[1:]

        def kernel(ka, ga, kb, gb, oa, ob):
            for k, g, out in ((ka, ga, oa), (kb, gb, ob)):
                out[:2] = k[...]
                out[2:] = g[...]

        out = [shape((4, *rest), BF16)] * 2
        oa, ob = small_call(kernel, out, [keep_a, self.got[0], keep_b, self.got[1]], [after], name)
        self.halves = [[None, oa], [None, ob]]
        self.got = [dp_swap(oa, first[0]), dp_swap(ob, second[0])]
        return oa

    def collect(self, which):
        if not self.direct:
            if self.summed[which] is None:
                send, keep = lax.psum(tuple(self.halves[which]), "dp")
                self.summed[which] = keep, send
            return self.summed[which]
        return self.halves[which][1], self.got[which]


HB = pl.BlockSpec(memory_space=pltpu.HBM)


def place_half(ids, order, value, flip, base, after, name):
    _, part, cols = value.shape
    given = [] if base is None else [pltpu.with_memory_space_constraint(base, pltpu.HBM)]

    def kernel(ids_ref, value_ref, *refs):
        out, wide, sems = refs[-3:]
        copies = []
        for r in range(4):
            start = ((ids_ref[order] ^ flip) * 4 + (ids_ref[order + 1] ^ r)) * part
            wide[r] = value_ref[r].astype(F32)
            rows = out.at[pl.ds(pl.multiple_of(start, 8), part), :]
            copies.append(pltpu.make_async_copy(wide.at[r], rows, sems.at[r]))
            copies[-1].start()
        for copy in copies:
            copy.wait()

    return pl.pallas_call(
        kernel,
        grid_spec=pltpu.PrefetchScalarGridSpec(
            num_scalar_prefetch=1,
            grid=(1,),
            in_specs=[VM] + [HB] * len(given) + [ANY] * len(after),
            out_specs=HB,
            scratch_shapes=[pltpu.VMEM((4, part, cols), F32), pltpu.SemaphoreType.DMA((4,))],
        ),
        out_shape=pltpu.HBM((8 * part, cols), F32),
        input_output_aliases={2: 0} if given else {},
        compiler_params=params(),
        cost_estimate=cost(name),
        name=name,
    )(ids, value, *given, *after)


def place_heads(ids, orders, a, b, flip, bases, after, name):
    _, _, part, cols = a.shape
    rows = 8 * part
    given = [pltpu.with_memory_space_constraint(x, pltpu.HBM) for x in bases]

    def kernel(ids_ref, a_ref, b_ref, *refs):
        qkv_out, proj_out, wide, sems = refs[-4:]
        copies = []
        for n, (pick, order) in enumerate(((a_ref, orders[0]), (b_ref, orders[1]))):
            for r in range(4):
                at = (ids_ref[order] ^ flip) * 4 + (ids_ref[order + 1] ^ r)
                at = pl.ds(pl.multiple_of(at * part, 8), part)
                for j in range(2):
                    k = len(copies)
                    wide[k] = pick[r, j].astype(F32)
                    out = proj_out.at[at, :] if n + j == 2 else qkv_out.at[2 * n + j, at, :]
                    copies.append(pltpu.make_async_copy(wide.at[k], out, sems.at[k]))
                    copies[-1].start()
        for copy in copies:
            copy.wait()

    return list(
        pl.pallas_call(
            kernel,
            grid_spec=pltpu.PrefetchScalarGridSpec(
                num_scalar_prefetch=1,
                grid=(1,),
                in_specs=[VM, VM] + [HB] * len(given) + [ANY] * len(after),
                out_specs=[HB, HB],
                scratch_shapes=[pltpu.VMEM((16, part, cols), F32), pltpu.SemaphoreType.DMA((16,))],
            ),
            out_shape=[pltpu.HBM((3, rows, cols), F32), pltpu.HBM((rows, cols), F32)],
            input_output_aliases={3: 0, 4: 1} if given else {},
            compiler_params=params(),
            cost_estimate=cost(name),
            name=name,
        )(ids, a, b, *given, *after)
    )


def mid_back_kernel(pair, other, residual, cot, gain, grad_out, *refs):
    low_out, sums = refs[:-1], refs[-1]
    i = pl.program_id(0)
    err = pair[...].astype(F32) + other[...].astype(F32)
    unit, scale = norm_stats(residual[...])
    top = cot[...].astype(F32)
    f = err * row_vector(gain)
    f_mean = jnp.mean(f, axis=-1, keepdims=True)
    fx_mean = jnp.mean(f * unit, axis=-1, keepdims=True)
    grad = top + scale * (f - f_mean - unit * fx_mean)
    grad_out[...] = grad
    low = grad.astype(BF16)
    per = PAIR // low_out[0].shape[0]
    for n, piece in enumerate(low_out):

        @pl.when(i == n // per)
        def _():
            rows = piece.shape[0]
            piece[...] = low[(n % per) * rows : (n % per + 1) * rows]

    @pl.when(i == 0)
    def _():
        sums[...] = jnp.zeros_like(sums)

    sums[0:1] += jnp.sum(err * unit, axis=0, keepdims=True)
    sums[1:2] += jnp.sum(err, axis=0, keepdims=True)
    sums[2:3] += jnp.sum(top, axis=0, keepdims=True)


def mid_back(chunk, chunks, ids, pair, other, residual, cot, gain, pieces, after):
    rows, width = residual.shape
    half = rows // PAIR
    row = pl.BlockSpec((PAIR, width), lambda i, ids: (i, 0))
    return pl.pallas_call(
        lambda ids, *refs: mid_back_kernel(*refs[:5], *refs[5 + len(after) :]),
        grid_spec=pltpu.PrefetchScalarGridSpec(
            num_scalar_prefetch=1,
            grid=(half,),
            in_specs=[
                row, row, row,
                pl.BlockSpec((PAIR, width), lambda i, ids: (block_of(i + half, ids, chunk, half, chunks), 0)),
                whole(gain),
            ]
            + [ANY] * len(after),
            out_specs=[row] + [VM] * pieces + [pl.BlockSpec((8, width), lambda i, ids: (0, 0))],
        ),
        out_shape=[shape((rows, width), F32)] + [shape((rows // pieces, width), BF16)] * pieces + [shape((8, width), F32)],
        compiler_params=params(),
        cost_estimate=cost("mid_back"),
        name="mid_back",
    )(ids, pair, other, residual, cot, gain, *after)


def attend_back_kernel(count, blocks, *refs):
    peers, owns = refs[:count], refs[count : 2 * count]
    q_ref, k_ref, v_ref, p_ref, w_qkv, wo = refs[2 * count : 2 * count + 6]
    sends, (keep, dq_out, dk_out, dv_out, low_ref, part_ref) = refs[2 * count + 6 : -6], refs[-6:]
    i = pl.program_id(0)
    half = blocks // 2
    rows = peers[0].shape[0]

    @pl.when(i == 0)
    def _():
        for n, piece in enumerate((*peers, *owns)):
            low_ref[n * rows : (n + 1) * rows] = piece[...]

    low = low_ref[pl.ds(pl.multiple_of(i * PAIR, PAIR), PAIR), :]
    grad_context = mm(low, wo[...], 1, 1).astype(BF16)
    q, k, v = q_ref[...], k_ref[...], v_ref[...]
    width = q.shape[1]
    head = lax.broadcasted_iota(jnp.int32, (1, width), 1) // HEAD_DIM
    zero = jnp.zeros_like(q)
    dq = dk = dv = jnp.zeros((PAIR, width), F32)
    for h in range(width // HEAD_DIM):
        mine = head == h
        gh = jnp.where(mine, grad_context, zero)
        weights = p_ref[0, h]
        grad_p = mm(gh, v, 1, 1)
        wide = weights.astype(F32)
        dot = jnp.sum(wide * grad_p, axis=-1, keepdims=True)
        grad_s = (wide * (grad_p - dot)).astype(BF16)
        dv = dv + mm(weights, gh, 0, 0)
        dq = dq + mm(grad_s, jnp.where(mine, k, zero), 1, 0)
        dk = dk + mm(grad_s, jnp.where(mine, q, zero), 0, 0)
    scale = HEAD_DIM**-0.5
    dq = (dq * scale).astype(BF16)
    dk = (dk * scale).astype(BF16)
    dv = dv.astype(BF16)
    dq_out[...] = dq
    dk_out[...] = dk
    dv_out[...] = dv
    part = (mm(dq, w_qkv[0], 1, 0) + mm(dk, w_qkv[1], 1, 0) + mm(dv, w_qkv[2], 1, 0)).astype(BF16)
    part_ref[...] = part
    per = PAIR // sends[0].shape[0]
    for n, piece in enumerate(sends):

        @pl.when(i == n // per)
        def _():
            size = piece.shape[0]
            piece[...] = part_ref[(n % per) * size : (n % per + 1) * size]

    @pl.when(i >= half)
    def _():
        keep[...] = part


def attend_back(peers, owns, q, k, v, p, w_qkv, wo, pieces, after):
    rows, local = q.shape
    width = wo.shape[1]
    blocks = rows // PAIR
    half = blocks // 2
    heads = local // HEAD_DIM
    count = len(peers)
    ins = 2 * count + 6
    second = pl.BlockSpec((PAIR, width), lambda i: (jnp.maximum(i - half, 0), 0))
    thin = pl.BlockSpec((PAIR, local), lambda i: (i, 0))
    return pl.pallas_call(
        lambda *refs: attend_back_kernel(count, blocks, *refs[:ins], *refs[ins + len(after) :]),
        grid=(blocks,),
        in_specs=[VM] * (2 * count)
        + [
            thin, thin, thin,
            pl.BlockSpec((1, heads, PAIR, PAIR), lambda i: (i, 0, 0, 0)),
            whole(w_qkv), whole(wo),
        ]
        + [ANY] * len(after),
        out_specs=[VM] * pieces + [second, thin, thin, thin],
        out_shape=[shape((rows // 2 // pieces, width), BF16)] * pieces
        + [shape((rows // 2, width), BF16)]
        + [shape((rows, local), BF16)] * 3,
        scratch_shapes=[pltpu.VMEM((rows, width), BF16), pltpu.VMEM((PAIR, width), BF16)],
        compiler_params=params(),
        cost_estimate=cost("attend_back"),
        name="attend_back",
    )(*peers, *owns, q, k, v, p, w_qkv, wo, *after)


def last_kernel(count, *refs):
    pairs, others = refs[:count], refs[count : 2 * count]
    hidden, grad_residual, gain, low_out, sums, times = refs[2 * count :]
    i = pl.program_id(0)
    pair = jnp.where(i == 0, pairs[0][...], pairs[1][...])
    other = jnp.where(i == 0, others[0][...], others[1][...])
    err = pair.astype(F32) + other.astype(F32)
    unit, scale = norm_stats(hidden[...])
    f = err * row_vector(gain)
    f_mean = jnp.mean(f, axis=-1, keepdims=True)
    fx_mean = jnp.mean(f * unit, axis=-1, keepdims=True)
    grad = grad_residual[...] + scale * (f - f_mean - unit * fx_mean)
    low_out[...] = grad.astype(BF16)

    @pl.when(i == 0)
    def _():
        sums[...] = jnp.zeros_like(sums)

    sums[0:1] += jnp.sum(err * unit, axis=0, keepdims=True)
    sums[1:2] += jnp.sum(err, axis=0, keepdims=True)
    times[0, 0:1] = jnp.sum(grad[:SHORT], axis=0, keepdims=True)
    times[0, 1:2] = jnp.sum(grad[SHORT:], axis=0, keepdims=True)


def last_back(pair, other, hidden, grad_residual, gain, after):
    rows, width = hidden.shape
    half = rows // PAIR
    row = pl.BlockSpec((PAIR, width), lambda i: (i, 0))
    return pl.pallas_call(
        lambda *refs: last_kernel(2, *refs[:7], *refs[7 + len(after) :]),
        grid=(half,),
        in_specs=[VM] * 4 + [row, row, whole(gain)] + [ANY] * len(after),
        out_specs=[
            row,
            pl.BlockSpec((8, width), lambda i: (0, 0)),
            pl.BlockSpec((1, 2, width), lambda i: (i, 0, 0)),
        ],
        out_shape=[shape((rows, width), BF16), shape((8, width), F32), shape((half, 2, width), F32)],
        compiler_params=params(),
        cost_estimate=cost("last_back"),
        name="last_back",
    )(*pair, *other, hidden, grad_residual, gain, *after)


def pack_sums(vec2, vec1, up_a, up_b, times, after):
    pairs, _, width = times.shape

    def kernel(v2, v1, ua, ub, t, out):
        out[0:3] = v2[0:3]
        out[3:5] = v1[0:2]
        out[5:6] = ua[...] + ub[...]
        out[6:8] = jnp.zeros((2, width), F32)
        for n in range(pairs):
            out[8 + 2 * n : 10 + 2 * n] = t[n]

    return small_call(kernel, [shape((8 + 2 * pairs, width), F32)], [vec2, vec1, up_a, up_b, times], after, "pack_sums")[0]


def join_sums(a, b, after, name):
    rows, width = a.shape
    more = rows - 8

    def kernel(a_ref, b_ref, out):
        out[0:8] = a_ref[0:8] + b_ref[0:8]
        out[8 : 8 + more] = a_ref[8:]
        out[8 + more :] = b_ref[8:]

    return small_call(kernel, [shape((8 + 2 * more, width), F32)], [a, b], after, name)[0]


def table_kernel(slots, steps, ids, own, other, *refs):
    vec_out, (out, table, acc, at_ref) = refs[:6], refs[6:]
    groups = at_ref.shape[0]
    rows, (row_length, row_group, row_step) = row_fields(ids)
    local = table.shape[2]
    half = slots // 2
    for n, vec in enumerate(vec_out):
        row = own[n : n + 1] + (other[n : n + 1] if n < 5 else 0.0)
        vec[...] = row.reshape(row.shape[1])
    for p in range(own.shape[1] // local):

        @pl.when(ids[2] == p)
        def _():
            table[0] = own[8:, p * local : (p + 1) * local]
            table[1] = other[8:, p * local : (p + 1) * local]

    acc[...] = jnp.zeros_like(acc)

    def clear(g, _):
        at_ref[g] = 0
        return 0

    lax.fori_loop(0, groups, clear, 0)

    def place(long):
        def one(r, _):
            @pl.when((row_length(r) > SHORT) == long)
            def _():
                g = row_group(r)
                at = at_ref[g]
                at_ref[g] = at + (2 if long else 1)
                which = (at // half) ^ ids[0]
                base = (g ^ ids[1]) * half + lax.rem(at, half)
                value = table[which, pl.ds(base, 1), :]
                if long:
                    value = value + table[which, pl.ds(base + 1, 1), :]
                step = pl.ds(row_step(r), 1)
                acc[step, :] = acc[step, :] + value

            return 0

        lax.fori_loop(0, rows, one, 0)

    place(True)
    place(False)
    out[...] = jnp.transpose(acc[...])[:, :steps]


def table_grad(scalars, own, other, steps, local, slots, after):
    rows, width = own.shape
    groups = (rows - 8) * 2 // slots
    return pl.pallas_call(
        lambda *refs: table_kernel(slots, steps, *refs[:3], *refs[3 + len(after) :]),
        grid_spec=pltpu.PrefetchScalarGridSpec(
            num_scalar_prefetch=1,
            grid=(1,),
            in_specs=[VM, VM] + [ANY] * len(after),
            out_specs=[pl.BlockSpec((width,), lambda *_: (0,))] * 6 + [pl.BlockSpec((local, steps), lambda *_: (0, 0))],
            scratch_shapes=[
                pltpu.VMEM((2, rows - 8, local), F32),
                pltpu.VMEM((pl.cdiv(steps, 128) * 128, local), F32),
                pltpu.SMEM((groups,), jnp.int32),
            ],
        ),
        out_shape=[pltpu.HBM((width,), F32)] * 6 + [pltpu.HBM((local, steps), F32)],
        compiler_params=params(),
        cost_estimate=cost("table_grad"),
        name="table_grad",
    )(scalars, own, other, *after)


def finish(residuals, pair, other, bias, after):
    rows, width = pair.shape
    part = rows // len(residuals)

    def kernel(*refs):
        res = refs[: len(residuals)]
        pair_ref, other_ref, bias_ref = refs[len(residuals) : len(residuals) + 3]
        out = refs[-1]
        for n, r in enumerate(res):
            at = slice(n * part, (n + 1) * part)
            total = r[...] + (pair_ref[at].astype(F32) + other_ref[at].astype(F32))
            out[at] = (total + row_vector(bias_ref)).astype(BF16)

    return small_call(kernel, [shape((rows, width), BF16)], [*residuals, pair, other, bias], after, "finish")[0]


def order_rows(ids, own, other, after, name):
    part, width = own.shape

    def kernel(ids_ref, own_ref, other_ref, *refs):
        out, sems = refs[len(after) :]
        copies = []
        for n, ref in enumerate((own_ref, other_ref)):
            start = pl.multiple_of((ids_ref[0] ^ n) * part, 16)
            copies.append(pltpu.make_async_copy(ref, out.at[pl.ds(start, part), :], sems.at[n]))
            copies[-1].start()
        for copy in copies:
            copy.wait()

    return pl.pallas_call(
        kernel,
        grid_spec=pltpu.PrefetchScalarGridSpec(
            num_scalar_prefetch=1,
            grid=(1,),
            in_specs=[VM, VM] + [ANY] * len(after),
            out_specs=HB,
            scratch_shapes=[pltpu.SemaphoreType.DMA((2,))],
        ),
        out_shape=pltpu.HBM((2 * part, width), BF16),
        compiler_params=params(),
        cost_estimate=cost(name),
        name=name,
    )(ids, own, other, *after)


def shards(
    tokens, row_length, row_group, row_step, time_table, norm1_gain, norm1_bias, w_qkv, w_out,
    norm2_gain, norm2_bias, w_up, up_bias, w_down, down_bias, cotangent,
):
    count, width = tokens.shape
    n_dp = lax.axis_size("dp")
    dp = lax.axis_index("dp")
    part = lax.axis_index("tensor")
    core = lax.rem(part, 2)
    direct = n_dp == 8
    low_bit, top_bit = dp & 1, (dp >> 2) & 1
    mid_bit = ((dp >> 1) & 1) ^ top_bit
    if direct:
        orders = [low_bit, 2 * mid_bit + top_bit, mid_bit, 2 * low_bit + top_bit]
    else:
        orders = [1, 0, 1, 0]
    own = jnp.stack([core, dp, part, *[jnp.int32(o) for o in orders], jnp.int32(0)]).astype(jnp.int32)
    ids = jnp.concatenate([own, row_length, row_group, row_step])
    scalars = ids
    order_a, order_b = 3, 5
    bits = ((1, 2, 6), (2, 1, 6))
    local = w_out.shape[0]
    slots = count // SHORT
    heads = jnp.transpose(w_qkv, (1, 2, 0))
    far = lambda x: pltpu.with_memory_space_constraint(x, pltpu.HBM)
    size = count // 2
    peer_rows = lambda ids: 1 - ids[0]
    own_rows = lambda ids: ids[0]
    zero = lambda ids: 0

    send, keep, hidden, normed, q, k, v, p, ctx = attend(
        0, 1, scalars, *[far(x) for x in (tokens, time_table, norm1_gain, norm1_bias, heads, w_out)], []
    )
    pair = add_two(keep, core_swap(send), [], "pair_one")
    other = chip_swap(pair)
    w_up, w_down, cotangent = stage([far(x) for x in (w_up, w_down, cotangent)], [pair])
    grad_act = act_grad(cotangent, w_down)
    residual, own2 = mid_forward(hidden, pair, other, norm2_gain, norm2_bias, [grad_act])
    peer2 = core_swap(own2)
    keep, act_own, low_rows_own, up_own = expand(ids, True, own2, grad_act, w_up, up_bias, [])
    send, act_peer, low_rows_peer, up_peer = expand(ids, False, peer2, grad_act, w_up, up_bias, [keep])
    got_two = core_swap(send)
    first_keep = keep
    start = send
    cots = [(cotangent, size, f) for f in (peer_rows, own_rows)]
    acts = [(act_peer, size, zero), (act_own, size, zero)]
    lows = [(low_rows_peer, size, zero), (low_rows_own, size, zero)]
    norms = [(peer2, size, zero), (own2, size, zero)]
    mlp = Dual(bits, direct)
    heads_sum = Dual(bits, direct)
    it = types.SimpleNamespace(attn=[])
    placed = [None, None]

    def down_grad(after):
        halves = weight_grad(ids, order_a, [list(zip(acts, cots))], after, "down_grad")
        mlp.begin(0, halves)
        return halves[1]

    def up_grad(after):
        halves = weight_grad(ids, order_b, [list(zip(norms, lows))], after, "up_grad")
        mlp.begin(1, halves)
        return halves[1]

    def pair_two(after):
        it.pair2 = add_two(first_keep, got_two, after, "pair_two")
        it.other2 = chip_swap(it.pair2)
        return it.pair2

    def contract(after):
        send, it.keep_e = contract_rows(act_peer, act_own, w_down, after)
        it.got_e = core_swap(send)
        return it.keep_e

    def mid(after):
        it.grad_res, *it.low_own, it.vec2 = mid_back(
            0, 1, ids, it.pair2, it.other2, residual, cotangent, norm2_gain, LOW_PIECES, after
        )
        it.low_peer = [core_swap(x) for x in it.low_own]
        return it.low_own[0]

    def attend_grad(after):
        *send, it.keep3, it.dq, it.dk, it.dv = attend_back(
            it.low_peer, it.low_own, q, k, v, p, heads, w_out, PART_PIECES, after
        )
        it.got3 = [core_swap(x) for x in send]
        return it.keep3

    def qk_grad(after):
        halves = head_grad(ids, order_a, (it.dq, [normed]), (it.dk, [normed]), after, "qk_grad")
        heads_sum.begin(0, halves)
        return halves[1]

    def vo_grad(after):
        lows = [*it.low_peer, *it.low_own]
        halves = head_grad(ids, order_b, (it.dv, [normed]), (ctx, lows), after, "vo_grad")
        heads_sum.begin(1, halves)
        return halves[1]

    def pair_three(after):
        it.pair3 = add_pieces(it.keep3, it.got3, 2, after, "pair_three")
        it.other3 = [chip_swap(x) for x in it.pair3]
        return it.pair3[0]

    def pair_out(after):
        it.pair_e = add_two(it.keep_e, it.got_e, after, "pair_out")
        it.other_e = chip_swap(it.pair_e)
        return it.pair_e

    def last(after):
        it.low_in, it.vec1, it.times = last_back(
            it.pair3, it.other3, hidden, it.grad_res, norm1_gain, after
        )
        it.low_got = core_swap(it.low_in)
        return it.low_in

    def pack(after):
        it.sums = pack_sums(it.vec2, it.vec1, up_own, up_peer, it.times, after)
        it.sums_got = dp_swap(it.sums, 1)
        return it.sums

    def join(level):
        def run(after):
            bit = 2 << level
            sums = join_sums(it.sums, it.sums_got, after, "join_sums")
            while level == 2 and bit < n_dp:
                sums = join_sums(sums, dp_swap(sums, bit), [], "join_sums")
                bit *= 2
            it.sums = sums
            if level < 2:
                it.sums_got = dp_swap(sums, bit)
            else:
                it.sums_peer = core_swap(sums)
            return sums

        return run

    def input_rows(after):
        it.input_grad = order_rows(ids, it.low_in, it.low_got, after, "order_input")
        return far(it.input_grad)

    def final(after):
        it.final = finish([residual], it.pair_e, it.other_e, down_bias, after)
        it.final_got = core_swap(it.final)
        return it.final

    def output_rows(after):
        it.block_output = order_rows(ids, it.final, it.final_got, after, "order_output")
        return far(it.block_output)

    def table(after):
        *it.vec, it.time_grad = table_grad(
            scalars, it.sums, it.sums_peer, time_table.shape[0], local, slots, after
        )
        return far(it.vec[0])

    def place(which, half):
        def run(after):
            order, value = (order_a, order_b)[which], mlp.collect(which)[half]
            placed[which] = place_half(ids, order, value, half, placed[which], after, ("place_down", "place_up")[which])
            return far(placed[which])

        return run

    def place_attn(half):
        def run(after):
            a, b = heads_sum.collect(0)[half], heads_sum.collect(1)[half]
            it.attn = place_heads(ids, (order_a, order_b), a, b, half, it.attn, after, "place_heads")
            return far(it.attn[1])

        return run

    def sum_step(group):
        return lambda after: group.step(after[0])

    order = (
        down_grad, pair_two, up_grad, contract, mid, sum_step(mlp), attend_grad, sum_step(mlp), vo_grad,
        pair_out, pair_three, qk_grad, sum_step(heads_sum), last, sum_step(heads_sum), pack, sum_step(mlp),
        sum_step(heads_sum), join(0), join(1), sum_step(mlp), sum_step(heads_sum), place_attn(0), join(2),
        final, place(0, 0), place(1, 0), input_rows, output_rows, table, place(1, 1), place(0, 1),
        place_attn(1),
    )
    mark = first_keep
    for step in order:
        mark = step([mark])
    vec, time_grad = it.vec, it.time_grad
    block_output, input_grad = it.block_output, it.input_grad
    down_out, up_out = placed
    qkv_out, proj_out = it.attn

    return (
        block_output,
        input_grad,
        time_grad.T,
        vec[3],
        vec[4],
        jnp.transpose(qkv_out, (2, 0, 1)),
        proj_out,
        vec[0],
        vec[1],
        up_out,
        vec[5],
        down_out,
        vec[2],
    )


def solution(mesh):
    in_specs = (
        P("dp", None), P(), P(), P(), P(), P(), P(), P(None, None, "tensor"), P("tensor", None), P(), P(),
        P(None, "tensor"), P("tensor"), P("tensor", None), P(), P("dp", None),
    )
    out_specs = (
        P("dp", None), P("dp", None), P(None, "tensor"), P(), P(), P(None, None, "tensor"), P("tensor", None),
        P(), P(), P(None, "tensor"), P("tensor"), P("tensor", None), P(),
    )
    return jax.shard_map(shards, mesh=mesh, in_specs=in_specs, out_specs=out_specs, check_vma=False)
```

```python
import functools
import types

import jax
import jax.numpy as jnp
from jax import lax
from jax.experimental import pallas as pl
from jax.experimental.pallas import tpu as pltpu
from jax.sharding import PartitionSpec as P

HEAD_DIM = 64
SHORT = 128
PAIR = 256
EPS = 1e-05
NEG = -1000000000.0
SQRT_HALF = 0.7071067811865476
PHI_ZERO = 0.3989422804014327
VMEM_MB = 16
LOW_PIECES = 2
PART_PIECES = 4

SMALL_MB = 8

F32 = jnp.float32
BF16 = jnp.bfloat16


def mm(left, right, left_dim, right_dim):
    return lax.dot_general(
        left, right, (((left_dim,), (right_dim,)), ((), ())), preferred_element_type=F32
    )


def params(dims=1):
    return pltpu.CompilerParams(
        dimension_semantics=("arbitrary",) * dims, vmem_limit_bytes=VMEM_MB << 20
    )


COSTS = {"finish": 0.5, "up_grad": 1}


def cost(name):
    return pl.CostEstimate(flops=int(COSTS.get(name, 0) * 1e9), bytes_accessed=1, transcendentals=0)


def shape(dims, dtype):
    return jax.ShapeDtypeStruct(dims, dtype)


def whole(array):
    zeros = (0,) * array.ndim
    return pl.BlockSpec(array.shape, lambda *_: zeros)


def swap(value, axis, bit):
    return lax.ppermute(value, axis, [(i, i ^ bit) for i in range(lax.axis_size(axis))])


def core_swap(value):
    return swap(value, "tensor", 1)


def chip_swap(value):
    return swap(value, "tensor", 2)


def dp_swap(value, bit):
    return swap(value, "dp", bit)


def norm_stats(values):
    mean = jnp.mean(values, axis=-1, keepdims=True)
    centred = values - mean
    variance = jnp.mean(centred * centred, axis=-1, keepdims=True)
    scale = lax.rsqrt(variance + EPS)
    return centred * scale, scale


IDS = 8


def row_fields(info):
    rows = (info.shape[0] - IDS) // 3
    return rows, [lambda r, at=at: info[IDS + at * rows + r] for at in range(3)]


def fill_slots(slot_ref, info):
    group = info[1]
    rows, (row_length, row_group, row_step) = row_fields(info)

    def long_row(r, pos):
        step = row_step(r)
        slot_ref[pos] = step
        slot_ref[pos + 1] = step
        hit = (row_group(r) == group) & (row_length(r) > SHORT)
        return pos + jnp.where(hit, 2, 0)

    def short_row(r, pos):
        slot_ref[pos] = row_step(r)
        hit = (row_group(r) == group) & (row_length(r) <= SHORT)
        return pos + jnp.where(hit, 1, 0)

    long_slots = lax.fori_loop(0, rows, long_row, 0, unroll=8)
    lax.fori_loop(0, rows, short_row, long_slots, unroll=8)
    return long_slots


def block_of(i, ids, chunk, half, chunks):
    side = jnp.where(i < half, 1 - ids[0], ids[0])
    return side * (half * chunks) + chunk * half + lax.rem(i, half)


def add_low(a, b):
    return (a.astype(F32) + b.astype(F32)).astype(BF16)


def row_vector(ref):
    return ref[...].reshape(1, ref.shape[0])


VM = pl.BlockSpec(memory_space=pltpu.VMEM)
ANY = pl.BlockSpec(memory_space=pl.ANY)


def small_call(kernel, out_shape, operands, after, name):
    count = len(operands)
    return pl.pallas_call(
        lambda *refs: kernel(*refs[:count], *refs[count + len(after) :]),
        in_specs=[VM] * count + [ANY] * len(after),
        out_specs=[VM] * len(out_shape),
        out_shape=out_shape,
        compiler_params=pltpu.CompilerParams(vmem_limit_bytes=SMALL_MB << 20),
        cost_estimate=cost(name),
        name=name,
    )(*operands, *after)


def stage(arrays, after):
    count = len(arrays)

    def kernel(*refs):
        out, sems = refs[count + len(after) : -1], refs[-1]
        copies = [pltpu.make_async_copy(refs[n], out[n], sems.at[n]) for n in range(count)]
        for copy in copies:
            copy.start()
        for copy in copies:
            copy.wait()

    return pl.pallas_call(
        kernel,
        in_specs=[pl.BlockSpec(memory_space=pltpu.HBM)] * count + [ANY] * len(after),
        out_specs=[VM] * count,
        out_shape=[pltpu.VMEM(a.shape, a.dtype) for a in arrays],
        scratch_shapes=[pltpu.SemaphoreType.DMA((count,))],
        compiler_params=pltpu.CompilerParams(vmem_limit_bytes=SMALL_MB << 20),
        cost_estimate=cost("stage"),
        name="stage",
    )(*arrays, *after)


def add_two(a, b, after, name):
    def kernel(a_ref, b_ref, out):
        out[...] = add_low(a_ref[...], b_ref[...])

    return small_call(kernel, [shape(a.shape, BF16)], [a, b], after, name)[0]


def attend_kernel(
    chunk, half, chunks, slots, ids,
    tokens, table, gain, bias, w_qkv, wo,
    send, keep, hidden_out, normed_out, q_out, k_out, v_out, p_out, c_out,
    slot_ref, rows_ref, sems,
):
    i = pl.program_id(0)

    def fetch(s):
        step = slot_ref[s]
        start = pl.multiple_of((step // 8) * 8, 8)
        return pltpu.make_async_copy(table.at[pl.ds(start, 8), :], rows_ref.at[s], sems.at[s])

    @pl.when(i == 0)
    def _():
        slot_ref[slots + 2] = fill_slots(slot_ref, ids)
        for s in range(slots):
            fetch(s).start()
        for s in range(slots):
            fetch(s).wait()

    block = block_of(i, ids, chunk, half, chunks)
    sub = lax.broadcasted_iota(jnp.int32, (8, 1), 0)

    def row_of(s):
        picked = sub == lax.rem(slot_ref[s], 8)
        return jnp.sum(jnp.where(picked, rows_ref[s].astype(F32), 0.0), axis=0, keepdims=True)

    low_half = lax.broadcasted_iota(jnp.int32, (PAIR, 1), 0) < SHORT
    step_row = jnp.where(low_half, row_of(2 * block), row_of(2 * block + 1))
    hidden = tokens[...].astype(F32) + step_row
    unit, _ = norm_stats(hidden)
    normed = (unit * row_vector(gain) + row_vector(bias)).astype(BF16)
    normed_out[...] = normed
    q = mm(normed, w_qkv[0], 1, 1).astype(BF16)
    k = mm(normed, w_qkv[1], 1, 1).astype(BF16)
    v = mm(normed, w_qkv[2], 1, 1).astype(BF16)
    q_out[...] = q
    k_out[...] = k
    v_out[...] = v
    split = (2 * block >= slot_ref[slots + 2]).astype(jnp.int32)
    row_half = lax.broadcasted_iota(jnp.int32, (PAIR, PAIR), 0) // SHORT
    col_half = lax.broadcasted_iota(jnp.int32, (PAIR, PAIR), 1) // SHORT
    allowed = ((row_half ^ col_half) * split) == 0
    width = q.shape[1]
    head = lax.broadcasted_iota(jnp.int32, (1, width), 1) // HEAD_DIM
    context = jnp.zeros((PAIR, width), F32)
    for h in range(width // HEAD_DIM):
        mine = head == h
        qh = jnp.where(mine, q, jnp.zeros_like(q))
        scores = mm(qh, k, 1, 1) * (HEAD_DIM**-0.5)
        scores = jnp.where(allowed, scores, NEG)
        top = jnp.max(scores, axis=-1, keepdims=True)
        powers = jnp.exp(scores - top)
        total = jnp.sum(powers, axis=-1, keepdims=True)
        weights = (powers * (1.0 / total)).astype(BF16)
        p_out[0, h] = weights
        context = context + mm(weights, jnp.where(mine, v, jnp.zeros_like(v)), 1, 0)
    low = context.astype(BF16)
    c_out[...] = low
    part = mm(low, wo[...], 1, 0).astype(BF16)

    @pl.when(i < half)
    def _():
        send[...] = part

    @pl.when(i >= half)
    def _():
        keep[...] = part
        hidden_out[...] = hidden


def attend(chunk, chunks, scalars, tokens, table, gain, bias, w_qkv, wo, after):
    count, width = tokens.shape
    local = wo.shape[0]
    blocks = count // PAIR // chunks
    half = blocks // 2
    rows = blocks * PAIR
    slots = count // SHORT
    own = rows // 2
    heads = local // HEAD_DIM
    first = lambda i, *_: (jnp.minimum(i, half - 1), 0)
    second = lambda i, *_: (jnp.maximum(i - half, 0), 0)
    step = lambda i, *_: (i, 0)
    row = pl.BlockSpec((PAIR, width), step)
    thin = pl.BlockSpec((PAIR, local), step)
    return pl.pallas_call(
        lambda *refs: attend_kernel(chunk, half, chunks, slots, *refs[:7], *refs[7 + len(after) :]),
        grid_spec=pltpu.PrefetchScalarGridSpec(
            num_scalar_prefetch=1,
            grid=(blocks,),
            in_specs=[
                pl.BlockSpec((PAIR, width), lambda i, ids, *_: (block_of(i, ids, chunk, half, chunks), 0)),
                pl.BlockSpec(memory_space=pltpu.HBM),
                whole(gain), whole(bias), whole(w_qkv), whole(wo),
            ]
            + [ANY] * len(after),
            out_specs=[
                pl.BlockSpec((PAIR, width), first),
                pl.BlockSpec((PAIR, width), second),
                pl.BlockSpec((PAIR, width), second),
                row, thin, thin, thin,
                pl.BlockSpec((1, heads, PAIR, PAIR), lambda i, *_: (i, 0, 0, 0)),
                thin,
            ],
            scratch_shapes=[
                pltpu.SMEM((slots + 4,), jnp.int32),
                pltpu.VMEM((slots, 8, width), BF16),
                pltpu.SemaphoreType.DMA((slots,)),
            ],
        ),
        out_shape=[
            shape((own, width), BF16), shape((own, width), BF16), shape((own, width), F32),
            shape((rows, width), BF16),
            shape((rows, local), BF16), shape((rows, local), BF16), shape((rows, local), BF16),
            shape((blocks, heads, PAIR, PAIR), BF16),
            shape((rows, local), BF16),
        ],
        compiler_params=params(),
        cost_estimate=cost("attend"),
        name="attend",
    )(scalars, tokens, table, gain, bias, w_qkv, wo, *after)


def mid_kernel(hidden, pair, other, gain, bias, residual_out, normed_out):
    residual = hidden[...] + (pair[...].astype(F32) + other[...].astype(F32))
    residual_out[...] = residual
    unit, _ = norm_stats(residual)
    normed_out[...] = (unit * row_vector(gain) + row_vector(bias)).astype(BF16)


def mid_forward(hidden, pair, other, gain, bias, after):
    rows, width = hidden.shape
    row = pl.BlockSpec((PAIR, width), lambda i: (i, 0))
    return pl.pallas_call(
        lambda *refs: mid_kernel(*refs[:5], *refs[5 + len(after) :]),
        grid=(rows // PAIR,),
        in_specs=[row, row, row, whole(gain), whole(bias)] + [ANY] * len(after),
        out_specs=[row, row],
        out_shape=[shape((rows, width), F32), shape((rows, width), BF16)],
        compiler_params=params(),
        cost_estimate=cost("mid_forward"),
        name="mid_forward",
    )(hidden, pair, other, gain, bias, *after)


def act_grad(cot, w_down):
    rows, width = cot.shape
    local = w_down.shape[0]

    def kernel(cot_ref, w_ref, out):
        out[...] = mm(cot_ref[...], w_ref[...], 1, 1)

    return pl.pallas_call(
        kernel,
        grid=(rows // PAIR,),
        in_specs=[pl.BlockSpec((PAIR, width), lambda i: (i, 0)), VM],
        out_specs=pl.BlockSpec((PAIR, local), lambda i: (i, 0)),
        out_shape=shape((rows, local), F32),
        compiler_params=params(),
        cost_estimate=cost("act_grad"),
        name="act_grad",
    )(cot, w_down)


def expand_kernel(ids, normed, grad_act, w_up, up_bias, part_out, act_out, low_out, bias_out):
    pre = mm(normed[...], w_up[...], 1, 0) + row_vector(up_bias)
    cdf = 0.5 * (1.0 + lax.erf(pre * SQRT_HALF))
    act_out[...] = (pre * cdf).astype(BF16)
    slope = cdf + pre * (PHI_ZERO * jnp.exp(-0.5 * (pre * pre)))
    grad_pre = grad_act[...] * slope

    @pl.when(pl.program_id(0) == 0)
    def _():
        bias_out[...] = jnp.zeros_like(bias_out)

    bias_out[...] += jnp.sum(grad_pre, axis=0, keepdims=True)
    low = grad_pre.astype(BF16)
    low_out[...] = low
    part_out[...] = mm(low, w_up[...], 1, 1).astype(BF16)


def expand(ids, own, normed, grad_act, w_up, up_bias, after):
    rows, width = normed.shape
    local = w_up.shape[1]
    blocks = rows // PAIR
    side = 0 if own else 1
    row = pl.BlockSpec((PAIR, width), lambda i, *_: (i, 0))
    thin = pl.BlockSpec((PAIR, local), lambda i, *_: (i, 0))
    return pl.pallas_call(
        lambda *refs: expand_kernel(*refs[:5], *refs[5 + len(after) :]),
        grid_spec=pltpu.PrefetchScalarGridSpec(
            num_scalar_prefetch=1,
            grid=(blocks,),
            in_specs=[
                row,
                pl.BlockSpec((PAIR, local), lambda i, ids: ((ids[0] ^ side) * blocks + i, 0)),
                VM, whole(up_bias),
            ]
            + [ANY] * len(after),
            out_specs=[row, thin, thin, pl.BlockSpec((1, local), lambda i, *_: (0, 0))],
        ),
        out_shape=[
            shape((rows, width), BF16), shape((rows, local), BF16), shape((rows, local), BF16),
            shape((1, local), F32),
        ],
        compiler_params=params(),
        cost_estimate=cost("expand"),
        name="expand",
    )(ids, normed, grad_act, w_up, up_bias, *after)


def contract_kernel(a, b, w_down, send, keep):
    i = pl.program_id(0)
    act = jnp.where(i < 2, a[...], b[...])
    part = mm(act, w_down[...], 1, 0).astype(BF16)

    @pl.when(i < 2)
    def _():
        send[...] = part

    @pl.when(i >= 2)
    def _():
        keep[...] = part


def contract_rows(peer, own, w_down, after):
    rows, local = peer.shape
    width = w_down.shape[1]
    first = lambda i: (jnp.minimum(i, 1), 0)
    second = lambda i: (jnp.maximum(i - 2, 0), 0)
    return pl.pallas_call(
        lambda *refs: contract_kernel(*refs[:3], *refs[3 + len(after) :]),
        grid=(2 * rows // PAIR,),
        in_specs=[pl.BlockSpec((PAIR, local), first), pl.BlockSpec((PAIR, local), second), VM] + [ANY] * len(after),
        out_specs=[pl.BlockSpec((PAIR, width), first), pl.BlockSpec((PAIR, width), second)],
        out_shape=[shape((rows, width), BF16), shape((rows, width), BF16)],
        compiler_params=params(),
        cost_estimate=cost("contract_rows"),
        name="contract_rows",
    )(peer, own, w_down, *after)


def weight_kernel(order, groups, ids, *refs):
    count = sum(len(lefts) for lefts in groups)
    left, right = refs[:count], refs[count : 2 * count]
    send, keep, scratch = refs[2 * count : 2 * count + 3]
    i = pl.program_id(0)
    many = len(groups) > 1
    rows = send.shape[-2]
    at = 0
    for n, sizes in enumerate(groups):
        total = mm(left[at][...], right[at][...], 0, 0)
        for j in range(at + 1, at + len(sizes)):
            total = total + mm(left[j][...], right[j][...], 0, 0)
        at += len(sizes)
        scratch[n] = total

    def write(out):
        for r in range(4):
            start = pl.multiple_of((ids[order + 1] ^ r) * rows, 8)
            for n in range(len(groups)):
                value = scratch[n, pl.ds(start, rows), :].astype(BF16)
                if many:
                    out[r, n] = value
                else:
                    out[r] = value

    @pl.when(i == 0)
    def _():
        write(send)

    @pl.when(i == 1)
    def _():
        write(keep)


def weight_grad(ids, order, groups, after, name):
    rows_out = groups[0][0][0][0].shape[1]
    tile = rows_out // 2
    part = tile // 4
    cols = groups[0][0][1][0].shape[1]
    lefts = [left for pieces in groups for left, _ in pieces]
    rights = [right for pieces in groups for _, right in pieces]
    count = sum(size for _, size, _ in lefts)

    def column(i, ids):
        return jnp.where(i == 0, 1 - ids[order], ids[order])

    specs = [pl.BlockSpec((size, tile), lambda i, ids, at=at: (at(ids), column(i, ids))) for _, size, at in lefts]
    specs += [pl.BlockSpec((size, cols), lambda i, ids, at=at: (at(ids), 0)) for _, size, at in rights]
    dims = (4, part, cols) if len(groups) == 1 else (4, len(groups), part, cols)
    out = pl.BlockSpec(dims, lambda i, ids: (0,) * len(dims))
    kernel = functools.partial(weight_kernel, order, [[size for (_, size, _), _ in g] for g in groups])
    total = len(lefts)
    return list(pl.pallas_call(
        lambda ids, *refs: kernel(ids, *refs[: 2 * total], *refs[2 * total + len(after) :]),
        grid_spec=pltpu.PrefetchScalarGridSpec(
            num_scalar_prefetch=1,
            grid=(2,),
            in_specs=specs + [ANY] * len(after),
            out_specs=[out, out],
            scratch_shapes=[pltpu.VMEM((len(groups), tile, cols), F32)],
        ),
        out_shape=[shape(dims, BF16), shape(dims, BF16)],
        compiler_params=params(),
        cost_estimate=cost(name),
        name=name,
    )(ids, *[a for a, _, _ in lefts], *[b for b, _, _ in rights], *after))


def head_grad(ids, order, first, second, after, name):
    rows_out, cols = first[0].shape[1], first[1][0].shape[1]
    part = rows_out // 8
    flat = [first[0], *first[1], second[0], *second[1]]

    def kernel(ids_ref, *refs):
        values = refs[: len(flat)]
        send, keep, scratch = refs[len(flat) + len(after) :]
        at = 0
        for n, (_, pieces) in enumerate((first, second)):
            rights = [values[at + 1 + j][...] for j in range(len(pieces))]
            right = rights[0] if len(rights) == 1 else jnp.concatenate(rights, axis=0)
            scratch[n] = mm(values[at][...], right, 0, 0)
            at += 1 + len(pieces)
        for half, out in ((1 - ids_ref[order], send), (ids_ref[order], keep)):
            for r in range(4):
                start = pl.multiple_of((half * 4 + (ids_ref[order + 1] ^ r)) * part, 8)
                for n in range(2):
                    out[r, n] = scratch[n, pl.ds(start, part), :].astype(BF16)

    dims = (4, 2, part, cols)
    return pl.pallas_call(
        kernel,
        grid_spec=pltpu.PrefetchScalarGridSpec(
            num_scalar_prefetch=1,
            grid=(1,),
            in_specs=[VM] * len(flat) + [ANY] * len(after),
            out_specs=[VM, VM],
            scratch_shapes=[pltpu.VMEM((2, rows_out, cols), F32)],
        ),
        out_shape=[shape(dims, BF16), shape(dims, BF16)],
        compiler_params=params(),
        cost_estimate=cost(name),
        name=name,
    )(ids, *flat, *after)


def add_pieces(a, b, pieces, after, name):
    rows, width = a.shape
    size, out_size = rows // len(b), rows // pieces
    step = min(size, out_size)

    def kernel(a_ref, *refs):
        given, out = refs[: len(b)], refs[len(b) :]
        for at in range(0, rows, step):
            got = given[at // size][at % size : at % size + step]
            out[at // out_size][at % out_size : at % out_size + step] = add_low(a_ref[at : at + step], got)

    return list(small_call(kernel, [shape((out_size, width), BF16)] * pieces, [a, *b], after, name))


class Dual:
    def __init__(self, bits, direct):
        self.bits, self.direct, self.level = bits, direct, 0
        self.summed = [None, None]
        self.halves, self.got = [None, None], [None, None]

    def begin(self, which, halves):
        self.halves[which] = list(halves)
        if self.direct:
            self.got[which] = dp_swap(halves[0], self.bits[which][0])

    def step(self, after):
        if not self.direct:
            return after
        (_, keep_a), (_, keep_b) = self.halves
        level, name = self.level, "exchange"
        self.level += 1
        first, second = self.bits
        if level < 2:
            parts, rest = keep_a.shape[0], keep_a.shape[1:]
            half = parts // 2
            if level == 0:

                def kernel(ka, ga, kb, gb, sa, oa, sb, ob):
                    for k, g, send, out in ((ka, ga, sa, oa), (kb, gb, sb, ob)):
                        send[...] = add_low(k[half:], g[half:])
                        out[...] = add_low(k[:half], g[:half])

                out = [shape((half, *rest), BF16)] * 4
                sa, oa, sb, ob = small_call(kernel, out, [keep_a, self.got[0], keep_b, self.got[1]], [after], name)
                self.halves = [[sa, oa], [sb, ob]]
                self.got = [dp_swap(sa, first[1]), dp_swap(sb, second[1])]
                return oa

            def kernel(ka, ga, kb, gb, out):
                for n, (k, g) in enumerate(((ka, ga), (kb, gb))):
                    out[n] = add_low(k[...], g[...])

            out = [shape((2, parts, *rest), BF16)]
            both = small_call(kernel, out, [keep_a, self.got[0], keep_b, self.got[1]], [after], name)[0]
            self.halves = [[None, both], [None, both]]
            self.got = [dp_swap(both, first[2]), None]
            return both
        if level == 2:

            def kernel(k, g, oa, ob):
                for n, out in enumerate((oa, ob)):
                    for j in range(2):
                        out[j] = add_low(k[n, j], g[n, 1 - j])

            out = [shape(keep_a.shape[1:], BF16)] * 2
            oa, ob = small_call(kernel, out, [keep_a, self.got[0]], [after], name)
            self.halves = [[None, oa], [None, ob]]
            self.got = [dp_swap(oa, first[1]), dp_swap(ob, second[1])]
            return oa
        rest = keep_a.shape[1:]

        def kernel(ka, ga, kb, gb, oa, ob):
            for k, g, out in ((ka, ga, oa), (kb, gb, ob)):
                out[:2] = k[...]
                out[2:] = g[...]

        out = [shape((4, *rest), BF16)] * 2
        oa, ob = small_call(kernel, out, [keep_a, self.got[0], keep_b, self.got[1]], [after], name)
        self.halves = [[None, oa], [None, ob]]
        self.got = [dp_swap(oa, first[0]), dp_swap(ob, second[0])]
        return oa

    def collect(self, which):
        if not self.direct:
            if self.summed[which] is None:
                send, keep = lax.psum(tuple(self.halves[which]), "dp")
                self.summed[which] = keep, send
            return self.summed[which]
        return self.halves[which][1], self.got[which]


HB = pl.BlockSpec(memory_space=pltpu.HBM)


def place_half(ids, order, value, flip, base, after, name):
    _, part, cols = value.shape
    given = [] if base is None else [pltpu.with_memory_space_constraint(base, pltpu.HBM)]

    def kernel(ids_ref, value_ref, *refs):
        out, wide, sems = refs[-3:]
        copies = []
        for r in range(4):
            start = ((ids_ref[order] ^ flip) * 4 + (ids_ref[order + 1] ^ r)) * part
            wide[r] = value_ref[r].astype(F32)
            rows = out.at[pl.ds(pl.multiple_of(start, 8), part), :]
            copies.append(pltpu.make_async_copy(wide.at[r], rows, sems.at[r]))
            copies[-1].start()
        for copy in copies:
            copy.wait()

    return pl.pallas_call(
        kernel,
        grid_spec=pltpu.PrefetchScalarGridSpec(
            num_scalar_prefetch=1,
            grid=(1,),
            in_specs=[VM] + [HB] * len(given) + [ANY] * len(after),
            out_specs=HB,
            scratch_shapes=[pltpu.VMEM((4, part, cols), F32), pltpu.SemaphoreType.DMA((4,))],
        ),
        out_shape=pltpu.HBM((8 * part, cols), F32),
        input_output_aliases={2: 0} if given else {},
        compiler_params=params(),
        cost_estimate=cost(name),
        name=name,
    )(ids, value, *given, *after)


def place_heads(ids, orders, a, b, flip, bases, after, name):
    _, _, part, cols = a.shape
    rows = 8 * part
    given = [pltpu.with_memory_space_constraint(x, pltpu.HBM) for x in bases]

    def kernel(ids_ref, a_ref, b_ref, *refs):
        qkv_out, proj_out, wide, sems = refs[-4:]
        copies = []
        for n, (pick, order) in enumerate(((a_ref, orders[0]), (b_ref, orders[1]))):
            for r in range(4):
                at = (ids_ref[order] ^ flip) * 4 + (ids_ref[order + 1] ^ r)
                at = pl.ds(pl.multiple_of(at * part, 8), part)
                for j in range(2):
                    k = len(copies)
                    wide[k] = pick[r, j].astype(F32)
                    out = proj_out.at[at, :] if n + j == 2 else qkv_out.at[2 * n + j, at, :]
                    copies.append(pltpu.make_async_copy(wide.at[k], out, sems.at[k]))
                    copies[-1].start()
        for copy in copies:
            copy.wait()

    return list(
        pl.pallas_call(
            kernel,
            grid_spec=pltpu.PrefetchScalarGridSpec(
                num_scalar_prefetch=1,
                grid=(1,),
                in_specs=[VM, VM] + [HB] * len(given) + [ANY] * len(after),
                out_specs=[HB, HB],
                scratch_shapes=[pltpu.VMEM((16, part, cols), F32), pltpu.SemaphoreType.DMA((16,))],
            ),
            out_shape=[pltpu.HBM((3, rows, cols), F32), pltpu.HBM((rows, cols), F32)],
            input_output_aliases={3: 0, 4: 1} if given else {},
            compiler_params=params(),
            cost_estimate=cost(name),
            name=name,
        )(ids, a, b, *given, *after)
    )


def units(values, after):
    rows, width = values.shape
    row = pl.BlockSpec((PAIR, width), lambda i: (i, 0))

    def kernel(value_ref, *refs):
        unit_out, scale_out = refs[len(after) :]
        unit_out[...], scale_out[...] = norm_stats(value_ref[...])

    return pl.pallas_call(
        kernel,
        grid=(rows // PAIR,),
        in_specs=[row] + [ANY] * len(after),
        out_specs=[row, pl.BlockSpec((PAIR, 1), lambda i: (i, 0))],
        out_shape=[shape((rows, width), F32), shape((rows, 1), F32)],
        compiler_params=params(),
        cost_estimate=cost("units"),
        name="units",
    )(values, *after)


def mid_back_kernel(pair, other, unit_ref, scale_ref, cot, gain, grad_out, *refs):
    low_out, sums = refs[:-1], refs[-1]
    i = pl.program_id(0)
    err = pair[...].astype(F32) + other[...].astype(F32)
    unit, scale = unit_ref[...], scale_ref[...]
    top = cot[...].astype(F32)
    f = err * row_vector(gain)
    f_mean = jnp.mean(f, axis=-1, keepdims=True)
    fx_mean = jnp.mean(f * unit, axis=-1, keepdims=True)
    grad = top + scale * (f - f_mean - unit * fx_mean)
    grad_out[...] = grad
    low = grad.astype(BF16)
    per = PAIR // low_out[0].shape[0]
    for n, piece in enumerate(low_out):

        @pl.when(i == n // per)
        def _():
            rows = piece.shape[0]
            piece[...] = low[(n % per) * rows : (n % per + 1) * rows]

    @pl.when(i == 0)
    def _():
        sums[...] = jnp.zeros_like(sums)

    sums[0:1] += jnp.sum(err * unit, axis=0, keepdims=True)
    sums[1:2] += jnp.sum(err, axis=0, keepdims=True)
    sums[2:3] += jnp.sum(top, axis=0, keepdims=True)


def mid_back(chunk, chunks, ids, pair, other, unit, scale, cot, gain, pieces, after):
    rows, width = unit.shape
    half = rows // PAIR
    row = pl.BlockSpec((PAIR, width), lambda i, ids: (i, 0))
    return pl.pallas_call(
        lambda ids, *refs: mid_back_kernel(*refs[:6], *refs[6 + len(after) :]),
        grid_spec=pltpu.PrefetchScalarGridSpec(
            num_scalar_prefetch=1,
            grid=(half,),
            in_specs=[
                row, row, row, pl.BlockSpec((PAIR, 1), lambda i, ids: (i, 0)),
                pl.BlockSpec((PAIR, width), lambda i, ids: (block_of(i + half, ids, chunk, half, chunks), 0)),
                whole(gain),
            ]
            + [ANY] * len(after),
            out_specs=[row] + [VM] * pieces + [pl.BlockSpec((8, width), lambda i, ids: (0, 0))],
        ),
        out_shape=[shape((rows, width), F32)] + [shape((rows // pieces, width), BF16)] * pieces + [shape((8, width), F32)],
        compiler_params=params(),
        cost_estimate=cost("mid_back"),
        name="mid_back",
    )(ids, pair, other, unit, scale, cot, gain, *after)


def attend_back_kernel(count, blocks, *refs):
    peers, owns = refs[:count], refs[count : 2 * count]
    q_ref, k_ref, v_ref, p_ref, w_qkv, wo = refs[2 * count : 2 * count + 6]
    sends, (keep, dq_out, dk_out, dv_out, low_ref, part_ref) = refs[2 * count + 6 : -6], refs[-6:]
    i = pl.program_id(0)
    half = blocks // 2
    rows = peers[0].shape[0]

    @pl.when(i == 0)
    def _():
        for n, piece in enumerate((*peers, *owns)):
            low_ref[n * rows : (n + 1) * rows] = piece[...]

    low = low_ref[pl.ds(pl.multiple_of(i * PAIR, PAIR), PAIR), :]
    grad_context = mm(low, wo[...], 1, 1).astype(BF16)
    q, k, v = q_ref[...], k_ref[...], v_ref[...]
    width = q.shape[1]
    head = lax.broadcasted_iota(jnp.int32, (1, width), 1) // HEAD_DIM
    zero = jnp.zeros_like(q)
    dq = dk = dv = jnp.zeros((PAIR, width), F32)
    for h in range(width // HEAD_DIM):
        mine = head == h
        gh = jnp.where(mine, grad_context, zero)
        weights = p_ref[0, h]
        grad_p = mm(gh, v, 1, 1)
        wide = weights.astype(F32)
        dot = jnp.sum(wide * grad_p, axis=-1, keepdims=True)
        grad_s = (wide * (grad_p - dot)).astype(BF16)
        dv = dv + mm(weights, gh, 0, 0)
        dq = dq + mm(grad_s, jnp.where(mine, k, zero), 1, 0)
        dk = dk + mm(grad_s, jnp.where(mine, q, zero), 0, 0)
    scale = HEAD_DIM**-0.5
    dq = (dq * scale).astype(BF16)
    dk = (dk * scale).astype(BF16)
    dv = dv.astype(BF16)
    dq_out[...] = dq
    dk_out[...] = dk
    dv_out[...] = dv
    part = (mm(dq, w_qkv[0], 1, 0) + mm(dk, w_qkv[1], 1, 0) + mm(dv, w_qkv[2], 1, 0)).astype(BF16)
    part_ref[...] = part
    per = PAIR // sends[0].shape[0]
    for n, piece in enumerate(sends):

        @pl.when(i == n // per)
        def _():
            size = piece.shape[0]
            piece[...] = part_ref[(n % per) * size : (n % per + 1) * size]

    @pl.when(i >= half)
    def _():
        keep[...] = part


def attend_back(peers, owns, q, k, v, p, w_qkv, wo, pieces, after):
    rows, local = q.shape
    width = wo.shape[1]
    blocks = rows // PAIR
    half = blocks // 2
    heads = local // HEAD_DIM
    count = len(peers)
    ins = 2 * count + 6
    second = pl.BlockSpec((PAIR, width), lambda i: (jnp.maximum(i - half, 0), 0))
    thin = pl.BlockSpec((PAIR, local), lambda i: (i, 0))
    return pl.pallas_call(
        lambda *refs: attend_back_kernel(count, blocks, *refs[:ins], *refs[ins + len(after) :]),
        grid=(blocks,),
        in_specs=[VM] * (2 * count)
        + [
            thin, thin, thin,
            pl.BlockSpec((1, heads, PAIR, PAIR), lambda i: (i, 0, 0, 0)),
            whole(w_qkv), whole(wo),
        ]
        + [ANY] * len(after),
        out_specs=[VM] * pieces + [second, thin, thin, thin],
        out_shape=[shape((rows // 2 // pieces, width), BF16)] * pieces
        + [shape((rows // 2, width), BF16)]
        + [shape((rows, local), BF16)] * 3,
        scratch_shapes=[pltpu.VMEM((rows, width), BF16), pltpu.VMEM((PAIR, width), BF16)],
        compiler_params=params(),
        cost_estimate=cost("attend_back"),
        name="attend_back",
    )(*peers, *owns, q, k, v, p, w_qkv, wo, *after)


def last_kernel(count, *refs):
    pairs, others = refs[:count], refs[count : 2 * count]
    unit_ref, scale_ref, grad_residual, gain, low_out, sums, times = refs[2 * count :]
    i = pl.program_id(0)
    pair = jnp.where(i == 0, pairs[0][...], pairs[1][...])
    other = jnp.where(i == 0, others[0][...], others[1][...])
    err = pair.astype(F32) + other.astype(F32)
    unit, scale = unit_ref[...], scale_ref[...]
    f = err * row_vector(gain)
    f_mean = jnp.mean(f, axis=-1, keepdims=True)
    fx_mean = jnp.mean(f * unit, axis=-1, keepdims=True)
    grad = grad_residual[...] + scale * (f - f_mean - unit * fx_mean)
    low_out[...] = grad.astype(BF16)

    @pl.when(i == 0)
    def _():
        sums[...] = jnp.zeros_like(sums)

    sums[0:1] += jnp.sum(err * unit, axis=0, keepdims=True)
    sums[1:2] += jnp.sum(err, axis=0, keepdims=True)
    times[0, 0:1] = jnp.sum(grad[:SHORT], axis=0, keepdims=True)
    times[0, 1:2] = jnp.sum(grad[SHORT:], axis=0, keepdims=True)


def last_back(pair, other, unit, scale, grad_residual, gain, after):
    rows, width = unit.shape
    half = rows // PAIR
    row = pl.BlockSpec((PAIR, width), lambda i: (i, 0))
    return pl.pallas_call(
        lambda *refs: last_kernel(2, *refs[:8], *refs[8 + len(after) :]),
        grid=(half,),
        in_specs=[VM] * 4 + [row, pl.BlockSpec((PAIR, 1), lambda i: (i, 0)), row, whole(gain)] + [ANY] * len(after),
        out_specs=[
            row,
            pl.BlockSpec((8, width), lambda i: (0, 0)),
            pl.BlockSpec((1, 2, width), lambda i: (i, 0, 0)),
        ],
        out_shape=[shape((rows, width), BF16), shape((8, width), F32), shape((half, 2, width), F32)],
        compiler_params=params(),
        cost_estimate=cost("last_back"),
        name="last_back",
    )(*pair, *other, unit, scale, grad_residual, gain, *after)


def pack_sums(vec2, vec1, up_a, up_b, times, after):
    pairs, _, width = times.shape

    def kernel(v2, v1, ua, ub, t, out):
        out[0:3] = v2[0:3]
        out[3:5] = v1[0:2]
        out[5:6] = ua[...] + ub[...]
        out[6:8] = jnp.zeros((2, width), F32)
        for n in range(pairs):
            out[8 + 2 * n : 10 + 2 * n] = t[n]

    return small_call(kernel, [shape((8 + 2 * pairs, width), F32)], [vec2, vec1, up_a, up_b, times], after, "pack_sums")[0]


def join_sums(a, b, after, name):
    rows, width = a.shape
    more = rows - 8

    def kernel(a_ref, b_ref, out):
        out[0:8] = a_ref[0:8] + b_ref[0:8]
        out[8 : 8 + more] = a_ref[8:]
        out[8 + more :] = b_ref[8:]

    return small_call(kernel, [shape((8 + 2 * more, width), F32)], [a, b], after, name)[0]


def table_kernel(slots, steps, ids, own, other, *refs):
    vec_out, (out, table, acc, at_ref) = refs[:6], refs[6:]
    groups = at_ref.shape[0]
    rows, (row_length, row_group, row_step) = row_fields(ids)
    local = table.shape[2]
    half = slots // 2
    for n, vec in enumerate(vec_out):
        row = own[n : n + 1] + (other[n : n + 1] if n < 5 else 0.0)
        vec[...] = row.reshape(row.shape[1])
    for p in range(own.shape[1] // local):

        @pl.when(ids[2] == p)
        def _():
            table[0] = own[8:, p * local : (p + 1) * local]
            table[1] = other[8:, p * local : (p + 1) * local]

    acc[...] = jnp.zeros_like(acc)

    def clear(g, _):
        at_ref[g] = 0
        return 0

    lax.fori_loop(0, groups, clear, 0)

    def place(long):
        def one(r, _):
            @pl.when((row_length(r) > SHORT) == long)
            def _():
                g = row_group(r)
                at = at_ref[g]
                at_ref[g] = at + (2 if long else 1)
                which = (at // half) ^ ids[0]
                base = (g ^ ids[1]) * half + lax.rem(at, half)
                value = table[which, pl.ds(base, 1), :]
                if long:
                    value = value + table[which, pl.ds(base + 1, 1), :]
                step = pl.ds(row_step(r), 1)
                acc[step, :] = acc[step, :] + value

            return 0

        lax.fori_loop(0, rows, one, 0)

    place(True)
    place(False)
    out[...] = jnp.transpose(acc[...])[:, :steps]


def table_grad(scalars, own, other, steps, local, slots, after):
    rows, width = own.shape
    groups = (rows - 8) * 2 // slots
    return pl.pallas_call(
        lambda *refs: table_kernel(slots, steps, *refs[:3], *refs[3 + len(after) :]),
        grid_spec=pltpu.PrefetchScalarGridSpec(
            num_scalar_prefetch=1,
            grid=(1,),
            in_specs=[VM, VM] + [ANY] * len(after),
            out_specs=[pl.BlockSpec((width,), lambda *_: (0,))] * 6 + [pl.BlockSpec((local, steps), lambda *_: (0, 0))],
            scratch_shapes=[
                pltpu.VMEM((2, rows - 8, local), F32),
                pltpu.VMEM((pl.cdiv(steps, 128) * 128, local), F32),
                pltpu.SMEM((groups,), jnp.int32),
            ],
        ),
        out_shape=[pltpu.HBM((width,), F32)] * 6 + [pltpu.HBM((local, steps), F32)],
        compiler_params=params(),
        cost_estimate=cost("table_grad"),
        name="table_grad",
    )(scalars, own, other, *after)


def finish(residuals, pair, other, bias, after):
    rows, width = pair.shape
    part = rows // len(residuals)

    def kernel(*refs):
        res = refs[: len(residuals)]
        pair_ref, other_ref, bias_ref = refs[len(residuals) : len(residuals) + 3]
        out = refs[-1]
        for n, r in enumerate(res):
            at = slice(n * part, (n + 1) * part)
            total = r[...] + (pair_ref[at].astype(F32) + other_ref[at].astype(F32))
            out[at] = (total + row_vector(bias_ref)).astype(BF16)

    return small_call(kernel, [shape((rows, width), BF16)], [*residuals, pair, other, bias], after, "finish")[0]


def order_rows(ids, own, other, after, name):
    part, width = own.shape

    def kernel(ids_ref, own_ref, other_ref, *refs):
        out, sems = refs[len(after) :]
        copies = []
        for n, ref in enumerate((own_ref, other_ref)):
            start = pl.multiple_of((ids_ref[0] ^ n) * part, 16)
            copies.append(pltpu.make_async_copy(ref, out.at[pl.ds(start, part), :], sems.at[n]))
            copies[-1].start()
        for copy in copies:
            copy.wait()

    return pl.pallas_call(
        kernel,
        grid_spec=pltpu.PrefetchScalarGridSpec(
            num_scalar_prefetch=1,
            grid=(1,),
            in_specs=[VM, VM] + [ANY] * len(after),
            out_specs=HB,
            scratch_shapes=[pltpu.SemaphoreType.DMA((2,))],
        ),
        out_shape=pltpu.HBM((2 * part, width), BF16),
        compiler_params=params(),
        cost_estimate=cost(name),
        name=name,
    )(ids, own, other, *after)


def shards(
    tokens, row_length, row_group, row_step, time_table, norm1_gain, norm1_bias, w_qkv, w_out,
    norm2_gain, norm2_bias, w_up, up_bias, w_down, down_bias, cotangent,
):
    count, width = tokens.shape
    n_dp = lax.axis_size("dp")
    dp = lax.axis_index("dp")
    part = lax.axis_index("tensor")
    core = lax.rem(part, 2)
    direct = n_dp == 8
    low_bit, top_bit = dp & 1, (dp >> 2) & 1
    mid_bit = ((dp >> 1) & 1) ^ top_bit
    if direct:
        orders = [low_bit, 2 * mid_bit + top_bit, mid_bit, 2 * low_bit + top_bit]
    else:
        orders = [1, 0, 1, 0]
    own = jnp.stack([core, dp, part, *[jnp.int32(o) for o in orders], jnp.int32(0)]).astype(jnp.int32)
    ids = jnp.concatenate([own, row_length, row_group, row_step])
    scalars = ids
    order_a, order_b = 3, 5
    bits = ((1, 2, 6), (2, 1, 6))
    local = w_out.shape[0]
    slots = count // SHORT
    heads = jnp.transpose(w_qkv, (1, 2, 0))
    far = lambda x: pltpu.with_memory_space_constraint(x, pltpu.HBM)
    size = count // 2
    peer_rows = lambda ids: 1 - ids[0]
    own_rows = lambda ids: ids[0]
    zero = lambda ids: 0

    send, keep, hidden, normed, q, k, v, p, ctx = attend(
        0, 1, scalars, *[far(x) for x in (tokens, time_table, norm1_gain, norm1_bias, heads, w_out)], []
    )
    pair = add_two(keep, core_swap(send), [], "pair_one")
    other = chip_swap(pair)
    w_up, w_down, cotangent = stage([far(x) for x in (w_up, w_down, cotangent)], [pair])
    grad_act = act_grad(cotangent, w_down)
    unit1, scale1 = units(hidden, [grad_act])
    residual, own2 = mid_forward(hidden, pair, other, norm2_gain, norm2_bias, [unit1])
    peer2 = core_swap(own2)
    keep, act_own, low_rows_own, up_own = expand(ids, True, own2, grad_act, w_up, up_bias, [])
    send, act_peer, low_rows_peer, up_peer = expand(ids, False, peer2, grad_act, w_up, up_bias, [keep])
    got_two = core_swap(send)
    first_keep = keep
    start = send
    cots = [(cotangent, size, f) for f in (peer_rows, own_rows)]
    acts = [(act_peer, size, zero), (act_own, size, zero)]
    lows = [(low_rows_peer, size, zero), (low_rows_own, size, zero)]
    norms = [(peer2, size, zero), (own2, size, zero)]
    mlp = Dual(bits, direct)
    heads_sum = Dual(bits, direct)
    it = types.SimpleNamespace(attn=[])
    placed = [None, None]

    def down_grad(after):
        halves = weight_grad(ids, order_a, [list(zip(acts, cots))], after, "down_grad")
        mlp.begin(0, halves)
        return halves[1]

    def up_grad(after):
        halves = weight_grad(ids, order_b, [list(zip(norms, lows))], after, "up_grad")
        mlp.begin(1, halves)
        return halves[1]

    def pair_two(after):
        it.pair2 = add_two(first_keep, got_two, after, "pair_two")
        it.other2 = chip_swap(it.pair2)
        return it.pair2

    def contract(after):
        send, it.keep_e = contract_rows(act_peer, act_own, w_down, after)
        it.got_e = core_swap(send)
        it.unit2, it.scale2 = units(residual, [it.keep_e])
        return it.unit2

    def mid(after):
        it.grad_res, *it.low_own, it.vec2 = mid_back(
            0, 1, ids, it.pair2, it.other2, it.unit2, it.scale2, cotangent, norm2_gain, LOW_PIECES, after
        )
        it.low_peer = [core_swap(x) for x in it.low_own]
        return it.low_own[0]

    def attend_grad(after):
        *send, it.keep3, it.dq, it.dk, it.dv = attend_back(
            it.low_peer, it.low_own, q, k, v, p, heads, w_out, PART_PIECES, after
        )
        it.got3 = [core_swap(x) for x in send]
        return it.keep3

    def qk_grad(after):
        halves = head_grad(ids, order_a, (it.dq, [normed]), (it.dk, [normed]), after, "qk_grad")
        heads_sum.begin(0, halves)
        return halves[1]

    def vo_grad(after):
        lows = [*it.low_peer, *it.low_own]
        halves = head_grad(ids, order_b, (it.dv, [normed]), (ctx, lows), after, "vo_grad")
        heads_sum.begin(1, halves)
        return halves[1]

    def pair_three(after):
        it.pair3 = add_pieces(it.keep3, it.got3, 2, after, "pair_three")
        it.other3 = [chip_swap(x) for x in it.pair3]
        return it.pair3[0]

    def pair_out(after):
        it.pair_e = add_two(it.keep_e, it.got_e, after, "pair_out")
        it.other_e = chip_swap(it.pair_e)
        return it.pair_e

    def last(after):
        it.low_in, it.vec1, it.times = last_back(
            it.pair3, it.other3, unit1, scale1, it.grad_res, norm1_gain, after
        )
        it.low_got = core_swap(it.low_in)
        return it.low_in

    def pack(after):
        it.sums = pack_sums(it.vec2, it.vec1, up_own, up_peer, it.times, after)
        it.sums_got = dp_swap(it.sums, 1)
        return it.sums

    def join(level):
        def run(after):
            bit = 2 << level
            sums = join_sums(it.sums, it.sums_got, after, "join_sums")
            while level == 2 and bit < n_dp:
                sums = join_sums(sums, dp_swap(sums, bit), [], "join_sums")
                bit *= 2
            it.sums = sums
            if level < 2:
                it.sums_got = dp_swap(sums, bit)
            else:
                it.sums_peer = core_swap(sums)
            return sums

        return run

    def input_rows(after):
        it.input_grad = order_rows(ids, it.low_in, it.low_got, after, "order_input")
        return far(it.input_grad)

    def final(after):
        it.final = finish([residual], it.pair_e, it.other_e, down_bias, after)
        it.final_got = core_swap(it.final)
        return it.final

    def output_rows(after):
        it.block_output = order_rows(ids, it.final, it.final_got, after, "order_output")
        return far(it.block_output)

    def table(after):
        *it.vec, it.time_grad = table_grad(
            scalars, it.sums, it.sums_peer, time_table.shape[0], local, slots, after
        )
        return far(it.vec[0])

    def place(which, half):
        def run(after):
            order, value = (order_a, order_b)[which], mlp.collect(which)[half]
            placed[which] = place_half(ids, order, value, half, placed[which], after, ("place_down", "place_up")[which])
            return far(placed[which])

        return run

    def place_attn(half):
        def run(after):
            a, b = heads_sum.collect(0)[half], heads_sum.collect(1)[half]
            it.attn = place_heads(ids, (order_a, order_b), a, b, half, it.attn, after, "place_heads")
            return far(it.attn[1])

        return run

    def sum_step(group):
        return lambda after: group.step(after[0])

    order = (
        down_grad, pair_two, up_grad, contract, mid, sum_step(mlp), attend_grad, sum_step(mlp), vo_grad,
        pair_out, pair_three, qk_grad, sum_step(heads_sum), last, sum_step(heads_sum), pack, sum_step(mlp),
        sum_step(heads_sum), join(0), join(1), sum_step(mlp), sum_step(heads_sum), place(1, 0), place_attn(0),
        join(2), final, place(0, 0), input_rows, output_rows, table, place(1, 1), place(0, 1), place_attn(1),
    )
    mark = first_keep
    for step in order:
        mark = step([mark])
    vec, time_grad = it.vec, it.time_grad
    block_output, input_grad = it.block_output, it.input_grad
    down_out, up_out = placed
    qkv_out, proj_out = it.attn

    return (
        block_output,
        input_grad,
        time_grad.T,
        vec[3],
        vec[4],
        jnp.transpose(qkv_out, (2, 0, 1)),
        proj_out,
        vec[0],
        vec[1],
        up_out,
        vec[5],
        down_out,
        vec[2],
    )


def solution(mesh):
    in_specs = (
        P("dp", None), P(), P(), P(), P(), P(), P(), P(None, None, "tensor"), P("tensor", None), P(), P(),
        P(None, "tensor"), P("tensor"), P("tensor", None), P(), P("dp", None),
    )
    out_specs = (
        P("dp", None), P("dp", None), P(None, "tensor"), P(), P(), P(None, None, "tensor"), P("tensor", None),
        P(), P(), P(None, "tensor"), P("tensor"), P("tensor", None), P(),
    )
    return jax.shard_map(shards, mesh=mesh, in_specs=in_specs, out_specs=out_specs, check_vma=False)
```
